32 devices in a mesh: dp: 16 (over z, x, core), tensor: 2 (over y).
Axes of the slice: x: 2, y: 2, z: 4, core: 2. Of those that a mesh axis runs over, the one named last changes fastest.
Arguments:
- layer_in: bfloat16 [8192, 1536], P(('dp', 'tensor')), may hold values from -6 to 6
- segment_ids: int32 [16, 512], P('dp'), may hold values from 0 to 1, never falling along the last dimension, each value on 1 to 384 neighbouring positions
- norm1_gain: bfloat16 [1536], P('dp'), may hold values from 0.5 to 1.5
- w_query: bfloat16 [1536, 1536], P('dp', 'tensor'), may hold values from -0.15625 to 0.15625
- w_key: bfloat16 [1536, 1536], P('dp', 'tensor'), may hold values from -0.15625 to 0.15625
- w_value: bfloat16 [1536, 1536], P('dp', 'tensor'), may hold values from -0.15625 to 0.15625
- w_forget: bfloat16 [1536, 24], P('dp', 'tensor'), may hold values from -0.15625 to 0.15625
- forget_bias: float32 [24], P('tensor'), may hold values from 2 to 7
- w_output: bfloat16 [1536, 1536], P('dp', 'tensor'), may hold values from -0.625 to 0.625
- norm2_gain: bfloat16 [1536], P('dp'), may hold values from 0.5 to 1.5
- w_gate: bfloat16 [1536, 4096], P('dp', 'tensor'), may hold values from -0.15625 to 0.15625
- w_up: bfloat16 [1536, 4096], P('dp', 'tensor'), may hold values from -0.15625 to 0.15625
- w_down: bfloat16 [1536, 4096], P('dp', 'tensor'), may hold values from -0.09375 to 0.09375
- clip_tau: float32 [24], P('tensor'), may hold values from 2 to 6
- out_grad: bfloat16 [8192, 1536], P(('dp', 'tensor')), may hold values from -6 to 6
Outputs:
- layer_out: bfloat16 [8192, 1536], P(('dp', 'tensor'))
- x_grad: bfloat16 [8192, 1536], P(('dp', 'tensor'))
- g_norm1: float32 [1536], P('tensor')
- g_query: float32 [1536, 1536], P('dp', 'tensor')
- g_key: float32 [1536, 1536], P('dp', 'tensor')
- g_value: float32 [1536, 1536], P('dp', 'tensor')
- g_forget: float32 [1536, 24], P('dp', 'tensor')
- g_bias: float32 [24], P('tensor')
- g_output: float32 [1536, 1536], P('dp', 'tensor')
- g_norm2: float32 [1536], P('tensor')
- g_gate: float32 [1536, 4096], P('dp', 'tensor')
- g_up: float32 [1536, 4096], P('dp', 'tensor')
- g_down: float32 [1536, 4096], P('dp', 'tensor')
- clip_factor: float32 [24], P('tensor')
- clipped_query: bfloat16 [1536, 1536], P('dp', 'tensor')
- clipped_key: bfloat16 [1536, 1536], P('dp', 'tensor')
The draws below stay inside these ranges and needn't reach their ends.
Inputs may be any that keep to these rules, and one draw needn't show every extreme that they name: `segment_ids`: segment numbers never fall along a pack; each segment has 1 to 384 positions.
All inputs are finite; a program needn't handle non-finite values.
Results may differ from the reference program's by a relative error of at most 0.02.
Values may be sent and summed in bfloat16 or wider, within the bound.
No kernel may reach another device: no remote copies, remote signals or barrier semaphores. Data moves between devices by JAX's collectives and lax.ppermute only.
A program may use at most 192 MiB of HBM per device.

```python
import math
import jax
import jax.numpy as jnp
import numpy as np
from jax import lax

D = 1536
HEADS = 24
HEAD_DIM = 64
FF = 4096
BLOCK = 256
TOK_DEV = 512
PACKS = 16
TOKENS = 8192


def with_spikes(drawn, stream_key, source, target, blocks, factor):
    owner, partner = [(jnp.arange(drawn.shape[axis_at]) // (drawn.shape[axis_at] // blocks)).reshape([-1 if axis == axis_at else 1 for axis in range(drawn.ndim)]) for axis_at in (source, target)]
    chosen = jax.random.permutation(stream_key, blocks)[partner]
    strong = (owner == chosen) | (owner == (partner + blocks // 2) % blocks)
    return jnp.where(strong, factor * drawn, drawn)


def steps_of(own_key, shape, cuts, low, top_value):
    loudness, own = 1.0, jax.random.fold_in(own_key, 6)
    for position, parts in cuts:
        draws = jnp.exp(jax.random.uniform(jax.random.fold_in(own, position), (parts,), jnp.float32, low / len(cuts), top_value / len(cuts)))
        loudness = loudness * jnp.repeat(draws, shape[position] // parts).reshape([-1 if axis == position else 1 for axis in range(len(shape))])
    return loudness


def profile(count, total, bound, lean):
    weights = [(1 << 20) // math.isqrt(grade ** lean) + 1 for grade in range(2, count + 1)]
    surplus, given = total - bound - (count - 1), [1] * (count - 1)
    while surplus > 0:
        movable = [i for i in range(count - 1) if given[i] < bound]
        whole, left = sum([weights[i] for i in movable]), surplus
        for i in movable:
            addition = min(bound - given[i], max(1, left * weights[i] // whole), surplus)
            given[i] = given[i] + addition
            surplus = surplus - addition
    return np.array([bound] + given)


def uneven(rng, amount, total, most, slope):
    if amount == 2:
        one = jax.random.randint(rng, (), max(1, total - most), min(most, total - 1) + 1)
        return jnp.stack([one, total - one])
    lengths = jnp.asarray(profile(amount, total, most, slope), jnp.int32)
    twos = (amount - 1) // 2
    giver, sink = lengths[1:1 + 2 * twos:2], lengths[2:2 + 2 * twos:2]
    room = jnp.minimum(giver - 1, most - sink)
    moved = jax.random.randint(jax.random.fold_in(rng, 1), (twos,), 0, 1 << 20) % (room + 1)
    lengths = lengths.at[1:1 + 2 * twos:2].set(giver - moved).at[2:2 + 2 * twos:2].set(sink + moved)
    return lengths[jax.random.permutation(jax.random.fold_in(rng, 2), amount)]


def centred(own_key, shape, deviation, bound, cuts=(), held_as=jnp.bfloat16):
    loudness = steps_of(own_key, shape, cuts, -0.22, 0.18) if cuts else 1.0
    values = jax.random.normal(own_key, shape, jnp.float32) * deviation * loudness
    return jnp.minimum(jnp.maximum(values, -bound), bound).astype(held_as)


def heavy_noise(stream_key, shape, width, limit, cuts, heavy, held_as=jnp.bfloat16):
    drawn = width * jax.random.normal(stream_key, shape, jnp.float32)
    if cuts:
        drawn = drawn * steps_of(stream_key, shape, cuts, -0.22, 0.18)
    return jnp.clip(with_spikes(drawn, jax.random.fold_in(stream_key, 3), *heavy), -limit, limit).astype(held_as)


def setup_inputs(seed: int = 0) -> dict:
    key_list = jax.random.split(jax.random.key(seed), 16)
    return {
        "layer_in": heavy_noise(key_list[0], (TOKENS, D), 1.0, 6.0, ((0, 32),), (0, 1, 32, 2.75)),
        "segment_ids": jax.vmap(lambda own: jnp.searchsorted(jnp.cumsum(uneven(own, 2, TOK_DEV, TOK_DEV * 3 // 4, 0)), jnp.arange(TOK_DEV), side="right"))(jax.random.split(key_list[1], PACKS)).reshape((PACKS, TOK_DEV)).astype(jnp.int32),
        "norm1_gain": jnp.clip(1.0 + 0.1 * jax.random.normal(key_list[2], (D,), jnp.float32), 0.5, 1.5).astype(jnp.bfloat16),
        "w_query": centred(key_list[3], (D, HEADS * HEAD_DIM), D ** -0.5, 0.15625, ((0, 16), (1, 2))),
        "w_key": centred(key_list[4], (D, HEADS * HEAD_DIM), D ** -0.5, 0.15625, ((0, 16), (1, 2))),
        "w_value": centred(key_list[5], (D, HEADS * HEAD_DIM), D ** -0.5, 0.15625, ((0, 16), (1, 2))),
        "w_forget": centred(key_list[6], (D, HEADS), D ** -0.5, 0.15625, ((0, 16), (1, 2))),
        "forget_bias": jnp.clip(2.0 + 5.0 * jax.random.uniform(key_list[7], (HEADS,), jnp.float32) ** steps_of(key_list[7], (HEADS,), ((0, 2),), -0.2, 0.2), 2.0, 7.0),
        "w_output": centred(key_list[8], (D, HEADS * HEAD_DIM), (HEADS * HEAD_DIM // 16) ** -0.5, 0.625, ((0, 16), (1, 2))),
        "norm2_gain": jnp.clip(1.0 + 0.1 * jax.random.normal(key_list[9], (D,), jnp.float32), 0.5, 1.5).astype(jnp.bfloat16),
        "w_gate": centred(key_list[10], (D, FF), D ** -0.5, 0.15625, ((0, 16), (1, 2))),
        "w_up": centred(key_list[11], (D, FF), D ** -0.5, 0.15625, ((0, 16), (1, 2))),
        "w_down": centred(key_list[12], (D, FF), FF ** -0.5, 0.09375, ((0, 16), (1, 2))),
        "clip_tau": jnp.clip(2.0 + 4.0 * jax.random.uniform(key_list[13], (HEADS,), jnp.float32) ** steps_of(key_list[13], (HEADS,), ((0, 2),), -0.2, 0.2), 2.0, 6.0),
        "out_grad": centred(key_list[14], (TOKENS, D), 1.0, 6.0, ((0, 32),)),
    }


EPSILON = 1e-06
HIGHEST = lax.Precision.HIGHEST
NEGATIVE = -1e+30

@jax.custom_vjp
def low(v):
    return lax.optimization_barrier(v.astype(jnp.bfloat16)).astype(jnp.float32)

@jax.custom_vjp
def low_back(v):
    return v

def low_keep(v):
    return (low(v), None)

def low_pass(kept, grad):
    return (grad,)

def back_keep(v):
    return (v, None)

def back_low(kept, grad):
    return (low(grad),)
low.defvjp(low_keep, low_pass)
low_back.defvjp(back_keep, back_low)

def both_ways(values_in):
    return low_back(low(values_in))

def rms_norm(values_in, gain_vec):
    factor = lax.rsqrt(lax.optimization_barrier(jnp.mean(values_in * values_in, axis=-1, keepdims=True)) + EPSILON)
    return values_in * factor * gain_vec

def pack_layer(params, pack_in, seg_row):
    gain_one, wq_all, wk_all, wv_all, wf_all, fbias, wo_all, gain_two, wg_all, wu_all, wd_all = params
    normed_one = low(rms_norm(pack_in, gain_one))
    queries = both_ways(jnp.dot(normed_one, wq_all, precision=HIGHEST)).reshape(TOK_DEV, HEADS, HEAD_DIM)
    keys_all = both_ways(jnp.dot(normed_one, wk_all, precision=HIGHEST)).reshape(TOK_DEV, HEADS, HEAD_DIM)
    values_all = both_ways(jnp.dot(normed_one, wv_all, precision=HIGHEST)).reshape(TOK_DEV, HEADS, HEAD_DIM)
    logits = jnp.dot(normed_one, wf_all, precision=HIGHEST) + fbias
    cumul = jnp.cumsum(jax.nn.log_sigmoid(logits), axis=0)
    positions = jnp.arange(TOK_DEV, dtype=jnp.int32)
    rows_blk = min(512, TOK_DEV)
    blocks = TOK_DEV // rows_blk
    factor = HEAD_DIM ** (-0.5)

    def attend_block(number):
        offset = number * rows_blk
        q_blk = lax.dynamic_slice_in_dim(queries, offset, rows_blk, 0)
        q_pos = offset + jnp.arange(rows_blk, dtype=jnp.int32)
        q_seg = lax.dynamic_slice_in_dim(seg_row, offset, rows_blk, 0)
        q_cum = lax.dynamic_slice_in_dim(cumul, offset, rows_blk, 0)
        allowed = (q_seg[:, None] == seg_row[None, :]) & (q_pos[:, None] // BLOCK >= positions[None, :] // BLOCK)
        earlier_key = positions[None, :] <= q_pos[:, None]
        raw_blk = jnp.einsum('qhe,khe->hqk', q_blk, keys_all, precision=HIGHEST) * factor
        differ = q_cum.T[:, :, None] - cumul.T[:, None, :]
        bias_blk = jnp.where(earlier_key[None], differ, -differ)
        scores = low_back(raw_blk + bias_blk)
        scores = jnp.where(allowed[None], scores, NEGATIVE)
        weights = low(jax.nn.softmax(scores, axis=-1))
        mixed_out = both_ways(jnp.einsum('hqk,khe->qhe', weights, values_all, precision=HIGHEST))
        top_blk = lax.optimization_barrier(jnp.max(jnp.where(allowed[None], raw_blk, NEGATIVE), axis=(1, 2)))
        return (mixed_out, top_blk)
    mixed_out, top_blk = lax.map(jax.checkpoint(attend_block), jnp.arange(blocks, dtype=jnp.int32))
    mixed_flat = mixed_out.reshape(TOK_DEV, HEADS * HEAD_DIM)
    attn_out = low_back(jnp.dot(mixed_flat, wo_all.T, precision=HIGHEST))
    resid_one = pack_in + attn_out
    normed_two = low(rms_norm(resid_one, gain_two))
    gate_pre = low_back(jnp.dot(normed_two, wg_all, precision=HIGHEST))
    up_pre = low_back(jnp.dot(normed_two, wu_all, precision=HIGHEST))
    hidden = low(jax.nn.silu(gate_pre) * up_pre)
    pack_out = resid_one + jnp.dot(hidden, wd_all.T, precision=HIGHEST)
    return (pack_out, lax.optimization_barrier(jnp.max(top_blk, axis=0)))

def reference(layer_in, segment_ids, norm1_gain, w_query, w_key, w_value, w_forget, forget_bias, w_output, norm2_gain, w_gate, w_up, w_down, clip_tau, out_grad):
    params = (norm1_gain.astype(jnp.float32), w_query.astype(jnp.float32), w_key.astype(jnp.float32), w_value.astype(jnp.float32), w_forget.astype(jnp.float32), forget_bias.astype(jnp.float32), w_output.astype(jnp.float32), norm2_gain.astype(jnp.float32), w_gate.astype(jnp.float32), w_up.astype(jnp.float32), w_down.astype(jnp.float32))
    packs = layer_in.astype(jnp.float32).reshape(PACKS, TOK_DEV, D)
    checked = jax.checkpoint(pack_layer)

    def full_layer(params, packs):

        def pack_step(carried, pack_item):
            pack_out, top_pack = checked(params, pack_item[0], pack_item[1])
            return (carried, (pack_out, top_pack))
        _, (outs_all, tops_all) = lax.scan(pack_step, jnp.zeros((), jnp.float32), (packs, segment_ids))
        return (outs_all, tops_all)
    outs_all, pull_back, tops_all = jax.vjp(full_layer, params, packs, has_aux=True)
    grads, grad_packs = pull_back(out_grad.astype(jnp.float32).reshape(PACKS, TOK_DEV, D))
    maxima = lax.optimization_barrier(jnp.max(tops_all, axis=0))
    clip_factor = jnp.minimum(1.0, clip_tau / jnp.maximum(maxima, 1.0))
    columns = jnp.repeat(jnp.sqrt(clip_factor), HEAD_DIM)
    clipped_query = (w_query.astype(jnp.float32) * columns[None, :]).astype(jnp.bfloat16)
    clipped_key = (w_key.astype(jnp.float32) * columns[None, :]).astype(jnp.bfloat16)
    layer_out = outs_all.reshape(TOKENS, D).astype(jnp.bfloat16)
    x_grad = grad_packs.reshape(TOKENS, D).astype(jnp.bfloat16)
    return (layer_out, x_grad, grads[0], grads[1], grads[2], grads[3], grads[4], grads[5], grads[6], grads[7], grads[8], grads[9], grads[10], clip_factor, clipped_query, clipped_key)
```

```python
import math
from functools import partial

import jax
import jax.numpy as jnp
from jax import lax
from jax.experimental import pallas as pl
from jax.experimental.pallas import tpu as pltpu
from jax.sharding import PartitionSpec as P

HEAD_DIM = 64
BLOCK = 256
LANES = 128
EPSILON = 1e-06
HIGHEST = lax.Precision.HIGHEST
NEGATIVE = -1e30
F32 = jnp.float32
BF16 = jnp.bfloat16
def combined_all(part, axis, combine):
    gathered = jax.tree.map(lambda a: lax.all_gather(a, axis), part)

    def take(source):
        return jax.tree.map(lambda a: lax.dynamic_index_in_dim(a, source, 0, False), gathered)

    return lax.fori_loop(
        1, lax.axis_size(axis), lambda source, state: combine(state, take(source)), take(0)
    )


def contract_last(left_op, right_op):
    return lax.dot_general(
        left_op, right_op, (((1,), (1,)), ((), ())), preferred_element_type=jnp.float32
    )


def contract_first(left_op, right_op):
    return lax.dot_general(
        left_op, right_op, (((0,), (0,)), ((), ())), preferred_element_type=jnp.float32
    )


def block_terms(q_blk, keys_all, cumul, seg_row, offset, rows_blk):
    positions = jnp.arange(keys_all.shape[0], dtype=jnp.int32)
    q_pos = offset + jnp.arange(rows_blk, dtype=jnp.int32)
    allowed = (seg_row[:, None] == seg_row[None, :]) & (
        q_pos[:, None] // BLOCK >= positions[None, :] // BLOCK
    )
    signs = jnp.where(positions[None, :] <= q_pos[:, None], 1.0, -1.0).astype(jnp.float32)
    raw_blk = jnp.einsum("qhe,khe->hqk", q_blk, keys_all, preferred_element_type=jnp.float32) * (
        1.0 / math.sqrt(HEAD_DIM)
    )
    differ = cumul.T[:, :, None] - cumul.T[:, None, :]
    scores = jnp.where(allowed[None], raw_blk + signs[None] * differ, NEGATIVE)
    return (raw_blk, scores, allowed, signs)


def combine(former, latter):
    return (
        jnp.maximum(former[0], latter[0]),
        former[1] + latter[1],
        former[2] + latter[2],
        former[3] + latter[3],
    )


def general_body(
    layer_in,
    segment_ids,
    norm1_gain,
    w_query,
    w_key,
    w_value,
    w_forget,
    forget_bias,
    w_output,
    norm2_gain,
    w_gate,
    w_up,
    w_down,
    clip_tau,
    out_grad,
):
    gain_one, wq_all, wk_all, wv_all, wf_all, wo_all, gain_two, wg_all, wu_all, wd_all = (
        lax.all_gather(norm1_gain, "dp", axis=0, tiled=True),
        lax.all_gather(w_query, "dp", axis=0, tiled=True),
        lax.all_gather(w_key, "dp", axis=0, tiled=True),
        lax.all_gather(w_value, "dp", axis=0, tiled=True),
        lax.all_gather(w_forget, "dp", axis=0, tiled=True),
        lax.all_gather(w_output, "dp", axis=0, tiled=True),
        lax.all_gather(norm2_gain, "dp", axis=0, tiled=True),
        lax.all_gather(w_gate, "dp", axis=0, tiled=True),
        lax.all_gather(w_up, "dp", axis=0, tiled=True),
        lax.all_gather(w_down, "dp", axis=0, tiled=True),
    )
    gain_one = gain_one.astype(jnp.float32)
    gain_two = gain_two.astype(jnp.float32)
    tok_local = layer_in.shape[0]
    tokens = tok_local * lax.axis_size("tensor")
    heads_loc = forget_bias.shape[0]
    row_start = lax.axis_index("tensor") * tok_local
    seg_row = segment_ids[0]
    factor = 1.0 / math.sqrt(HEAD_DIM)
    rows_full = lax.all_gather(layer_in, "tensor", axis=0, tiled=True).astype(jnp.float32)
    scale_one = lax.rsqrt(jnp.mean(rows_full * rows_full, axis=1, keepdims=True) + EPSILON)
    unit_one = rows_full * scale_one
    normed_one = (unit_one * gain_one).astype(jnp.bfloat16)
    queries = (
        jnp.dot(normed_one, wq_all, preferred_element_type=jnp.float32)
        .astype(jnp.bfloat16)
        .reshape(tokens, heads_loc, HEAD_DIM)
    )
    keys_all = (
        jnp.dot(normed_one, wk_all, preferred_element_type=jnp.float32)
        .astype(jnp.bfloat16)
        .reshape(tokens, heads_loc, HEAD_DIM)
    )
    values_all = (
        jnp.dot(normed_one, wv_all, preferred_element_type=jnp.float32)
        .astype(jnp.bfloat16)
        .reshape(tokens, heads_loc, HEAD_DIM)
    )
    logits = jnp.dot(normed_one, wf_all, preferred_element_type=jnp.float32) + forget_bias
    cumul = jnp.cumsum(jax.nn.log_sigmoid(logits), axis=0)
    rows_blk = min(512, tokens)
    blocks = tokens // rows_blk
    numbers = jnp.arange(blocks, dtype=jnp.int32)

    def forward_block(number):
        offset = number * rows_blk
        raw_blk, scores, allowed, signs = block_terms(
            queries, keys_all, cumul, seg_row, offset, rows_blk
        )
        top_blk = jnp.max(jnp.where(allowed[None], raw_blk, NEGATIVE), axis=(1, 2))
        row_peak = jnp.max(scores, axis=2, keepdims=True)
        expo_blk = jnp.exp(scores - row_peak)
        totals = jnp.sum(expo_blk, axis=2, keepdims=True)
        weights = (expo_blk / totals).astype(jnp.bfloat16)
        mixed_out = jnp.einsum(
            "hqk,khe->qhe", weights, values_all, preferred_element_type=jnp.float32
        ).astype(jnp.bfloat16)
        return (mixed_out, (row_peak + jnp.log(totals))[:, :, 0], top_blk)

    mixed_out, log_sums, top_blk = lax.map(forward_block, numbers)
    mixed_flat = mixed_out.reshape(tokens, heads_loc * HEAD_DIM)
    maxima = jnp.max(top_blk, axis=0)
    attn_part = contract_last(mixed_flat, wo_all)
    resid_full = rows_full + lax.psum(attn_part.astype(jnp.bfloat16), "tensor").astype(jnp.float32)
    scale_full = lax.rsqrt(jnp.mean(resid_full * resid_full, axis=1, keepdims=True) + EPSILON)
    normed_two = (resid_full * scale_full * gain_two).astype(jnp.bfloat16)
    resid_part = lax.dynamic_slice_in_dim(resid_full, row_start, tok_local, 0)
    scale_two = lax.dynamic_slice_in_dim(scale_full, row_start, tok_local, 0)
    gate_pre = jnp.dot(normed_two, wg_all, preferred_element_type=jnp.float32)
    up_pre = jnp.dot(normed_two, wu_all, preferred_element_type=jnp.float32)
    gate_sig = jax.nn.sigmoid(gate_pre)
    gate_act = gate_pre * gate_sig
    hidden = (gate_act * up_pre).astype(jnp.bfloat16)
    ffn_part = lax.psum_scatter(
        contract_last(hidden, wd_all).astype(jnp.bfloat16),
        "tensor",
        scatter_dimension=0,
        tiled=True,
    ).astype(jnp.float32)
    layer_out = (resid_part + ffn_part).astype(jnp.bfloat16)
    grad_full = lax.all_gather(out_grad, "tensor", axis=0, tiled=True)
    grad_hidden = jnp.dot(grad_full, wd_all, preferred_element_type=jnp.float32)
    grad_gate = (grad_hidden * up_pre * gate_sig * (1.0 + gate_pre * (1.0 - gate_sig))).astype(
        jnp.bfloat16
    )
    grad_up = (grad_hidden * gate_act).astype(jnp.bfloat16)
    g_down = contract_first(grad_full, hidden)
    g_gate = contract_first(normed_two, grad_gate)
    g_up = contract_first(normed_two, grad_up)
    grad_normed = contract_last(grad_gate, wg_all) + contract_last(grad_up, wu_all)
    grad_two = lax.psum_scatter(
        grad_normed.astype(jnp.bfloat16), "tensor", scatter_dimension=0, tiled=True
    ).astype(jnp.float32)
    unit_two = resid_part * scale_two
    inner_two = jnp.mean(unit_two * gain_two * grad_two, axis=1, keepdims=True)
    norm2_part = jnp.sum(grad_two * unit_two, axis=0)
    grad_resid = out_grad.astype(jnp.float32) + scale_two * (
        gain_two * grad_two - unit_two * inner_two
    )
    grad_attn = lax.all_gather(grad_resid.astype(jnp.bfloat16), "tensor", axis=0, tiled=True)
    g_output = contract_first(grad_attn, mixed_flat)
    grad_mixed = jnp.dot(grad_attn, wo_all, preferred_element_type=jnp.float32).astype(jnp.bfloat16)
    grad_mixed = grad_mixed.reshape(blocks, rows_blk, heads_loc, HEAD_DIM)

    def backward_block(carried, block_in):
        key_acc, value_acc, column_acc = carried
        number, log_blk, grad_blk = block_in
        offset = number * rows_blk
        raw_blk, scores, allowed, signs = block_terms(
            queries, keys_all, cumul, seg_row, offset, rows_blk
        )
        prob_blk = jnp.exp(scores - log_blk[:, :, None])
        weights = prob_blk.astype(jnp.bfloat16)
        grad_prob = jnp.einsum(
            "qhe,khe->hqk", grad_blk, values_all, preferred_element_type=jnp.float32
        )
        inner = jnp.sum(prob_blk * grad_prob, axis=2, keepdims=True)
        grad_scores = (prob_blk * (grad_prob - inner)).astype(jnp.bfloat16)
        value_acc = value_acc + jnp.einsum(
            "hqk,qhe->khe", weights, grad_blk, preferred_element_type=jnp.float32
        )
        key_acc = key_acc + jnp.einsum(
            "hqk,qhe->khe", grad_scores, queries, preferred_element_type=jnp.float32
        )
        grad_query = (
            jnp.einsum("hqk,khe->qhe", grad_scores, keys_all, preferred_element_type=jnp.float32)
            * factor
        ).astype(jnp.bfloat16)
        signed = grad_scores.astype(jnp.float32) * signs[None]
        column_acc = column_acc - jnp.sum(signed, axis=1).T
        return ((key_acc, value_acc, column_acc), (grad_query, jnp.sum(signed, axis=2).T))

    start_acc = (
        jnp.zeros((tokens, heads_loc, HEAD_DIM), jnp.float32),
        jnp.zeros((tokens, heads_loc, HEAD_DIM), jnp.float32),
        jnp.zeros((tokens, heads_loc), jnp.float32),
    )
    (key_acc, value_acc, column_acc), (grad_query, row_parts) = lax.scan(
        backward_block, start_acc, (numbers, log_sums, grad_mixed)
    )
    grad_q = grad_query.reshape(tokens, heads_loc * HEAD_DIM)
    grad_k = (key_acc * factor).astype(jnp.bfloat16).reshape(tokens, heads_loc * HEAD_DIM)
    grad_v = value_acc.astype(jnp.bfloat16).reshape(tokens, heads_loc * HEAD_DIM)
    grad_cum = row_parts.reshape(tokens, heads_loc) + column_acc
    grad_logs = jnp.cumsum(grad_cum[::-1], axis=0)[::-1]
    grad_logit = grad_logs * jax.nn.sigmoid(-logits)
    g_bias = jnp.sum(grad_logit, axis=0)
    g_forget = jnp.einsum(
        "td,th->dh", normed_one, grad_logit, precision=HIGHEST, preferred_element_type=jnp.float32
    )
    g_query = contract_first(normed_one, grad_q)
    g_key = contract_first(normed_one, grad_k)
    g_value = contract_first(normed_one, grad_v)
    grad_one = (
        contract_last(grad_q, wq_all)
        + contract_last(grad_k, wk_all)
        + contract_last(grad_v, wv_all)
    )
    grad_one = grad_one + jnp.einsum(
        "th,dh->td", grad_logit, wf_all, precision=HIGHEST, preferred_element_type=jnp.float32
    )
    weighted = gain_one * grad_one
    grad_rows_one = scale_one * (
        weighted - unit_one * jnp.mean(unit_one * weighted, axis=1, keepdims=True)
    )
    norm1_part = jnp.sum(grad_one * unit_one, axis=0)
    grad_input, g_norm1_part, g_norm2_part = (
        lax.psum_scatter(
            grad_rows_one.astype(jnp.bfloat16), "tensor", scatter_dimension=0, tiled=True
        ).astype(jnp.float32),
        lax.psum_scatter(
            norm1_part.astype(jnp.bfloat16), "tensor", scatter_dimension=0, tiled=True
        ).astype(jnp.float32),
        lax.psum_scatter(
            norm2_part.astype(jnp.bfloat16), "tensor", scatter_dimension=0, tiled=True
        ).astype(jnp.float32),
    )
    x_grad = (grad_resid + grad_input).astype(jnp.bfloat16)
    g_query, g_key, g_value, g_forget, g_output, g_gate, g_up, g_down = (
        lax.psum_scatter(
            g_query.astype(jnp.bfloat16), "dp", scatter_dimension=0, tiled=True
        ).astype(jnp.float32),
        lax.psum_scatter(g_key.astype(jnp.bfloat16), "dp", scatter_dimension=0, tiled=True).astype(
            jnp.float32
        ),
        lax.psum_scatter(
            g_value.astype(jnp.bfloat16), "dp", scatter_dimension=0, tiled=True
        ).astype(jnp.float32),
        lax.psum_scatter(
            g_forget.astype(jnp.bfloat16), "dp", scatter_dimension=0, tiled=True
        ).astype(jnp.float32),
        lax.psum_scatter(
            g_output.astype(jnp.bfloat16), "dp", scatter_dimension=0, tiled=True
        ).astype(jnp.float32),
        lax.psum_scatter(g_gate.astype(jnp.bfloat16), "dp", scatter_dimension=0, tiled=True).astype(
            jnp.float32
        ),
        lax.psum_scatter(g_up.astype(jnp.bfloat16), "dp", scatter_dimension=0, tiled=True).astype(
            jnp.float32
        ),
        lax.psum_scatter(g_down.astype(jnp.bfloat16), "dp", scatter_dimension=0, tiled=True).astype(
            jnp.float32
        ),
    )
    maxima, g_bias, g_norm1, g_norm2 = combined_all(
        (maxima, g_bias, g_norm1_part, g_norm2_part), "dp", combine
    )
    clip_factor = jnp.minimum(1.0, clip_tau / jnp.maximum(maxima, 1.0))
    columns = jnp.repeat(jnp.sqrt(clip_factor), HEAD_DIM)
    clipped_query = (w_query.astype(jnp.float32) * columns[None, :]).astype(jnp.bfloat16)
    clipped_key = (w_key.astype(jnp.float32) * columns[None, :]).astype(jnp.bfloat16)
    return (
        layer_out,
        x_grad,
        g_norm1,
        g_query,
        g_key,
        g_value,
        g_forget,
        g_bias,
        g_output,
        g_norm2,
        g_gate,
        g_up,
        g_down,
        clip_factor,
        clipped_query,
        clipped_key,
    )


def dot_nt(left, right):
    return lax.dot_general(left, right, (((1,), (1,)), ((), ())), preferred_element_type=F32)


def dot_nn(left, right):
    return lax.dot_general(left, right, (((1,), (0,)), ((), ())), preferred_element_type=F32)


def dot_tn(left, right):
    return lax.dot_general(left, right, (((0,), (0,)), ((), ())), preferred_element_type=F32)


def attend_kernel(y_ref, qkv_ref, aux_ref, o_ref, inv_ref, exp_ref, top_ref):
    y = y_ref[0]
    starts = (pl.multiple_of(y * BLOCK, BLOCK), pl.multiple_of((1 - y) * BLOCK, BLOCK))
    lane = lax.broadcasted_iota(jnp.int32, (1, LANES), 1)
    first = lane < HEAD_DIM
    aux = [aux_ref[0, :, pl.ds(start, BLOCK)] for start in starts]
    aux_col = [a.T for a in aux]
    q_blk = [qkv_ref[pl.ds(s, BLOCK), 0:LANES] * 0.125 for s in starts]
    k_blk = [qkv_ref[pl.ds(s, BLOCK), LANES : 2 * LANES] for s in starts]
    v_blk = [qkv_ref[pl.ds(s, BLOCK), 2 * LANES : 3 * LANES] for s in starts]
    same = {}
    for i, j in ((0, 0), (1, 0), (1, 1)):
        same[i, j] = aux_col[i][:, 2:3] == aux[j][2:3, :]
    tops = []
    results = [[], []]
    for head in range(2):
        mine = first if head == 0 else jnp.logical_not(first)
        top = None
        v_ext = [jnp.where(mine, v, jnp.ones_like(v)) for v in v_blk]
        k_head = [jnp.where(mine, k, jnp.zeros_like(k)) for k in k_blk]
        for i in range(2):
            scores = []
            for j in range(i + 1):
                raw = dot_nt(q_blk[i], k_head[j])
                seen = jnp.where(same[i, j], raw, NEGATIVE)
                high = jnp.max(seen, axis=0, keepdims=True)
                top = high if top is None else jnp.maximum(top, high)
                differ = aux_col[i][:, head : head + 1] - aux[j][head : head + 1, :]
                scores.append(seen - jnp.abs(differ))
            peak = jnp.max(scores[0], axis=1, keepdims=True)
            if i == 1:
                peak = jnp.maximum(peak, jnp.max(scores[1], axis=1, keepdims=True))
            acc = None
            for j in range(i + 1):
                weights = jnp.exp(scores[j] - peak).astype(BF16)
                exp_ref[0, 0, head, :, (i + j) * BLOCK : (i + j + 1) * BLOCK] = weights
                part = dot_nn(weights, v_ext[j])
                acc = part if acc is None else acc + part
            results[i].append(acc)
        tops.append(jnp.maximum(top[:, :LANES], top[:, LANES:]))
    for i in range(2):
        one, two = results[i]
        total = pltpu.roll(jnp.where(first, two, one), HEAD_DIM, 1)
        inverse = 1.0 / total
        inv_ref[pl.ds(starts[i], BLOCK), :] = inverse
        o_ref[pl.ds(starts[i], BLOCK), :] = (jnp.where(first, one, two) * inverse).astype(BF16)
    row = lax.broadcasted_iota(jnp.int32, (8, LANES), 0)
    top_ref[0, 0] = jnp.where(row == 0, tops[0], tops[1])


def attend(y_index, qkv, aux, packs, pairs):
    rows = qkv.shape[0] // packs
    wide = 3 * LANES
    grid_spec = pltpu.PrefetchScalarGridSpec(
        num_scalar_prefetch=1,
        grid=(packs, pairs),
        in_specs=[
            pl.BlockSpec((rows, wide), lambda p, h, y: (p, h)),
            pl.BlockSpec((1, 8, rows), lambda p, h, y: (h, 0, p)),
        ],
        out_specs=[
            pl.BlockSpec((rows, LANES), lambda p, h, y: (p, h)),
            pl.BlockSpec((rows, LANES), lambda p, h, y: (p, h)),
            pl.BlockSpec((1, 1, 2, BLOCK, 3 * BLOCK), lambda p, h, y: (p, h, 0, 0, 0)),
            pl.BlockSpec((1, 1, 8, LANES), lambda p, h, y: (p, h, 0, 0)),
        ],
    )
    return pl.pallas_call(
        attend_kernel,
        grid_spec=grid_spec,
        out_shape=(
            jax.ShapeDtypeStruct((packs * rows, pairs * LANES), BF16),
            jax.ShapeDtypeStruct((packs * rows, pairs * LANES), F32),
            jax.ShapeDtypeStruct((packs, pairs, 2, BLOCK, 3 * BLOCK), BF16),
            jax.ShapeDtypeStruct((packs, pairs, 8, LANES), F32),
        ),
        cost_estimate=pl.CostEstimate(
            flops=packs * pairs * 2 * 6 * BLOCK * BLOCK * LANES * 2,
            bytes_accessed=20_000_000,
            transcendentals=packs * pairs * 2 * 3 * BLOCK * BLOCK,
        ),
        name="attend",
    )(y_index, qkv, aux)


def attend_back_kernel(y_ref, qkv_ref, do_ref, inv_ref, exp_ref, dqkv_ref, dc_ref):
    y = y_ref[0]
    starts = (pl.multiple_of(y * BLOCK, BLOCK), pl.multiple_of((1 - y) * BLOCK, BLOCK))
    lane = lax.broadcasted_iota(jnp.int32, (1, LANES), 1)
    first = lane < HEAD_DIM
    ones = jnp.ones((8, BLOCK), BF16)
    lower = lax.broadcasted_iota(jnp.int32, (BLOCK, BLOCK), 1) <= lax.broadcasted_iota(
        jnp.int32, (BLOCK, BLOCK), 0
    )
    q_blk = [qkv_ref[pl.ds(s, BLOCK), 0:LANES] * 0.125 for s in starts]
    k_blk = [qkv_ref[pl.ds(s, BLOCK), LANES : 2 * LANES] for s in starts]
    v_blk = [qkv_ref[pl.ds(s, BLOCK), 2 * LANES : 3 * LANES] for s in starts]
    inv_blk = [inv_ref[pl.ds(s, BLOCK), :] for s in starts]
    do_blk = [
        (do_ref[pl.ds(s, BLOCK), :].astype(F32) * inv).astype(BF16)
        for s, inv in zip(starts, inv_blk)
    ]
    dq, dk, dv, dc = ([], []), ([], []), ([], []), ([], [])
    for head in range(2):
        mine = first if head == 0 else jnp.logical_not(first)
        v_head = [jnp.where(mine, v, jnp.zeros_like(v)) for v in v_blk]
        dk_acc, dv_acc, row_acc, col_acc = [None] * 2, [None] * 2, [None] * 2, [None] * 2
        for i in range(2):
            expos, probs, inner = [], [], None
            inv_col = inv_blk[i][:, head * HEAD_DIM : head * HEAD_DIM + 1]
            for j in range(i + 1):
                expo = exp_ref[0, 0, head, :, (i + j) * BLOCK : (i + j + 1) * BLOCK]
                grad_prob = dot_nt(do_blk[i], v_head[j])
                wide = expo.astype(F32)
                part = jnp.sum(wide * grad_prob, axis=1, keepdims=True)
                inner = part if inner is None else inner + part
                expos.append((expo, wide))
                probs.append(grad_prob)
            inner = inner * inv_col
            dq_acc = None
            for j in range(i + 1):
                expo, wide = expos[j]
                grad_score = wide * (probs[j] - inner)
                low = grad_score.astype(BF16)
                if i == j:
                    signed = jnp.where(lower, low, -low)
                else:
                    signed = low
                part = dot_nn(low, k_blk[j])
                dq_acc = part if dq_acc is None else dq_acc + part
                part = dot_tn(low, q_blk[i])
                dk_acc[j] = part if dk_acc[j] is None else dk_acc[j] + part
                part = dot_tn(expo, do_blk[i])
                dv_acc[j] = part if dv_acc[j] is None else dv_acc[j] + part
                part = dot_nt(ones, signed)
                row_acc[i] = part if row_acc[i] is None else row_acc[i] + part
                part = dot_nn(ones, signed)
                col_acc[j] = part if col_acc[j] is None else col_acc[j] + part
            dq[i].append(dq_acc)
        for j in range(2):
            dk[j].append(dk_acc[j])
            dv[j].append(dv_acc[j])
            dc[j].append(row_acc[j] - col_acc[j])
    row = lax.broadcasted_iota(jnp.int32, (8, BLOCK), 0)
    for i in range(2):
        rows = pl.ds(starts[i], BLOCK)
        dqkv_ref[rows, 0:LANES] = (jnp.where(first, *dq[i]) * 0.125).astype(BF16)
        dqkv_ref[rows, LANES : 2 * LANES] = jnp.where(first, *dk[i]).astype(BF16)
        dqkv_ref[rows, 2 * LANES : 3 * LANES] = jnp.where(first, *dv[i]).astype(BF16)
        dc_ref[0, :, rows] = jnp.where(row == 0, *dc[i])


def attend_back(y_index, qkv, d_out, inverse, expos, packs, pairs):
    rows = qkv.shape[0] // packs
    wide = 3 * LANES
    grid_spec = pltpu.PrefetchScalarGridSpec(
        num_scalar_prefetch=1,
        grid=(packs, pairs),
        in_specs=[
            pl.BlockSpec((rows, wide), lambda p, h, y: (p, h)),
            pl.BlockSpec((rows, LANES), lambda p, h, y: (p, h)),
            pl.BlockSpec((rows, LANES), lambda p, h, y: (p, h)),
            pl.BlockSpec((1, 1, 2, BLOCK, 3 * BLOCK), lambda p, h, y: (p, h, 0, 0, 0)),
        ],
        out_specs=[
            pl.BlockSpec((rows, wide), lambda p, h, y: (p, h)),
            pl.BlockSpec((1, 8, rows), lambda p, h, y: (h, 0, p)),
        ],
    )
    return pl.pallas_call(
        attend_back_kernel,
        grid_spec=grid_spec,
        out_shape=(
            jax.ShapeDtypeStruct((packs * rows, pairs * wide), BF16),
            jax.ShapeDtypeStruct((pairs, 8, packs * rows), F32),
        ),
        cost_estimate=pl.CostEstimate(
            flops=packs * pairs * 2 * 18 * BLOCK * BLOCK * LANES * 2,
            bytes_accessed=20_000_000,
            transcendentals=0,
        ),
        name="attend_back",
    )(y_index, qkv, d_out, inverse, expos)


class Place:
    def __init__(self):
        self.dp = lax.axis_size("dp")
        self.depth = self.dp // 4
        index = lax.axis_index("dp")
        self.core = index % 2
        self.x = (index // 2) % 2
        self.z = index // 4
        self.y = lax.axis_index("tensor")

    def swap_core(self, value):
        return lax.ppermute(value, "dp", [(i, i ^ 1) for i in range(self.dp)])

    def swap_x(self, value):
        return lax.ppermute(value, "dp", [(i, i ^ 2) for i in range(self.dp)])

    def swap_y(self, value):
        return lax.ppermute(value, "tensor", [(0, 1), (1, 0)])

    def swap_z(self, value, bit):
        return lax.ppermute(value, "dp", [(i, i ^ (4 * bit)) for i in range(self.dp)])

    def shift_z(self, value, step):
        n = self.dp
        return lax.ppermute(value, "dp", [(i, (i + 4 * step) % n) for i in range(n)])

    def gather_rows(self, shard):
        parts = [shard] + [self.shift_z(shard, s) for s in range(1, self.depth)]
        others = [self.swap_x(part) for part in parts]
        whole = jnp.zeros((self.depth, 2) + shard.shape, shard.dtype)
        for step in range(self.depth):
            spot = (self.z - step + self.depth) % self.depth
            for side, source in ((self.x, parts), (1 - self.x, others)):
                whole = lax.dynamic_update_slice(
                    whole, source[step][None, None], (spot, side, 0, 0)
                )
        return whole.reshape(-1, shard.shape[1]), parts

    def scatter_rows(self, grad):
        rows = grad.shape[0] // (2 * self.depth)
        blocks = grad.reshape(self.depth, 2, rows, grad.shape[1])
        there = lax.dynamic_index_in_dim(blocks, 1 - self.x, 1, False)
        here = lax.dynamic_index_in_dim(blocks, self.x, 1, False)
        both = here.astype(F32) + self.swap_x(there).astype(F32)
        low = both.astype(BF16)
        own = lax.dynamic_index_in_dim(both, self.z, 0, False)
        for step in range(1, self.depth):
            spot = (self.z + step) % self.depth
            sent = lax.dynamic_index_in_dim(low, spot, 0, False)
            own = own + self.shift_z(sent, step).astype(F32)
        return own

    def by_core(self, mine, other, axis):
        return jnp.where(
            self.core == 0,
            jnp.concatenate([mine, other], axis=axis),
            jnp.concatenate([other, mine], axis=axis),
        )

    def core_columns(self, weights):
        half = [w.shape[1] // 2 for w in weights]
        keep = [
            lax.dynamic_slice_in_dim(w, self.core * h, h, 1) for w, h in zip(weights, half)
        ]
        give = [
            lax.dynamic_slice_in_dim(w, (1 - self.core) * h, h, 1) for w, h in zip(weights, half)
        ]
        return keep, give

    def finish_grad(self, own):
        rows = own.shape[0] // 2
        keep = lax.dynamic_slice_in_dim(own, self.core * rows, rows, 0)
        give = lax.dynamic_slice_in_dim(own, (1 - self.core) * rows, rows, 0)
        return keep, self.swap_core(give.astype(BF16)).astype(F32)

    def gather_tokens(self, rows):
        near = self.swap_y(rows)
        return jnp.concatenate(
            [rows, near, self.swap_core(rows), self.swap_core(near)], axis=0
        )

    def scatter_tokens(self, partial_rows):
        rows = partial_rows.shape[0] // 4
        given = partial_rows[2 * rows :].astype(BF16)
        pack = partial_rows[: 2 * rows].astype(F32) + self.swap_core(given).astype(F32)
        return pack[:rows] + self.swap_y(pack[rows:].astype(BF16)).astype(F32)

    def sum_plane(self, value, combine):
        value = combine(value, self.swap_x(value))
        bit = 1
        while bit < self.depth:
            value = combine(value, self.swap_z(value, bit))
            bit *= 2
        return value


def after(value, *others):
    return lax.optimization_barrier((value,) + others)[0]


def interleave(parts):
    rows = parts[0].shape[0]
    stacked = jnp.stack([p.reshape(rows, -1, LANES) for p in parts], axis=2)
    return stacked.reshape(rows, -1)


def split_low(value):
    high = value.astype(BF16)
    return high, (value - high.astype(F32)).astype(BF16)


def paired_body(
    layer_in,
    segment_ids,
    norm1_gain,
    w_query,
    w_key,
    w_value,
    w_forget,
    forget_bias,
    w_output,
    norm2_gain,
    w_gate,
    w_up,
    w_down,
    clip_tau,
    out_grad,
):
    at = Place()
    rows_loc = layer_in.shape[0]
    pack = 2 * rows_loc
    width = layer_in.shape[1]
    heads = forget_bias.shape[0] // 2
    pairs = heads // 2
    y_index = at.y.astype(jnp.int32).reshape(1)
    d_rows = norm1_gain.shape[0]

    (wf_keep,), (wf_give,) = at.core_columns([w_forget])
    gains = jnp.stack([norm1_gain, norm2_gain])
    pad = jnp.zeros((16 - 2 - heads, d_rows), BF16)
    mine = jnp.concatenate([gains, wf_keep.T, pad], axis=0)
    theirs = at.swap_core(jnp.concatenate([gains, wf_give.T, pad], axis=0))
    small = at.by_core(mine, theirs, 1)
    small = jnp.where(
        at.x == 0,
        jnp.concatenate([small, at.swap_x(small)], axis=1),
        jnp.concatenate([at.swap_x(small), small], axis=1),
    )
    whole = jnp.zeros((16, at.depth, 4 * d_rows), BF16)
    for step in range(at.depth):
        part = small if step == 0 else at.shift_z(small, step)
        spot = (at.z - step + at.depth) % at.depth
        whole = lax.dynamic_update_slice(whole, part[:, None], (0, spot, 0))
    small = whole.reshape(16, width)
    gain_one = small[0:1].astype(F32)
    gain_two = small[1:2].astype(F32)
    forget_t = small[2 : 2 + heads]

    keep, give = at.core_columns([w_query, w_key, w_value, w_output, w_gate, w_up, w_down])

    def shard_of(kept, given):
        return at.by_core(kept, at.swap_core(given), 0)

    attn_shard = shard_of(
        jnp.concatenate([interleave(keep[:3]), keep[3]], axis=1),
        jnp.concatenate([interleave(give[:3]), give[3]], axis=1),
    )
    ffn_shard = shard_of(
        jnp.concatenate(keep[4:], axis=1),
        jnp.concatenate(give[4:], axis=1),
    )
    attn_all, attn_parts = at.gather_rows(attn_shard)
    units = keep[4].shape[1]
    gu_shard = after(ffn_shard[:, : 2 * units], attn_parts[-1], attn_parts[-2])
    gu_all, gu_parts = at.gather_rows(gu_shard)
    down_shard = after(ffn_shard[:, 2 * units :], gu_parts[-1], gu_parts[-2])
    down_all, _ = at.gather_rows(down_shard)
    qkv_cols = 3 * heads * HEAD_DIM
    w_qkv, wo_all = attn_all[:, :qkv_cols], attn_all[:, qkv_cols:]

    x_own = layer_in.astype(F32)
    scale_one = lax.rsqrt(jnp.mean(x_own * x_own, axis=1, keepdims=True) + EPSILON)
    unit_one = x_own * scale_one
    normed_one = at.gather_tokens((unit_one * gain_one).astype(BF16))
    qkv = dot_nn(normed_one, w_qkv).astype(BF16)

    bias = lax.dynamic_slice_in_dim(forget_bias, at.core * heads, heads, 0)
    logits = dot_nt(forget_t, normed_one) + bias[:, None]
    logs = jax.nn.log_sigmoid(logits).reshape(heads, 2, 2, rows_loc)
    steps = jnp.arange(rows_loc, dtype=jnp.int32)
    upper = (steps[:, None] <= steps[None, :]).astype(F32)
    sums = jnp.einsum("hpbt,ts->hpbs", logs, upper, precision=HIGHEST)
    total = sums[..., -1:]
    later = at.y.astype(F32)
    cumul = jnp.stack(
        [sums[:, :, 0] + later * total[:, :, 1], sums[:, :, 1] + (1.0 - later) * total[:, :, 0]],
        axis=2,
    ).reshape(heads, 2 * pack)
    seg_own = segment_ids[0].reshape(2, rows_loc)
    seg_own = jnp.where(at.y == 0, seg_own, seg_own[::-1]).reshape(1, pack)
    seg_both = jnp.concatenate([seg_own, at.swap_core(seg_own)], axis=1).astype(F32)
    aux = jnp.concatenate(
        [
            cumul.reshape(pairs, 2, 2 * pack),
            jnp.broadcast_to(seg_both[None], (pairs, 6, 2 * pack)),
        ],
        axis=1,
    )
    mixed, inverse, expos, tops = attend(y_index, qkv, aux, 2, pairs)

    attn_part = dot_nt(mixed, wo_all)
    resid = x_own + at.scatter_tokens(attn_part)
    scale_two = lax.rsqrt(jnp.mean(resid * resid, axis=1, keepdims=True) + EPSILON)
    unit_two = resid * scale_two
    normed_two = at.gather_tokens((unit_two * gain_two).astype(BF16))
    grad_rows = at.gather_tokens(out_grad)

    maxima = jnp.max(tops[:, :, :2], axis=(0, 3)).reshape(1, heads)
    maxima = jnp.pad(maxima, ((0, 7), (0, LANES - heads)))
    maxima = at.sum_plane(maxima, jnp.maximum)
    maxima = at.by_core(maxima[0, :heads], at.swap_core(maxima)[0, :heads], 0)
    clip_factor = jnp.minimum(1.0, clip_tau / jnp.maximum(maxima, 1.0))
    columns = jnp.repeat(jnp.sqrt(clip_factor), HEAD_DIM)
    clipped_query = (w_query.astype(F32) * columns[None, :]).astype(BF16)
    clipped_key = (w_key.astype(F32) * columns[None, :]).astype(BF16)

    gate_up = dot_nn(normed_two, gu_all)
    gate_pre, up_pre = gate_up[:, :units], gate_up[:, units:]
    gate_sig = jax.nn.sigmoid(gate_pre)
    gate_act = gate_pre * gate_sig
    hidden = (gate_act * up_pre).astype(BF16)
    g_down = at.scatter_rows(dot_tn(grad_rows, hidden).astype(BF16))
    grad_hidden = dot_nn(grad_rows, down_all)
    grad_gate = (grad_hidden * up_pre * gate_sig * (1.0 + gate_pre * (1.0 - gate_sig))).astype(BF16)
    grad_up = (grad_hidden * gate_act).astype(BF16)
    g_gate = at.scatter_rows(dot_tn(normed_two, grad_gate).astype(BF16))
    g_up = at.scatter_rows(dot_tn(normed_two, grad_up).astype(BF16))
    grad_gu = jnp.concatenate([grad_gate, grad_up], axis=1)
    grad_two = at.scatter_tokens(dot_nt(grad_gu, gu_all))
    layer_out = (resid + at.scatter_tokens(dot_nt(hidden, down_all))).astype(BF16)

    weighted = gain_two * grad_two
    inner_two = jnp.mean(unit_two * weighted, axis=1, keepdims=True)
    norm2_part = jnp.sum(grad_two * unit_two, axis=0)
    grad_resid = out_grad.astype(F32) + scale_two * (weighted - unit_two * inner_two)
    grad_attn = at.gather_tokens(grad_resid.astype(BF16))

    grad_mixed = dot_nn(grad_attn, wo_all).astype(BF16)
    g_output = at.scatter_rows(dot_tn(grad_attn, mixed).astype(BF16))
    d_qkv, d_cum = attend_back(y_index, qkv, grad_mixed, inverse, expos, 2, pairs)
    g_qkv = at.scatter_rows(dot_tn(normed_one, d_qkv).astype(BF16))
    d_cum = d_cum[:, :2].reshape(heads, 2, 2, rows_loc)
    back = jnp.einsum("hpbt,st->hpbs", d_cum, upper, precision=HIGHEST)
    total = back[..., :1]
    d_log = jnp.stack(
        [back[:, :, 0] + (1.0 - later) * total[:, :, 1], back[:, :, 1] + later * total[:, :, 0]],
        axis=2,
    ).reshape(heads, 2 * pack)
    d_logit = d_log * jax.nn.sigmoid(-logits)
    bias_part = jnp.sum(d_logit, axis=1)
    d_split = jnp.concatenate(split_low(d_logit), axis=0)
    forget_part = dot_nn(d_split, normed_one)
    forget_part = forget_part[:heads] + forget_part[heads:]
    grad_one = dot_nt(d_qkv, w_qkv) + dot_tn(d_split, jnp.concatenate([forget_t, forget_t], axis=0))
    grad_one = at.scatter_tokens(grad_one)

    weighted = gain_one * grad_one
    inner_one = jnp.mean(unit_one * weighted, axis=1, keepdims=True)
    norm1_part = jnp.sum(grad_one * unit_one, axis=0)
    x_grad = (grad_resid + scale_one * (weighted - unit_one * inner_one)).astype(BF16)

    small = jnp.concatenate(
        [
            norm1_part[None],
            norm2_part[None],
            forget_part,
            jnp.pad(bias_part[None], ((0, 0), (0, width - heads))),
            jnp.zeros((16 - 3 - heads, width), F32),
        ],
        axis=0,
    )
    small = at.sum_plane(small, jnp.add)
    other = at.swap_core(small)
    norms = small[:2] + other[:2]
    norms = norms + at.swap_y(norms)
    norms = lax.dynamic_slice_in_dim(norms, at.y * (width // 2), width // 2, 1)
    forget = at.by_core(small[2 : 2 + heads], other[2 : 2 + heads], 0)
    index = lax.axis_index("dp")
    g_forget = lax.dynamic_slice_in_dim(forget, index * d_rows, d_rows, 1).T
    g_bias = at.by_core(small[2 + heads, :heads], other[2 + heads, :heads], 0)

    def place(own):
        keep, got = at.finish_grad(own)
        return at.by_core(keep, got, 1)

    keep, got = at.finish_grad(g_qkv)

    def third(which):
        def cut(value):
            return value.reshape(d_rows, pairs, 3, LANES)[:, :, which].reshape(d_rows, -1)

        return at.by_core(cut(keep), cut(got), 1)

    return (
        layer_out,
        x_grad,
        norms[0],
        third(0),
        third(1),
        third(2),
        g_forget,
        g_bias,
        place(g_output),
        norms[1],
        place(g_gate),
        place(g_up),
        place(g_down),
        clip_factor,
        clipped_query,
        clipped_key,
    )


def pick_body(mesh):
    dp, tensor = mesh.shape["dp"], mesh.shape["tensor"]

    def body(*args):
        rows, heads = args[0].shape[0], args[7].shape[0]
        depth = dp // 4
        paired = (
            tensor == 2
            and dp % 4 == 0
            and depth & (depth - 1) == 0
            and rows == BLOCK
            and heads % 4 == 0
        )
        return (paired_body if paired else general_body)(*args)

    return body
def solution(mesh):
    return jax.shard_map(
        pick_body(mesh),
        mesh=mesh,
        in_specs=(
            P(("dp", "tensor"), None),
            P("dp", None),
            P("dp"),
            P("dp", "tensor"),
            P("dp", "tensor"),
            P("dp", "tensor"),
            P("dp", "tensor"),
            P("tensor"),
            P("dp", "tensor"),
            P("dp"),
            P("dp", "tensor"),
            P("dp", "tensor"),
            P("dp", "tensor"),
            P("tensor"),
            P(("dp", "tensor"), None),
        ),
        out_specs=(
            P(("dp", "tensor"), None),
            P(("dp", "tensor"), None),
            P("tensor"),
            P("dp", "tensor"),
            P("dp", "tensor"),
            P("dp", "tensor"),
            P("dp", "tensor"),
            P("tensor"),
            P("dp", "tensor"),
            P("tensor"),
            P("dp", "tensor"),
            P("dp", "tensor"),
            P("dp", "tensor"),
            P("tensor"),
            P("dp", "tensor"),
            P("dp", "tensor"),
        ),
        check_vma=False,
    )
```

```python
import math
from functools import partial

import jax
import jax.numpy as jnp
from jax import lax
from jax.experimental import pallas as pl
from jax.experimental.pallas import tpu as pltpu
from jax.sharding import PartitionSpec as P

HEAD_DIM = 64
BLOCK = 256
LANES = 128
EPSILON = 1e-06
HIGHEST = lax.Precision.HIGHEST
NEGATIVE = -1e30
F32 = jnp.float32
BF16 = jnp.bfloat16
def combined_all(part, axis, combine):
    gathered = jax.tree.map(lambda a: lax.all_gather(a, axis), part)

    def take(source):
        return jax.tree.map(lambda a: lax.dynamic_index_in_dim(a, source, 0, False), gathered)

    return lax.fori_loop(
        1, lax.axis_size(axis), lambda source, state: combine(state, take(source)), take(0)
    )


def contract_last(left_op, right_op):
    return lax.dot_general(
        left_op, right_op, (((1,), (1,)), ((), ())), preferred_element_type=jnp.float32
    )


def contract_first(left_op, right_op):
    return lax.dot_general(
        left_op, right_op, (((0,), (0,)), ((), ())), preferred_element_type=jnp.float32
    )


def block_terms(q_blk, keys_all, cumul, seg_row, offset, rows_blk):
    positions = jnp.arange(keys_all.shape[0], dtype=jnp.int32)
    q_pos = offset + jnp.arange(rows_blk, dtype=jnp.int32)
    allowed = (seg_row[:, None] == seg_row[None, :]) & (
        q_pos[:, None] // BLOCK >= positions[None, :] // BLOCK
    )
    signs = jnp.where(positions[None, :] <= q_pos[:, None], 1.0, -1.0).astype(jnp.float32)
    raw_blk = jnp.einsum("qhe,khe->hqk", q_blk, keys_all, preferred_element_type=jnp.float32) * (
        1.0 / math.sqrt(HEAD_DIM)
    )
    differ = cumul.T[:, :, None] - cumul.T[:, None, :]
    scores = jnp.where(allowed[None], raw_blk + signs[None] * differ, NEGATIVE)
    return (raw_blk, scores, allowed, signs)


def combine(former, latter):
    return (
        jnp.maximum(former[0], latter[0]),
        former[1] + latter[1],
        former[2] + latter[2],
        former[3] + latter[3],
    )


def general_body(
    layer_in,
    segment_ids,
    norm1_gain,
    w_query,
    w_key,
    w_value,
    w_forget,
    forget_bias,
    w_output,
    norm2_gain,
    w_gate,
    w_up,
    w_down,
    clip_tau,
    out_grad,
):
    gain_one, wq_all, wk_all, wv_all, wf_all, wo_all, gain_two, wg_all, wu_all, wd_all = (
        lax.all_gather(norm1_gain, "dp", axis=0, tiled=True),
        lax.all_gather(w_query, "dp", axis=0, tiled=True),
        lax.all_gather(w_key, "dp", axis=0, tiled=True),
        lax.all_gather(w_value, "dp", axis=0, tiled=True),
        lax.all_gather(w_forget, "dp", axis=0, tiled=True),
        lax.all_gather(w_output, "dp", axis=0, tiled=True),
        lax.all_gather(norm2_gain, "dp", axis=0, tiled=True),
        lax.all_gather(w_gate, "dp", axis=0, tiled=True),
        lax.all_gather(w_up, "dp", axis=0, tiled=True),
        lax.all_gather(w_down, "dp", axis=0, tiled=True),
    )
    gain_one = gain_one.astype(jnp.float32)
    gain_two = gain_two.astype(jnp.float32)
    tok_local = layer_in.shape[0]
    tokens = tok_local * lax.axis_size("tensor")
    heads_loc = forget_bias.shape[0]
    row_start = lax.axis_index("tensor") * tok_local
    seg_row = segment_ids[0]
    factor = 1.0 / math.sqrt(HEAD_DIM)
    rows_full = lax.all_gather(layer_in, "tensor", axis=0, tiled=True).astype(jnp.float32)
    scale_one = lax.rsqrt(jnp.mean(rows_full * rows_full, axis=1, keepdims=True) + EPSILON)
    unit_one = rows_full * scale_one
    normed_one = (unit_one * gain_one).astype(jnp.bfloat16)
    queries = (
        jnp.dot(normed_one, wq_all, preferred_element_type=jnp.float32)
        .astype(jnp.bfloat16)
        .reshape(tokens, heads_loc, HEAD_DIM)
    )
    keys_all = (
        jnp.dot(normed_one, wk_all, preferred_element_type=jnp.float32)
        .astype(jnp.bfloat16)
        .reshape(tokens, heads_loc, HEAD_DIM)
    )
    values_all = (
        jnp.dot(normed_one, wv_all, preferred_element_type=jnp.float32)
        .astype(jnp.bfloat16)
        .reshape(tokens, heads_loc, HEAD_DIM)
    )
    logits = jnp.dot(normed_one, wf_all, preferred_element_type=jnp.float32) + forget_bias
    cumul = jnp.cumsum(jax.nn.log_sigmoid(logits), axis=0)
    rows_blk = min(512, tokens)
    blocks = tokens // rows_blk
    numbers = jnp.arange(blocks, dtype=jnp.int32)

    def forward_block(number):
        offset = number * rows_blk
        raw_blk, scores, allowed, signs = block_terms(
            queries, keys_all, cumul, seg_row, offset, rows_blk
        )
        top_blk = jnp.max(jnp.where(allowed[None], raw_blk, NEGATIVE), axis=(1, 2))
        row_peak = jnp.max(scores, axis=2, keepdims=True)
        expo_blk = jnp.exp(scores - row_peak)
        totals = jnp.sum(expo_blk, axis=2, keepdims=True)
        weights = (expo_blk / totals).astype(jnp.bfloat16)
        mixed_out = jnp.einsum(
            "hqk,khe->qhe", weights, values_all, preferred_element_type=jnp.float32
        ).astype(jnp.bfloat16)
        return (mixed_out, (row_peak + jnp.log(totals))[:, :, 0], top_blk)

    mixed_out, log_sums, top_blk = lax.map(forward_block, numbers)
    mixed_flat = mixed_out.reshape(tokens, heads_loc * HEAD_DIM)
    maxima = jnp.max(top_blk, axis=0)
    attn_part = contract_last(mixed_flat, wo_all)
    resid_full = rows_full + lax.psum(attn_part.astype(jnp.bfloat16), "tensor").astype(jnp.float32)
    scale_full = lax.rsqrt(jnp.mean(resid_full * resid_full, axis=1, keepdims=True) + EPSILON)
    normed_two = (resid_full * scale_full * gain_two).astype(jnp.bfloat16)
    resid_part = lax.dynamic_slice_in_dim(resid_full, row_start, tok_local, 0)
    scale_two = lax.dynamic_slice_in_dim(scale_full, row_start, tok_local, 0)
    gate_pre = jnp.dot(normed_two, wg_all, preferred_element_type=jnp.float32)
    up_pre = jnp.dot(normed_two, wu_all, preferred_element_type=jnp.float32)
    gate_sig = jax.nn.sigmoid(gate_pre)
    gate_act = gate_pre * gate_sig
    hidden = (gate_act * up_pre).astype(jnp.bfloat16)
    ffn_part = lax.psum_scatter(
        contract_last(hidden, wd_all).astype(jnp.bfloat16),
        "tensor",
        scatter_dimension=0,
        tiled=True,
    ).astype(jnp.float32)
    layer_out = (resid_part + ffn_part).astype(jnp.bfloat16)
    grad_full = lax.all_gather(out_grad, "tensor", axis=0, tiled=True)
    grad_hidden = jnp.dot(grad_full, wd_all, preferred_element_type=jnp.float32)
    grad_gate = (grad_hidden * up_pre * gate_sig * (1.0 + gate_pre * (1.0 - gate_sig))).astype(
        jnp.bfloat16
    )
    grad_up = (grad_hidden * gate_act).astype(jnp.bfloat16)
    g_down = contract_first(grad_full, hidden)
    g_gate = contract_first(normed_two, grad_gate)
    g_up = contract_first(normed_two, grad_up)
    grad_normed = contract_last(grad_gate, wg_all) + contract_last(grad_up, wu_all)
    grad_two = lax.psum_scatter(
        grad_normed.astype(jnp.bfloat16), "tensor", scatter_dimension=0, tiled=True
    ).astype(jnp.float32)
    unit_two = resid_part * scale_two
    inner_two = jnp.mean(unit_two * gain_two * grad_two, axis=1, keepdims=True)
    norm2_part = jnp.sum(grad_two * unit_two, axis=0)
    grad_resid = out_grad.astype(jnp.float32) + scale_two * (
        gain_two * grad_two - unit_two * inner_two
    )
    grad_attn = lax.all_gather(grad_resid.astype(jnp.bfloat16), "tensor", axis=0, tiled=True)
    g_output = contract_first(grad_attn, mixed_flat)
    grad_mixed = jnp.dot(grad_attn, wo_all, preferred_element_type=jnp.float32).astype(jnp.bfloat16)
    grad_mixed = grad_mixed.reshape(blocks, rows_blk, heads_loc, HEAD_DIM)

    def backward_block(carried, block_in):
        key_acc, value_acc, column_acc = carried
        number, log_blk, grad_blk = block_in
        offset = number * rows_blk
        raw_blk, scores, allowed, signs = block_terms(
            queries, keys_all, cumul, seg_row, offset, rows_blk
        )
        prob_blk = jnp.exp(scores - log_blk[:, :, None])
        weights = prob_blk.astype(jnp.bfloat16)
        grad_prob = jnp.einsum(
            "qhe,khe->hqk", grad_blk, values_all, preferred_element_type=jnp.float32
        )
        inner = jnp.sum(prob_blk * grad_prob, axis=2, keepdims=True)
        grad_scores = (prob_blk * (grad_prob - inner)).astype(jnp.bfloat16)
        value_acc = value_acc + jnp.einsum(
            "hqk,qhe->khe", weights, grad_blk, preferred_element_type=jnp.float32
        )
        key_acc = key_acc + jnp.einsum(
            "hqk,qhe->khe", grad_scores, queries, preferred_element_type=jnp.float32
        )
        grad_query = (
            jnp.einsum("hqk,khe->qhe", grad_scores, keys_all, preferred_element_type=jnp.float32)
            * factor
        ).astype(jnp.bfloat16)
        signed = grad_scores.astype(jnp.float32) * signs[None]
        column_acc = column_acc - jnp.sum(signed, axis=1).T
        return ((key_acc, value_acc, column_acc), (grad_query, jnp.sum(signed, axis=2).T))

    start_acc = (
        jnp.zeros((tokens, heads_loc, HEAD_DIM), jnp.float32),
        jnp.zeros((tokens, heads_loc, HEAD_DIM), jnp.float32),
        jnp.zeros((tokens, heads_loc), jnp.float32),
    )
    (key_acc, value_acc, column_acc), (grad_query, row_parts) = lax.scan(
        backward_block, start_acc, (numbers, log_sums, grad_mixed)
    )
    grad_q = grad_query.reshape(tokens, heads_loc * HEAD_DIM)
    grad_k = (key_acc * factor).astype(jnp.bfloat16).reshape(tokens, heads_loc * HEAD_DIM)
    grad_v = value_acc.astype(jnp.bfloat16).reshape(tokens, heads_loc * HEAD_DIM)
    grad_cum = row_parts.reshape(tokens, heads_loc) + column_acc
    grad_logs = jnp.cumsum(grad_cum[::-1], axis=0)[::-1]
    grad_logit = grad_logs * jax.nn.sigmoid(-logits)
    g_bias = jnp.sum(grad_logit, axis=0)
    g_forget = jnp.einsum(
        "td,th->dh", normed_one, grad_logit, precision=HIGHEST, preferred_element_type=jnp.float32
    )
    g_query = contract_first(normed_one, grad_q)
    g_key = contract_first(normed_one, grad_k)
    g_value = contract_first(normed_one, grad_v)
    grad_one = (
        contract_last(grad_q, wq_all)
        + contract_last(grad_k, wk_all)
        + contract_last(grad_v, wv_all)
    )
    grad_one = grad_one + jnp.einsum(
        "th,dh->td", grad_logit, wf_all, precision=HIGHEST, preferred_element_type=jnp.float32
    )
    weighted = gain_one * grad_one
    grad_rows_one = scale_one * (
        weighted - unit_one * jnp.mean(unit_one * weighted, axis=1, keepdims=True)
    )
    norm1_part = jnp.sum(grad_one * unit_one, axis=0)
    grad_input, g_norm1_part, g_norm2_part = (
        lax.psum_scatter(
            grad_rows_one.astype(jnp.bfloat16), "tensor", scatter_dimension=0, tiled=True
        ).astype(jnp.float32),
        lax.psum_scatter(
            norm1_part.astype(jnp.bfloat16), "tensor", scatter_dimension=0, tiled=True
        ).astype(jnp.float32),
        lax.psum_scatter(
            norm2_part.astype(jnp.bfloat16), "tensor", scatter_dimension=0, tiled=True
        ).astype(jnp.float32),
    )
    x_grad = (grad_resid + grad_input).astype(jnp.bfloat16)
    g_query, g_key, g_value, g_forget, g_output, g_gate, g_up, g_down = (
        lax.psum_scatter(
            g_query.astype(jnp.bfloat16), "dp", scatter_dimension=0, tiled=True
        ).astype(jnp.float32),
        lax.psum_scatter(g_key.astype(jnp.bfloat16), "dp", scatter_dimension=0, tiled=True).astype(
            jnp.float32
        ),
        lax.psum_scatter(
            g_value.astype(jnp.bfloat16), "dp", scatter_dimension=0, tiled=True
        ).astype(jnp.float32),
        lax.psum_scatter(
            g_forget.astype(jnp.bfloat16), "dp", scatter_dimension=0, tiled=True
        ).astype(jnp.float32),
        lax.psum_scatter(
            g_output.astype(jnp.bfloat16), "dp", scatter_dimension=0, tiled=True
        ).astype(jnp.float32),
        lax.psum_scatter(g_gate.astype(jnp.bfloat16), "dp", scatter_dimension=0, tiled=True).astype(
            jnp.float32
        ),
        lax.psum_scatter(g_up.astype(jnp.bfloat16), "dp", scatter_dimension=0, tiled=True).astype(
            jnp.float32
        ),
        lax.psum_scatter(g_down.astype(jnp.bfloat16), "dp", scatter_dimension=0, tiled=True).astype(
            jnp.float32
        ),
    )
    maxima, g_bias, g_norm1, g_norm2 = combined_all(
        (maxima, g_bias, g_norm1_part, g_norm2_part), "dp", combine
    )
    clip_factor = jnp.minimum(1.0, clip_tau / jnp.maximum(maxima, 1.0))
    columns = jnp.repeat(jnp.sqrt(clip_factor), HEAD_DIM)
    clipped_query = (w_query.astype(jnp.float32) * columns[None, :]).astype(jnp.bfloat16)
    clipped_key = (w_key.astype(jnp.float32) * columns[None, :]).astype(jnp.bfloat16)
    return (
        layer_out,
        x_grad,
        g_norm1,
        g_query,
        g_key,
        g_value,
        g_forget,
        g_bias,
        g_output,
        g_norm2,
        g_gate,
        g_up,
        g_down,
        clip_factor,
        clipped_query,
        clipped_key,
    )


def dot_nt(left, right):
    return lax.dot_general(left, right, (((1,), (1,)), ((), ())), preferred_element_type=F32)


def dot_nn(left, right):
    return lax.dot_general(left, right, (((1,), (0,)), ((), ())), preferred_element_type=F32)


def dot_tn(left, right):
    return lax.dot_general(left, right, (((0,), (0,)), ((), ())), preferred_element_type=F32)


def attend_kernel(y_ref, qkv_ref, aux_ref, o_ref, inv_ref, exp_ref, top_ref):
    y = y_ref[0]
    starts = (pl.multiple_of(y * BLOCK, BLOCK), pl.multiple_of((1 - y) * BLOCK, BLOCK))
    lane = lax.broadcasted_iota(jnp.int32, (1, LANES), 1)
    first = lane < HEAD_DIM
    aux = [aux_ref[0, :, pl.ds(start, BLOCK)] for start in starts]
    aux_col = [a.T for a in aux]
    q_blk = [qkv_ref[pl.ds(s, BLOCK), 0:LANES] * 0.125 for s in starts]
    k_blk = [qkv_ref[pl.ds(s, BLOCK), LANES : 2 * LANES] for s in starts]
    v_blk = [qkv_ref[pl.ds(s, BLOCK), 2 * LANES : 3 * LANES] for s in starts]
    same = {}
    for i, j in ((0, 0), (1, 0), (1, 1)):
        same[i, j] = aux_col[i][:, 2:3] == aux[j][2:3, :]
    tops = []
    results = [[], []]
    for head in range(2):
        mine = first if head == 0 else jnp.logical_not(first)
        top = None
        v_ext = [jnp.where(mine, v, jnp.ones_like(v)) for v in v_blk]
        k_head = [jnp.where(mine, k, jnp.zeros_like(k)) for k in k_blk]
        for i in range(2):
            scores = []
            for j in range(i + 1):
                raw = dot_nt(q_blk[i], k_head[j])
                seen = jnp.where(same[i, j], raw, NEGATIVE)
                high = jnp.max(seen, axis=0, keepdims=True)
                top = high if top is None else jnp.maximum(top, high)
                differ = aux_col[i][:, head : head + 1] - aux[j][head : head + 1, :]
                scores.append(seen - jnp.abs(differ))
            peak = jnp.max(scores[0], axis=1, keepdims=True)
            if i == 1:
                peak = jnp.maximum(peak, jnp.max(scores[1], axis=1, keepdims=True))
            acc = None
            for j in range(i + 1):
                weights = jnp.exp(scores[j] - peak).astype(BF16)
                exp_ref[0, 0, head, :, (i + j) * BLOCK : (i + j + 1) * BLOCK] = weights
                part = dot_nn(weights, v_ext[j])
                acc = part if acc is None else acc + part
            results[i].append(acc)
        tops.append(jnp.maximum(top[:, :LANES], top[:, LANES:]))
    for i in range(2):
        one, two = results[i]
        total = pltpu.roll(jnp.where(first, two, one), HEAD_DIM, 1)
        inverse = 1.0 / total
        inv_ref[pl.ds(starts[i], BLOCK), :] = inverse
        o_ref[pl.ds(starts[i], BLOCK), :] = (jnp.where(first, one, two) * inverse).astype(BF16)
    row = lax.broadcasted_iota(jnp.int32, (8, LANES), 0)
    top_ref[0, 0] = jnp.where(row == 0, tops[0], tops[1])


def attend(y_index, qkv, aux, packs, pairs):
    rows = qkv.shape[0] // packs
    wide = 3 * LANES
    grid_spec = pltpu.PrefetchScalarGridSpec(
        num_scalar_prefetch=1,
        grid=(packs, pairs),
        in_specs=[
            pl.BlockSpec((rows, wide), lambda p, h, y: (p, h)),
            pl.BlockSpec((1, 8, rows), lambda p, h, y: (h, 0, p)),
        ],
        out_specs=[
            pl.BlockSpec((rows, LANES), lambda p, h, y: (p, h)),
            pl.BlockSpec((rows, LANES), lambda p, h, y: (p, h)),
            pl.BlockSpec((1, 1, 2, BLOCK, 3 * BLOCK), lambda p, h, y: (p, h, 0, 0, 0)),
            pl.BlockSpec((1, 1, 8, LANES), lambda p, h, y: (p, h, 0, 0)),
        ],
    )
    return pl.pallas_call(
        attend_kernel,
        grid_spec=grid_spec,
        out_shape=(
            jax.ShapeDtypeStruct((packs * rows, pairs * LANES), BF16),
            jax.ShapeDtypeStruct((packs * rows, pairs * LANES), F32),
            jax.ShapeDtypeStruct((packs, pairs, 2, BLOCK, 3 * BLOCK), BF16),
            jax.ShapeDtypeStruct((packs, pairs, 8, LANES), F32),
        ),
        cost_estimate=pl.CostEstimate(
            flops=packs * pairs * 2 * 6 * BLOCK * BLOCK * LANES * 2,
            bytes_accessed=20_000_000,
            transcendentals=packs * pairs * 2 * 3 * BLOCK * BLOCK,
        ),
        name="attend",
    )(y_index, qkv, aux)


def attend_back_kernel(y_ref, qkv_ref, do_ref, inv_ref, exp_ref, dqkv_ref, dc_ref):
    y = y_ref[0]
    starts = (pl.multiple_of(y * BLOCK, BLOCK), pl.multiple_of((1 - y) * BLOCK, BLOCK))
    lane = lax.broadcasted_iota(jnp.int32, (1, LANES), 1)
    first = lane < HEAD_DIM
    ones = jnp.ones((8, BLOCK), BF16)
    lower = lax.broadcasted_iota(jnp.int32, (BLOCK, BLOCK), 1) <= lax.broadcasted_iota(
        jnp.int32, (BLOCK, BLOCK), 0
    )
    q_blk = [qkv_ref[pl.ds(s, BLOCK), 0:LANES] * 0.125 for s in starts]
    k_blk = [qkv_ref[pl.ds(s, BLOCK), LANES : 2 * LANES] for s in starts]
    v_blk = [qkv_ref[pl.ds(s, BLOCK), 2 * LANES : 3 * LANES] for s in starts]
    inv_blk = [inv_ref[pl.ds(s, BLOCK), :] for s in starts]
    do_blk = [
        (do_ref[pl.ds(s, BLOCK), :].astype(F32) * inv).astype(BF16)
        for s, inv in zip(starts, inv_blk)
    ]
    dq, dk, dv, dc = ([], []), ([], []), ([], []), ([], [])
    for head in range(2):
        mine = first if head == 0 else jnp.logical_not(first)
        v_head = [jnp.where(mine, v, jnp.zeros_like(v)) for v in v_blk]
        dk_acc, dv_acc, row_acc, col_acc = [None] * 2, [None] * 2, [None] * 2, [None] * 2
        for i in range(2):
            expos, probs, inner = [], [], None
            inv_col = inv_blk[i][:, head * HEAD_DIM : head * HEAD_DIM + 1]
            for j in range(i + 1):
                expo = exp_ref[0, 0, head, :, (i + j) * BLOCK : (i + j + 1) * BLOCK]
                grad_prob = dot_nt(do_blk[i], v_head[j])
                wide = expo.astype(F32)
                part = jnp.sum(wide * grad_prob, axis=1, keepdims=True)
                inner = part if inner is None else inner + part
                expos.append((expo, wide))
                probs.append(grad_prob)
            inner = inner * inv_col
            dq_acc = None
            for j in range(i + 1):
                expo, wide = expos[j]
                grad_score = wide * (probs[j] - inner)
                low = grad_score.astype(BF16)
                if i == j:
                    signed = jnp.where(lower, low, -low)
                else:
                    signed = low
                part = dot_nn(low, k_blk[j])
                dq_acc = part if dq_acc is None else dq_acc + part
                part = dot_tn(low, q_blk[i])
                dk_acc[j] = part if dk_acc[j] is None else dk_acc[j] + part
                part = dot_tn(expo, do_blk[i])
                dv_acc[j] = part if dv_acc[j] is None else dv_acc[j] + part
                part = dot_nt(ones, signed)
                row_acc[i] = part if row_acc[i] is None else row_acc[i] + part
                part = dot_nn(ones, signed)
                col_acc[j] = part if col_acc[j] is None else col_acc[j] + part
            dq[i].append(dq_acc)
        for j in range(2):
            dk[j].append(dk_acc[j])
            dv[j].append(dv_acc[j])
            dc[j].append(row_acc[j] - col_acc[j])
    row = lax.broadcasted_iota(jnp.int32, (8, BLOCK), 0)
    for i in range(2):
        rows = pl.ds(starts[i], BLOCK)
        dqkv_ref[rows, 0:LANES] = (jnp.where(first, *dq[i]) * 0.125).astype(BF16)
        dqkv_ref[rows, LANES : 2 * LANES] = jnp.where(first, *dk[i]).astype(BF16)
        dqkv_ref[rows, 2 * LANES : 3 * LANES] = jnp.where(first, *dv[i]).astype(BF16)
        dc_ref[0, :, rows] = jnp.where(row == 0, *dc[i])


def attend_back(y_index, qkv, d_out, inverse, expos, packs, pairs):
    rows = qkv.shape[0] // packs
    wide = 3 * LANES
    grid_spec = pltpu.PrefetchScalarGridSpec(
        num_scalar_prefetch=1,
        grid=(packs, pairs),
        in_specs=[
            pl.BlockSpec((rows, wide), lambda p, h, y: (p, h)),
            pl.BlockSpec((rows, LANES), lambda p, h, y: (p, h)),
            pl.BlockSpec((rows, LANES), lambda p, h, y: (p, h)),
            pl.BlockSpec((1, 1, 2, BLOCK, 3 * BLOCK), lambda p, h, y: (p, h, 0, 0, 0)),
        ],
        out_specs=[
            pl.BlockSpec((rows, wide), lambda p, h, y: (p, h)),
            pl.BlockSpec((1, 8, rows), lambda p, h, y: (h, 0, p)),
        ],
    )
    return pl.pallas_call(
        attend_back_kernel,
        grid_spec=grid_spec,
        out_shape=(
            jax.ShapeDtypeStruct((packs * rows, pairs * wide), BF16),
            jax.ShapeDtypeStruct((pairs, 8, packs * rows), F32),
        ),
        cost_estimate=pl.CostEstimate(
            flops=packs * pairs * 2 * 18 * BLOCK * BLOCK * LANES * 2,
            bytes_accessed=20_000_000,
            transcendentals=0,
        ),
        name="attend_back",
    )(y_index, qkv, d_out, inverse, expos)


class Place:
    def __init__(self):
        self.dp = lax.axis_size("dp")
        self.depth = self.dp // 4
        index = lax.axis_index("dp")
        self.core = index % 2
        self.x = (index // 2) % 2
        self.z = index // 4
        self.y = lax.axis_index("tensor")

    def swap_core(self, value):
        return lax.ppermute(value, "dp", [(i, i ^ 1) for i in range(self.dp)])

    def swap_y(self, value):
        return lax.ppermute(value, "tensor", [(0, 1), (1, 0)])

    def ring(self, value, step):
        spots = [4 * z for z in range(self.depth)]
        spots += [4 * z + 2 for z in reversed(range(self.depth))]
        count = len(spots)
        pairs = [
            (spots[r] + core, spots[(r + step) % count] + core)
            for r in range(count)
            for core in (0, 1)
        ]
        return lax.ppermute(value, "dp", pairs)

    def block_of(self, step):
        count = 2 * self.depth
        spot = (jnp.where(self.x == 0, self.z, count - 1 - self.z) + step + count) % count
        return jnp.where(spot < self.depth, 2 * spot, 2 * (count - 1 - spot) + 1)

    def gather_rings(self, shards):
        count = 2 * self.depth
        half = self.depth

        def put(whole, part, step, side=0):
            return lax.dynamic_update_slice(whole, part[None], (self.block_of(step), side, 0, 0))

        wholes = [put(jnp.zeros((count,) + s.shape, s.dtype), s, 0) for s in shards]
        up, down = list(shards), list(shards)
        last = None
        for step in range(1, half + 1):
            for k in range(len(shards)):
                if step < half:
                    up[k], down[k] = self.ring(up[k], 1), self.ring(down[k], -1)
                else:
                    up[k], down[k] = self.ring(up[k][:1], 1), self.ring(down[k][1:], -1)
            for k in range(len(shards)):
                wholes[k] = put(wholes[k], up[k], -step)
                wholes[k] = put(wholes[k], down[k], step, 0 if step < half else 1)
            if step == half - 1:
                last = up + down
        wholes = [w.reshape(-1, w.shape[-1]) for w in wholes]
        return wholes, last

    def scatter_rings(self, grads):
        count = 2 * self.depth
        half = self.depth
        blocks = [g.reshape(count, 2, g.shape[0] // (2 * count), g.shape[1]) for g in grads]

        def own(k, step):
            start = (self.block_of(step), 0, 0, 0)
            return lax.dynamic_slice(blocks[k], start, (1,) + blocks[k].shape[1:])[0]

        ups = [own(k, half)[:1] for k in range(len(grads))]
        downs = [own(k, half)[1:] for k in range(len(grads))]
        totals = []
        for step in range(1, half + 1):
            for k in range(len(grads)):
                ups[k], downs[k] = self.ring(ups[k], 1), self.ring(downs[k], -1)
                if step == half:
                    total = own(k, 0).astype(F32) + ups[k].astype(F32) + downs[k].astype(F32)
                    totals.append(total.reshape(-1, total.shape[-1]))
                    continue
                ahead, behind = own(k, half - step), own(k, step - half)
                if step == 1:
                    first = (ahead[:1].astype(F32) + ups[k].astype(F32)).astype(BF16)
                    ups[k] = jnp.concatenate([first, ahead[1:]], axis=0)
                    second = (behind[1:].astype(F32) + downs[k].astype(F32)).astype(BF16)
                    downs[k] = jnp.concatenate([behind[:1], second], axis=0)
                else:
                    ups[k] = (ahead.astype(F32) + ups[k].astype(F32)).astype(BF16)
                    downs[k] = (behind.astype(F32) + downs[k].astype(F32)).astype(BF16)
        return totals

    def share_plane(self, value):
        count = 2 * self.depth
        n = self.dp
        parts = [value] + [
            lax.ppermute(value, "dp", [(i, (i + 2 * k) % n) for i in range(n)])
            for k in range(1, count)
        ]
        back = [parts[-m % count] for m in range(count)]
        spot = 2 * self.z + self.x
        return lax.dynamic_slice_in_dim(jnp.stack(back + back), (count - spot) % count, count, 0)

    def by_core(self, mine, other, axis):
        return jnp.where(
            self.core == 0,
            jnp.concatenate([mine, other], axis=axis),
            jnp.concatenate([other, mine], axis=axis),
        )

    def core_columns(self, weights):
        half = [w.shape[1] // 2 for w in weights]
        keep = [
            lax.dynamic_slice_in_dim(w, self.core * h, h, 1) for w, h in zip(weights, half)
        ]
        give = [
            lax.dynamic_slice_in_dim(w, (1 - self.core) * h, h, 1) for w, h in zip(weights, half)
        ]
        return keep, give

    def finish_grad(self, own):
        rows = own.shape[0] // 2
        keep = lax.dynamic_slice_in_dim(own, self.core * rows, rows, 0)
        give = lax.dynamic_slice_in_dim(own, (1 - self.core) * rows, rows, 0)
        return keep, self.swap_core(give.astype(BF16)).astype(F32)

    def gather_tokens(self, rows):
        near = self.swap_y(rows)
        return jnp.concatenate(
            [rows, near, self.swap_core(rows), self.swap_core(near)], axis=0
        )

    def scatter_tokens(self, partial_rows):
        rows = partial_rows.shape[0] // 4
        given = partial_rows[2 * rows :].astype(BF16)
        pack = partial_rows[: 2 * rows].astype(F32) + self.swap_core(given).astype(F32)
        return pack[:rows] + self.swap_y(pack[rows:].astype(BF16)).astype(F32)


def after(value, *others):
    return lax.optimization_barrier((value,) + others)[0]


def interleave(parts):
    rows = parts[0].shape[0]
    stacked = jnp.stack([p.reshape(rows, -1, LANES) for p in parts], axis=2)
    return stacked.reshape(rows, -1)


def split_low(value):
    high = value.astype(BF16)
    return high, (value - high.astype(F32)).astype(BF16)


def paired_body(
    layer_in,
    segment_ids,
    norm1_gain,
    w_query,
    w_key,
    w_value,
    w_forget,
    forget_bias,
    w_output,
    norm2_gain,
    w_gate,
    w_up,
    w_down,
    clip_tau,
    out_grad,
):
    at = Place()
    rows_loc = layer_in.shape[0]
    pack = 2 * rows_loc
    width = layer_in.shape[1]
    heads = forget_bias.shape[0] // 2
    pairs = heads // 2
    y_index = at.y.astype(jnp.int32).reshape(1)
    d_rows = norm1_gain.shape[0]

    keep, give = at.core_columns(
        [w_query, w_key, w_value, w_output, w_gate, w_up, w_down, w_forget]
    )
    gains = jnp.stack([norm1_gain, norm2_gain], axis=1)
    pad = jnp.zeros((d_rows, LANES - 2 * heads - 2), BF16)

    def shard_of(kept, given):
        return at.by_core(kept[None], at.swap_core(given)[None], 0)

    def first_part(part):
        return jnp.concatenate(
            [interleave(part[:3]), part[7], part[7], gains, pad, part[3]], axis=1
        )

    attn_shard = shard_of(first_part(keep), first_part(give))
    ffn_shard = shard_of(
        jnp.concatenate(keep[4:7], axis=1),
        jnp.concatenate(give[4:7], axis=1),
    )
    rows_all = at.gather_tokens(layer_in)
    units = keep[4].shape[1]
    qkv_cols = 3 * heads * HEAD_DIM
    in_cols = qkv_cols + LANES
    (w_in, wo_all), last = at.gather_rings([attn_shard[..., :in_cols], attn_shard[..., in_cols:]])
    gu_shard = after(ffn_shard[..., : 2 * units], *last)
    (gu_all,), last = at.gather_rings([gu_shard])
    (down_all,), _ = at.gather_rings([after(ffn_shard[..., 2 * units :], *last)])
    w_qkv = w_in[:, :qkv_cols]
    small = w_in[:, qkv_cols:].T
    forget_t = small[:heads]
    gain_one = small[2 * heads : 2 * heads + 1].astype(F32)
    gain_two = small[2 * heads + 1 : 2 * heads + 2].astype(F32)

    x_all = rows_all.astype(F32)
    scale_one = lax.rsqrt(jnp.mean(x_all * x_all, axis=1, keepdims=True) + EPSILON)
    unit_one = x_all * scale_one
    normed_one = (unit_one * gain_one).astype(BF16)
    x_own, scale_one, unit_one = x_all[:rows_loc], scale_one[:rows_loc], unit_one[:rows_loc]
    qkv = dot_nn(normed_one, w_qkv).astype(BF16)

    bias = lax.dynamic_slice_in_dim(forget_bias, at.core * heads, heads, 0)
    logits = dot_nt(forget_t, normed_one) + bias[:, None]
    logs = jax.nn.log_sigmoid(logits).reshape(heads, 2, 2, rows_loc)
    steps = jnp.arange(rows_loc, dtype=jnp.int32)
    upper = (steps[:, None] <= steps[None, :]).astype(F32)
    sums = jnp.einsum("hpbt,ts->hpbs", logs, upper, precision=HIGHEST)
    total = sums[..., -1:]
    later = at.y.astype(F32)
    cumul = jnp.stack(
        [sums[:, :, 0] + later * total[:, :, 1], sums[:, :, 1] + (1.0 - later) * total[:, :, 0]],
        axis=2,
    ).reshape(heads, 2 * pack)
    seg_own = segment_ids[0].reshape(2, rows_loc)
    seg_own = jnp.where(at.y == 0, seg_own, seg_own[::-1]).reshape(1, pack)
    seg_both = jnp.concatenate([seg_own, at.swap_core(seg_own)], axis=1).astype(F32)
    aux = jnp.concatenate(
        [
            cumul.reshape(pairs, 2, 2 * pack),
            jnp.broadcast_to(seg_both[None], (pairs, 6, 2 * pack)),
        ],
        axis=1,
    )
    mixed, inverse, expos, tops = attend(y_index, qkv, aux, 2, pairs)

    attn_part = dot_nt(mixed, wo_all)
    resid = x_own + at.scatter_tokens(attn_part)
    scale_two = lax.rsqrt(jnp.mean(resid * resid, axis=1, keepdims=True) + EPSILON)
    unit_two = resid * scale_two
    normed_two = at.gather_tokens((unit_two * gain_two).astype(BF16))
    grad_rows = at.gather_tokens(out_grad)

    gate_up = dot_nn(normed_two, gu_all)
    gate_pre, up_pre = gate_up[:, :units], gate_up[:, units:]
    gate_sig = jax.nn.sigmoid(gate_pre)
    gate_act = gate_pre * gate_sig
    hidden = (gate_act * up_pre).astype(BF16)
    g_down = dot_tn(grad_rows, hidden).astype(BF16)
    grad_hidden = dot_nn(grad_rows, down_all)
    grad_gate = (grad_hidden * up_pre * gate_sig * (1.0 + gate_pre * (1.0 - gate_sig))).astype(BF16)
    grad_up = (grad_hidden * gate_act).astype(BF16)
    g_gate = dot_tn(normed_two, grad_gate).astype(BF16)
    g_up = dot_tn(normed_two, grad_up).astype(BF16)
    g_down, g_gate, g_up = at.scatter_rings([g_down, g_gate, g_up])
    grad_gu = jnp.concatenate([grad_gate, grad_up], axis=1)
    grad_two = at.scatter_tokens(dot_nt(grad_gu, gu_all))
    layer_out = (resid + at.scatter_tokens(dot_nt(hidden, down_all))).astype(BF16)

    weighted = gain_two * grad_two
    inner_two = jnp.mean(unit_two * weighted, axis=1, keepdims=True)
    norm2_part = jnp.sum(grad_two * unit_two, axis=0)
    grad_resid = out_grad.astype(F32) + scale_two * (weighted - unit_two * inner_two)
    grad_attn = at.gather_tokens(grad_resid.astype(BF16))

    grad_mixed = dot_nn(grad_attn, wo_all).astype(BF16)
    g_output = dot_tn(grad_attn, mixed).astype(BF16)
    d_qkv, d_cum = attend_back(y_index, qkv, grad_mixed, inverse, expos, 2, pairs)
    d_cum = d_cum[:, :2].reshape(heads, 2, 2, rows_loc)
    back = jnp.einsum("hpbt,st->hpbs", d_cum, upper, precision=HIGHEST)
    total = back[..., :1]
    d_log = jnp.stack(
        [back[:, :, 0] + (1.0 - later) * total[:, :, 1], back[:, :, 1] + later * total[:, :, 0]],
        axis=2,
    ).reshape(heads, 2 * pack)
    d_logit = d_log * jax.nn.sigmoid(-logits)
    bias_part = jnp.sum(d_logit, axis=1)
    d_split = jnp.concatenate(split_low(d_logit), axis=0).T
    d_split = jnp.pad(d_split, ((0, 0), (0, LANES - 2 * heads)))
    d_in = jnp.concatenate([d_qkv, d_split], axis=1)
    g_in = dot_tn(normed_one, d_in).astype(BF16)
    middle = in_cols // 2
    g_output, g_low, g_high = at.scatter_rings([g_output, g_in[:, :middle], g_in[:, middle:]])
    g_in = jnp.concatenate([g_low, g_high], axis=1)
    grad_one = dot_nt(d_in, w_in)
    grad_one = at.scatter_tokens(grad_one)

    weighted = gain_one * grad_one
    inner_one = jnp.mean(unit_one * weighted, axis=1, keepdims=True)
    norm1_part = jnp.sum(grad_one * unit_one, axis=0)
    x_grad = (grad_resid + scale_one * (weighted - unit_one * inner_one)).astype(BF16)

    norms = jnp.stack([norm1_part, norm2_part])
    norms = norms + at.swap_core(norms)
    cut = width // 2
    norms = lax.dynamic_slice_in_dim(norms, at.y * cut, cut, 1) + at.swap_y(
        lax.dynamic_slice_in_dim(norms, (1 - at.y) * cut, cut, 1)
    )
    maxima = jnp.max(tops[:, :, :2], axis=(0, 3)).reshape(heads)
    lone = jnp.pad(jnp.stack([bias_part, maxima]), ((0, 4), (0, cut - heads)))
    shared = at.share_plane(jnp.concatenate([norms, lone], axis=0))
    sums = jnp.sum(shared[:, :3], axis=0)
    lone = jnp.concatenate([sums[2:3], jnp.max(shared[:, 3:4], axis=0)], axis=0)[:, :LANES]
    lone = at.by_core(lone[:, :heads], at.swap_core(lone)[:, :heads], 1)
    g_bias = lone[0]
    clip_factor = jnp.minimum(1.0, clip_tau / jnp.maximum(lone[1], 1.0))
    columns = jnp.repeat(jnp.sqrt(clip_factor), HEAD_DIM)
    clipped_query = (w_query.astype(F32) * columns[None, :]).astype(BF16)
    clipped_key = (w_key.astype(F32) * columns[None, :]).astype(BF16)

    def place(own):
        keep, got = at.finish_grad(own)
        return at.by_core(keep, got, 1)

    keep, got = at.finish_grad(g_in)

    def third(which):
        def pick(value):
            value = value[:, :qkv_cols].reshape(d_rows, pairs, 3, LANES)
            return value[:, :, which].reshape(d_rows, -1)

        return at.by_core(pick(keep), pick(got), 1)

    def forget(value):
        return value[:, qkv_cols : qkv_cols + heads] + value[:, qkv_cols + heads :][:, :heads]

    return (
        layer_out,
        x_grad,
        sums[0],
        third(0),
        third(1),
        third(2),
        at.by_core(forget(keep), forget(got), 1),
        g_bias,
        place(g_output),
        sums[1],
        place(g_gate),
        place(g_up),
        place(g_down),
        clip_factor,
        clipped_query,
        clipped_key,
    )


def pick_body(mesh):
    dp, tensor = mesh.shape["dp"], mesh.shape["tensor"]

    def body(*args):
        rows, heads = args[0].shape[0], args[7].shape[0]
        depth = dp // 4
        paired = (
            tensor == 2
            and dp % 4 == 0
            and depth & (depth - 1) == 0
            and rows == BLOCK
            and heads % 4 == 0
        )
        return (paired_body if paired else general_body)(*args)

    return body
def solution(mesh):
    return jax.shard_map(
        pick_body(mesh),
        mesh=mesh,
        in_specs=(
            P(("dp", "tensor"), None),
            P("dp", None),
            P("dp"),
            P("dp", "tensor"),
            P("dp", "tensor"),
            P("dp", "tensor"),
            P("dp", "tensor"),
            P("tensor"),
            P("dp", "tensor"),
            P("dp"),
            P("dp", "tensor"),
            P("dp", "tensor"),
            P("dp", "tensor"),
            P("tensor"),
            P(("dp", "tensor"), None),
        ),
        out_specs=(
            P(("dp", "tensor"), None),
            P(("dp", "tensor"), None),
            P("tensor"),
            P("dp", "tensor"),
            P("dp", "tensor"),
            P("dp", "tensor"),
            P("dp", "tensor"),
            P("tensor"),
            P("dp", "tensor"),
            P("tensor"),
            P("dp", "tensor"),
            P("dp", "tensor"),
            P("dp", "tensor"),
            P("tensor"),
            P("dp", "tensor"),
            P("dp", "tensor"),
        ),
        check_vma=False,
    )
```

```python
import math
from functools import partial

import jax
import jax.numpy as jnp
from jax import lax
from jax.experimental import pallas as pl
from jax.experimental.pallas import tpu as pltpu
from jax.sharding import PartitionSpec as P

HEAD_DIM = 64
BLOCK = 256
LANES = 128
EPSILON = 1e-06
HIGHEST = lax.Precision.HIGHEST
NEGATIVE = -1e30
F32 = jnp.float32
BF16 = jnp.bfloat16
def combined_all(part, axis, combine):
    gathered = jax.tree.map(lambda a: lax.all_gather(a, axis), part)

    def take(source):
        return jax.tree.map(lambda a: lax.dynamic_index_in_dim(a, source, 0, False), gathered)

    return lax.fori_loop(
        1, lax.axis_size(axis), lambda source, state: combine(state, take(source)), take(0)
    )


def contract_last(left_op, right_op):
    return lax.dot_general(
        left_op, right_op, (((1,), (1,)), ((), ())), preferred_element_type=jnp.float32
    )


def contract_first(left_op, right_op):
    return lax.dot_general(
        left_op, right_op, (((0,), (0,)), ((), ())), preferred_element_type=jnp.float32
    )


def block_terms(q_blk, keys_all, cumul, seg_row, offset, rows_blk):
    positions = jnp.arange(keys_all.shape[0], dtype=jnp.int32)
    q_pos = offset + jnp.arange(rows_blk, dtype=jnp.int32)
    allowed = (seg_row[:, None] == seg_row[None, :]) & (
        q_pos[:, None] // BLOCK >= positions[None, :] // BLOCK
    )
    signs = jnp.where(positions[None, :] <= q_pos[:, None], 1.0, -1.0).astype(jnp.float32)
    raw_blk = jnp.einsum("qhe,khe->hqk", q_blk, keys_all, preferred_element_type=jnp.float32) * (
        1.0 / math.sqrt(HEAD_DIM)
    )
    differ = cumul.T[:, :, None] - cumul.T[:, None, :]
    scores = jnp.where(allowed[None], raw_blk + signs[None] * differ, NEGATIVE)
    return (raw_blk, scores, allowed, signs)


def combine(former, latter):
    return (
        jnp.maximum(former[0], latter[0]),
        former[1] + latter[1],
        former[2] + latter[2],
        former[3] + latter[3],
    )


def general_body(
    layer_in,
    segment_ids,
    norm1_gain,
    w_query,
    w_key,
    w_value,
    w_forget,
    forget_bias,
    w_output,
    norm2_gain,
    w_gate,
    w_up,
    w_down,
    clip_tau,
    out_grad,
):
    gain_one, wq_all, wk_all, wv_all, wf_all, wo_all, gain_two, wg_all, wu_all, wd_all = (
        lax.all_gather(norm1_gain, "dp", axis=0, tiled=True),
        lax.all_gather(w_query, "dp", axis=0, tiled=True),
        lax.all_gather(w_key, "dp", axis=0, tiled=True),
        lax.all_gather(w_value, "dp", axis=0, tiled=True),
        lax.all_gather(w_forget, "dp", axis=0, tiled=True),
        lax.all_gather(w_output, "dp", axis=0, tiled=True),
        lax.all_gather(norm2_gain, "dp", axis=0, tiled=True),
        lax.all_gather(w_gate, "dp", axis=0, tiled=True),
        lax.all_gather(w_up, "dp", axis=0, tiled=True),
        lax.all_gather(w_down, "dp", axis=0, tiled=True),
    )
    gain_one = gain_one.astype(jnp.float32)
    gain_two = gain_two.astype(jnp.float32)
    tok_local = layer_in.shape[0]
    tokens = tok_local * lax.axis_size("tensor")
    heads_loc = forget_bias.shape[0]
    row_start = lax.axis_index("tensor") * tok_local
    seg_row = segment_ids[0]
    factor = 1.0 / math.sqrt(HEAD_DIM)
    rows_full = lax.all_gather(layer_in, "tensor", axis=0, tiled=True).astype(jnp.float32)
    scale_one = lax.rsqrt(jnp.mean(rows_full * rows_full, axis=1, keepdims=True) + EPSILON)
    unit_one = rows_full * scale_one
    normed_one = (unit_one * gain_one).astype(jnp.bfloat16)
    queries = (
        jnp.dot(normed_one, wq_all, preferred_element_type=jnp.float32)
        .astype(jnp.bfloat16)
        .reshape(tokens, heads_loc, HEAD_DIM)
    )
    keys_all = (
        jnp.dot(normed_one, wk_all, preferred_element_type=jnp.float32)
        .astype(jnp.bfloat16)
        .reshape(tokens, heads_loc, HEAD_DIM)
    )
    values_all = (
        jnp.dot(normed_one, wv_all, preferred_element_type=jnp.float32)
        .astype(jnp.bfloat16)
        .reshape(tokens, heads_loc, HEAD_DIM)
    )
    logits = jnp.dot(normed_one, wf_all, preferred_element_type=jnp.float32) + forget_bias
    cumul = jnp.cumsum(jax.nn.log_sigmoid(logits), axis=0)
    rows_blk = min(512, tokens)
    blocks = tokens // rows_blk
    numbers = jnp.arange(blocks, dtype=jnp.int32)

    def forward_block(number):
        offset = number * rows_blk
        raw_blk, scores, allowed, signs = block_terms(
            queries, keys_all, cumul, seg_row, offset, rows_blk
        )
        top_blk = jnp.max(jnp.where(allowed[None], raw_blk, NEGATIVE), axis=(1, 2))
        row_peak = jnp.max(scores, axis=2, keepdims=True)
        expo_blk = jnp.exp(scores - row_peak)
        totals = jnp.sum(expo_blk, axis=2, keepdims=True)
        weights = (expo_blk / totals).astype(jnp.bfloat16)
        mixed_out = jnp.einsum(
            "hqk,khe->qhe", weights, values_all, preferred_element_type=jnp.float32
        ).astype(jnp.bfloat16)
        return (mixed_out, (row_peak + jnp.log(totals))[:, :, 0], top_blk)

    mixed_out, log_sums, top_blk = lax.map(forward_block, numbers)
    mixed_flat = mixed_out.reshape(tokens, heads_loc * HEAD_DIM)
    maxima = jnp.max(top_blk, axis=0)
    attn_part = contract_last(mixed_flat, wo_all)
    resid_full = rows_full + lax.psum(attn_part.astype(jnp.bfloat16), "tensor").astype(jnp.float32)
    scale_full = lax.rsqrt(jnp.mean(resid_full * resid_full, axis=1, keepdims=True) + EPSILON)
    normed_two = (resid_full * scale_full * gain_two).astype(jnp.bfloat16)
    resid_part = lax.dynamic_slice_in_dim(resid_full, row_start, tok_local, 0)
    scale_two = lax.dynamic_slice_in_dim(scale_full, row_start, tok_local, 0)
    gate_pre = jnp.dot(normed_two, wg_all, preferred_element_type=jnp.float32)
    up_pre = jnp.dot(normed_two, wu_all, preferred_element_type=jnp.float32)
    gate_sig = jax.nn.sigmoid(gate_pre)
    gate_act = gate_pre * gate_sig
    hidden = (gate_act * up_pre).astype(jnp.bfloat16)
    ffn_part = lax.psum_scatter(
        contract_last(hidden, wd_all).astype(jnp.bfloat16),
        "tensor",
        scatter_dimension=0,
        tiled=True,
    ).astype(jnp.float32)
    layer_out = (resid_part + ffn_part).astype(jnp.bfloat16)
    grad_full = lax.all_gather(out_grad, "tensor", axis=0, tiled=True)
    grad_hidden = jnp.dot(grad_full, wd_all, preferred_element_type=jnp.float32)
    grad_gate = (grad_hidden * up_pre * gate_sig * (1.0 + gate_pre * (1.0 - gate_sig))).astype(
        jnp.bfloat16
    )
    grad_up = (grad_hidden * gate_act).astype(jnp.bfloat16)
    g_down = contract_first(grad_full, hidden)
    g_gate = contract_first(normed_two, grad_gate)
    g_up = contract_first(normed_two, grad_up)
    grad_normed = contract_last(grad_gate, wg_all) + contract_last(grad_up, wu_all)
    grad_two = lax.psum_scatter(
        grad_normed.astype(jnp.bfloat16), "tensor", scatter_dimension=0, tiled=True
    ).astype(jnp.float32)
    unit_two = resid_part * scale_two
    inner_two = jnp.mean(unit_two * gain_two * grad_two, axis=1, keepdims=True)
    norm2_part = jnp.sum(grad_two * unit_two, axis=0)
    grad_resid = out_grad.astype(jnp.float32) + scale_two * (
        gain_two * grad_two - unit_two * inner_two
    )
    grad_attn = lax.all_gather(grad_resid.astype(jnp.bfloat16), "tensor", axis=0, tiled=True)
    g_output = contract_first(grad_attn, mixed_flat)
    grad_mixed = jnp.dot(grad_attn, wo_all, preferred_element_type=jnp.float32).astype(jnp.bfloat16)
    grad_mixed = grad_mixed.reshape(blocks, rows_blk, heads_loc, HEAD_DIM)

    def backward_block(carried, block_in):
        key_acc, value_acc, column_acc = carried
        number, log_blk, grad_blk = block_in
        offset = number * rows_blk
        raw_blk, scores, allowed, signs = block_terms(
            queries, keys_all, cumul, seg_row, offset, rows_blk
        )
        prob_blk = jnp.exp(scores - log_blk[:, :, None])
        weights = prob_blk.astype(jnp.bfloat16)
        grad_prob = jnp.einsum(
            "qhe,khe->hqk", grad_blk, values_all, preferred_element_type=jnp.float32
        )
        inner = jnp.sum(prob_blk * grad_prob, axis=2, keepdims=True)
        grad_scores = (prob_blk * (grad_prob - inner)).astype(jnp.bfloat16)
        value_acc = value_acc + jnp.einsum(
            "hqk,qhe->khe", weights, grad_blk, preferred_element_type=jnp.float32
        )
        key_acc = key_acc + jnp.einsum(
            "hqk,qhe->khe", grad_scores, queries, preferred_element_type=jnp.float32
        )
        grad_query = (
            jnp.einsum("hqk,khe->qhe", grad_scores, keys_all, preferred_element_type=jnp.float32)
            * factor
        ).astype(jnp.bfloat16)
        signed = grad_scores.astype(jnp.float32) * signs[None]
        column_acc = column_acc - jnp.sum(signed, axis=1).T
        return ((key_acc, value_acc, column_acc), (grad_query, jnp.sum(signed, axis=2).T))

    start_acc = (
        jnp.zeros((tokens, heads_loc, HEAD_DIM), jnp.float32),
        jnp.zeros((tokens, heads_loc, HEAD_DIM), jnp.float32),
        jnp.zeros((tokens, heads_loc), jnp.float32),
    )
    (key_acc, value_acc, column_acc), (grad_query, row_parts) = lax.scan(
        backward_block, start_acc, (numbers, log_sums, grad_mixed)
    )
    grad_q = grad_query.reshape(tokens, heads_loc * HEAD_DIM)
    grad_k = (key_acc * factor).astype(jnp.bfloat16).reshape(tokens, heads_loc * HEAD_DIM)
    grad_v = value_acc.astype(jnp.bfloat16).reshape(tokens, heads_loc * HEAD_DIM)
    grad_cum = row_parts.reshape(tokens, heads_loc) + column_acc
    grad_logs = jnp.cumsum(grad_cum[::-1], axis=0)[::-1]
    grad_logit = grad_logs * jax.nn.sigmoid(-logits)
    g_bias = jnp.sum(grad_logit, axis=0)
    g_forget = jnp.einsum(
        "td,th->dh", normed_one, grad_logit, precision=HIGHEST, preferred_element_type=jnp.float32
    )
    g_query = contract_first(normed_one, grad_q)
    g_key = contract_first(normed_one, grad_k)
    g_value = contract_first(normed_one, grad_v)
    grad_one = (
        contract_last(grad_q, wq_all)
        + contract_last(grad_k, wk_all)
        + contract_last(grad_v, wv_all)
    )
    grad_one = grad_one + jnp.einsum(
        "th,dh->td", grad_logit, wf_all, precision=HIGHEST, preferred_element_type=jnp.float32
    )
    weighted = gain_one * grad_one
    grad_rows_one = scale_one * (
        weighted - unit_one * jnp.mean(unit_one * weighted, axis=1, keepdims=True)
    )
    norm1_part = jnp.sum(grad_one * unit_one, axis=0)
    grad_input, g_norm1_part, g_norm2_part = (
        lax.psum_scatter(
            grad_rows_one.astype(jnp.bfloat16), "tensor", scatter_dimension=0, tiled=True
        ).astype(jnp.float32),
        lax.psum_scatter(
            norm1_part.astype(jnp.bfloat16), "tensor", scatter_dimension=0, tiled=True
        ).astype(jnp.float32),
        lax.psum_scatter(
            norm2_part.astype(jnp.bfloat16), "tensor", scatter_dimension=0, tiled=True
        ).astype(jnp.float32),
    )
    x_grad = (grad_resid + grad_input).astype(jnp.bfloat16)
    g_query, g_key, g_value, g_forget, g_output, g_gate, g_up, g_down = (
        lax.psum_scatter(
            g_query.astype(jnp.bfloat16), "dp", scatter_dimension=0, tiled=True
        ).astype(jnp.float32),
        lax.psum_scatter(g_key.astype(jnp.bfloat16), "dp", scatter_dimension=0, tiled=True).astype(
            jnp.float32
        ),
        lax.psum_scatter(
            g_value.astype(jnp.bfloat16), "dp", scatter_dimension=0, tiled=True
        ).astype(jnp.float32),
        lax.psum_scatter(
            g_forget.astype(jnp.bfloat16), "dp", scatter_dimension=0, tiled=True
        ).astype(jnp.float32),
        lax.psum_scatter(
            g_output.astype(jnp.bfloat16), "dp", scatter_dimension=0, tiled=True
        ).astype(jnp.float32),
        lax.psum_scatter(g_gate.astype(jnp.bfloat16), "dp", scatter_dimension=0, tiled=True).astype(
            jnp.float32
        ),
        lax.psum_scatter(g_up.astype(jnp.bfloat16), "dp", scatter_dimension=0, tiled=True).astype(
            jnp.float32
        ),
        lax.psum_scatter(g_down.astype(jnp.bfloat16), "dp", scatter_dimension=0, tiled=True).astype(
            jnp.float32
        ),
    )
    maxima, g_bias, g_norm1, g_norm2 = combined_all(
        (maxima, g_bias, g_norm1_part, g_norm2_part), "dp", combine
    )
    clip_factor = jnp.minimum(1.0, clip_tau / jnp.maximum(maxima, 1.0))
    columns = jnp.repeat(jnp.sqrt(clip_factor), HEAD_DIM)
    clipped_query = (w_query.astype(jnp.float32) * columns[None, :]).astype(jnp.bfloat16)
    clipped_key = (w_key.astype(jnp.float32) * columns[None, :]).astype(jnp.bfloat16)
    return (
        layer_out,
        x_grad,
        g_norm1,
        g_query,
        g_key,
        g_value,
        g_forget,
        g_bias,
        g_output,
        g_norm2,
        g_gate,
        g_up,
        g_down,
        clip_factor,
        clipped_query,
        clipped_key,
    )


def dot_nt(left, right):
    return lax.dot_general(left, right, (((1,), (1,)), ((), ())), preferred_element_type=F32)


def dot_nn(left, right):
    return lax.dot_general(left, right, (((1,), (0,)), ((), ())), preferred_element_type=F32)


def dot_tn(left, right):
    return lax.dot_general(left, right, (((0,), (0,)), ((), ())), preferred_element_type=F32)


def attend_kernel(y_ref, qkv_ref, aux_ref, o_ref, inv_ref, exp_ref, top_ref):
    y = y_ref[0]
    starts = (pl.multiple_of(y * BLOCK, BLOCK), pl.multiple_of((1 - y) * BLOCK, BLOCK))
    lane = lax.broadcasted_iota(jnp.int32, (1, LANES), 1)
    first = lane < HEAD_DIM
    aux = [aux_ref[0, :, pl.ds(start, BLOCK)] for start in starts]
    aux_col = [a.T for a in aux]
    q_blk = [qkv_ref[pl.ds(s, BLOCK), 0:LANES] * 0.125 for s in starts]
    k_blk = [qkv_ref[pl.ds(s, BLOCK), LANES : 2 * LANES] for s in starts]
    v_blk = [qkv_ref[pl.ds(s, BLOCK), 2 * LANES : 3 * LANES] for s in starts]
    same = {}
    for i, j in ((0, 0), (1, 0), (1, 1)):
        same[i, j] = aux_col[i][:, 2:3] == aux[j][2:3, :]
    tops = []
    results = [[], []]
    for head in range(2):
        mine = first if head == 0 else jnp.logical_not(first)
        top = None
        v_ext = [jnp.where(mine, v, jnp.ones_like(v)) for v in v_blk]
        k_head = [jnp.where(mine, k, jnp.zeros_like(k)) for k in k_blk]
        for i in range(2):
            scores = []
            for j in range(i + 1):
                raw = dot_nt(q_blk[i], k_head[j])
                seen = jnp.where(same[i, j], raw, NEGATIVE)
                high = jnp.max(seen, axis=0, keepdims=True)
                top = high if top is None else jnp.maximum(top, high)
                differ = aux_col[i][:, head : head + 1] - aux[j][head : head + 1, :]
                scores.append(seen - jnp.abs(differ))
            peak = jnp.max(scores[0], axis=1, keepdims=True)
            if i == 1:
                peak = jnp.maximum(peak, jnp.max(scores[1], axis=1, keepdims=True))
            acc = None
            for j in range(i + 1):
                weights = jnp.exp(scores[j] - peak).astype(BF16)
                exp_ref[0, 0, head, :, (i + j) * BLOCK : (i + j + 1) * BLOCK] = weights
                part = dot_nn(weights, v_ext[j])
                acc = part if acc is None else acc + part
            results[i].append(acc)
        tops.append(jnp.maximum(top[:, :LANES], top[:, LANES:]))
    for i in range(2):
        one, two = results[i]
        total = pltpu.roll(jnp.where(first, two, one), HEAD_DIM, 1)
        inverse = 1.0 / total
        inv_ref[pl.ds(starts[i], BLOCK), :] = inverse
        o_ref[pl.ds(starts[i], BLOCK), :] = (jnp.where(first, one, two) * inverse).astype(BF16)
    row = lax.broadcasted_iota(jnp.int32, (8, LANES), 0)
    top_ref[0, 0] = jnp.where(row == 0, tops[0], tops[1])


def attend(y_index, qkv, aux, packs, pairs):
    rows = qkv.shape[0] // packs
    wide = 3 * LANES
    grid_spec = pltpu.PrefetchScalarGridSpec(
        num_scalar_prefetch=1,
        grid=(packs, pairs),
        in_specs=[
            pl.BlockSpec((rows, wide), lambda p, h, y: (p, h)),
            pl.BlockSpec((1, 8, rows), lambda p, h, y: (h, 0, p)),
        ],
        out_specs=[
            pl.BlockSpec((rows, LANES), lambda p, h, y: (p, h)),
            pl.BlockSpec((rows, LANES), lambda p, h, y: (p, h)),
            pl.BlockSpec((1, 1, 2, BLOCK, 3 * BLOCK), lambda p, h, y: (p, h, 0, 0, 0)),
            pl.BlockSpec((1, 1, 8, LANES), lambda p, h, y: (p, h, 0, 0)),
        ],
    )
    return pl.pallas_call(
        attend_kernel,
        grid_spec=grid_spec,
        out_shape=(
            jax.ShapeDtypeStruct((packs * rows, pairs * LANES), BF16),
            jax.ShapeDtypeStruct((packs * rows, pairs * LANES), F32),
            jax.ShapeDtypeStruct((packs, pairs, 2, BLOCK, 3 * BLOCK), BF16),
            jax.ShapeDtypeStruct((packs, pairs, 8, LANES), F32),
        ),
        cost_estimate=pl.CostEstimate(
            flops=packs * pairs * 2 * 6 * BLOCK * BLOCK * LANES * 2,
            bytes_accessed=20_000_000,
            transcendentals=packs * pairs * 2 * 3 * BLOCK * BLOCK,
        ),
        name="attend",
    )(y_index, qkv, aux)


def attend_back_kernel(y_ref, qkv_ref, do_ref, inv_ref, exp_ref, dqkv_ref, dc_ref):
    y = y_ref[0]
    starts = (pl.multiple_of(y * BLOCK, BLOCK), pl.multiple_of((1 - y) * BLOCK, BLOCK))
    lane = lax.broadcasted_iota(jnp.int32, (1, LANES), 1)
    first = lane < HEAD_DIM
    ones = jnp.ones((8, BLOCK), BF16)
    lower = lax.broadcasted_iota(jnp.int32, (BLOCK, BLOCK), 1) <= lax.broadcasted_iota(
        jnp.int32, (BLOCK, BLOCK), 0
    )
    q_blk = [qkv_ref[pl.ds(s, BLOCK), 0:LANES] * 0.125 for s in starts]
    k_blk = [qkv_ref[pl.ds(s, BLOCK), LANES : 2 * LANES] for s in starts]
    v_blk = [qkv_ref[pl.ds(s, BLOCK), 2 * LANES : 3 * LANES] for s in starts]
    inv_blk = [inv_ref[pl.ds(s, BLOCK), :] for s in starts]
    do_blk = [
        (do_ref[pl.ds(s, BLOCK), :].astype(F32) * inv).astype(BF16)
        for s, inv in zip(starts, inv_blk)
    ]
    dq, dk, dv, dc = ([], []), ([], []), ([], []), ([], [])
    for head in range(2):
        mine = first if head == 0 else jnp.logical_not(first)
        v_head = [jnp.where(mine, v, jnp.zeros_like(v)) for v in v_blk]
        dk_acc, dv_acc, row_acc, col_acc = [None] * 2, [None] * 2, [None] * 2, [None] * 2
        for i in range(2):
            expos, probs, inner = [], [], None
            inv_col = inv_blk[i][:, head * HEAD_DIM : head * HEAD_DIM + 1]
            for j in range(i + 1):
                expo = exp_ref[0, 0, head, :, (i + j) * BLOCK : (i + j + 1) * BLOCK]
                grad_prob = dot_nt(do_blk[i], v_head[j])
                wide = expo.astype(F32)
                part = jnp.sum(wide * grad_prob, axis=1, keepdims=True)
                inner = part if inner is None else inner + part
                expos.append((expo, wide))
                probs.append(grad_prob)
            inner = inner * inv_col
            dq_acc = None
            for j in range(i + 1):
                expo, wide = expos[j]
                grad_score = wide * (probs[j] - inner)
                low = grad_score.astype(BF16)
                if i == j:
                    signed = jnp.where(lower, low, -low)
                else:
                    signed = low
                part = dot_nn(low, k_blk[j])
                dq_acc = part if dq_acc is None else dq_acc + part
                part = dot_tn(low, q_blk[i])
                dk_acc[j] = part if dk_acc[j] is None else dk_acc[j] + part
                part = dot_tn(expo, do_blk[i])
                dv_acc[j] = part if dv_acc[j] is None else dv_acc[j] + part
                part = dot_nt(ones, signed)
                row_acc[i] = part if row_acc[i] is None else row_acc[i] + part
                part = dot_nn(ones, signed)
                col_acc[j] = part if col_acc[j] is None else col_acc[j] + part
            dq[i].append(dq_acc)
        for j in range(2):
            dk[j].append(dk_acc[j])
            dv[j].append(dv_acc[j])
            dc[j].append(row_acc[j] - col_acc[j])
    row = lax.broadcasted_iota(jnp.int32, (8, BLOCK), 0)
    for i in range(2):
        rows = pl.ds(starts[i], BLOCK)
        dqkv_ref[rows, 0:LANES] = (jnp.where(first, *dq[i]) * 0.125).astype(BF16)
        dqkv_ref[rows, LANES : 2 * LANES] = jnp.where(first, *dk[i]).astype(BF16)
        dqkv_ref[rows, 2 * LANES : 3 * LANES] = jnp.where(first, *dv[i]).astype(BF16)
        dc_ref[0, :, rows] = jnp.where(row == 0, *dc[i])


def attend_back(y_index, qkv, d_out, inverse, expos, packs, pairs):
    rows = qkv.shape[0] // packs
    wide = 3 * LANES
    grid_spec = pltpu.PrefetchScalarGridSpec(
        num_scalar_prefetch=1,
        grid=(packs, pairs),
        in_specs=[
            pl.BlockSpec((rows, wide), lambda p, h, y: (p, h)),
            pl.BlockSpec((rows, LANES), lambda p, h, y: (p, h)),
            pl.BlockSpec((rows, LANES), lambda p, h, y: (p, h)),
            pl.BlockSpec((1, 1, 2, BLOCK, 3 * BLOCK), lambda p, h, y: (p, h, 0, 0, 0)),
        ],
        out_specs=[
            pl.BlockSpec((rows, wide), lambda p, h, y: (p, h)),
            pl.BlockSpec((1, 8, rows), lambda p, h, y: (h, 0, p)),
        ],
    )
    return pl.pallas_call(
        attend_back_kernel,
        grid_spec=grid_spec,
        out_shape=(
            jax.ShapeDtypeStruct((packs * rows, pairs * wide), BF16),
            jax.ShapeDtypeStruct((pairs, 8, packs * rows), F32),
        ),
        cost_estimate=pl.CostEstimate(
            flops=packs * pairs * 2 * 18 * BLOCK * BLOCK * LANES * 2,
            bytes_accessed=20_000_000,
            transcendentals=0,
        ),
        name="attend_back",
    )(y_index, qkv, d_out, inverse, expos)


class Gathering:
    def __init__(self, at, shard):
        self.at, self.step, self.half = at, 1, at.depth
        self.whole = jnp.zeros((2 * at.depth,) + shard.shape, shard.dtype)
        self.put(shard, 0, 0)
        self.send(shard, shard)

    def put(self, part, step, side):
        start = (self.at.block_of(step), side, 0, 0)
        self.whole = lax.dynamic_update_slice(self.whole, part[None], start)

    def send(self, up, down):
        if self.step == self.half:
            up, down = up[:1], down[1:]
        self.came = (self.at.ring(up, 1), self.at.ring(down, -1))

    def take(self, *others):
        up, down = after_all(self.came, *others)
        self.put(up, -self.step, 0)
        self.put(down, self.step, 1 if self.step == self.half else 0)
        return up, down

    def advance(self, *others):
        up, down = self.take(*others)
        self.step += 1
        self.send(up, down)
        return up, down

    def finish(self, *others):
        self.take(*others)
        return self.whole.reshape(-1, self.whole.shape[-1])


class Reduction:
    def __init__(self, at, grad, *others):
        self.at, self.step, self.half = at, 1, at.depth
        count = 2 * at.depth
        self.blocks = grad.reshape(count, 2, grad.shape[0] // (2 * count), grad.shape[1])
        far = self.own(self.half)
        self.sent = after_all((far[:1], far[1:]), *others) if others else (far[:1], far[1:])
        self.send()

    def own(self, step):
        start = (self.at.block_of(step), 0, 0, 0)
        return lax.dynamic_slice(self.blocks, start, (1,) + self.blocks.shape[1:])[0]

    def send(self):
        self.came = (self.at.ring(self.sent[0], 1), self.at.ring(self.sent[1], -1))

    def advance(self, *others):
        up, down = after_all(self.came, *others)
        ahead, behind = self.own(self.half - self.step), self.own(self.step - self.half)
        if self.step == 1:
            first = (ahead[:1].astype(F32) + up.astype(F32)).astype(BF16)
            second = (behind[1:].astype(F32) + down.astype(F32)).astype(BF16)
            up = jnp.concatenate([first, ahead[1:]], axis=0)
            down = jnp.concatenate([behind[:1], second], axis=0)
        else:
            up = (ahead.astype(F32) + up.astype(F32)).astype(BF16)
            down = (behind.astype(F32) + down.astype(F32)).astype(BF16)
        self.sent = (up, down)
        self.step += 1
        self.send()
        return up, down

    def finish(self, *others):
        up, down = after_all(self.came, *others)
        total = self.own(0).astype(F32) + up.astype(F32) + down.astype(F32)
        return total.reshape(-1, total.shape[-1])


class Place:
    def __init__(self):
        self.dp = lax.axis_size("dp")
        self.depth = self.dp // 4
        index = lax.axis_index("dp")
        self.core = index % 2
        self.x = (index // 2) % 2
        self.z = index // 4
        self.y = lax.axis_index("tensor")

    def swap_core(self, value):
        return lax.ppermute(value, "dp", [(i, i ^ 1) for i in range(self.dp)])

    def swap_y(self, value):
        return lax.ppermute(value, "tensor", [(0, 1), (1, 0)])

    def ring(self, value, step):
        spots = [4 * z for z in range(self.depth)]
        spots += [4 * z + 2 for z in reversed(range(self.depth))]
        count = len(spots)
        pairs = [
            (spots[r] + core, spots[(r + step) % count] + core)
            for r in range(count)
            for core in (0, 1)
        ]
        return lax.ppermute(value, "dp", pairs)

    def block_of(self, step):
        count = 2 * self.depth
        spot = (jnp.where(self.x == 0, self.z, count - 1 - self.z) + step + count) % count
        return jnp.where(spot < self.depth, 2 * spot, 2 * (count - 1 - spot) + 1)

    def sum_plane(self, value, combine):
        step = 2
        while step < self.dp:
            value = combine(
                value, lax.ppermute(value, "dp", [(i, i ^ step) for i in range(self.dp)])
            )
            step *= 2
        return value

    def by_core(self, mine, other, axis):
        return jnp.where(
            self.core == 0,
            jnp.concatenate([mine, other], axis=axis),
            jnp.concatenate([other, mine], axis=axis),
        )

    def core_columns(self, weights):
        half = [w.shape[1] // 2 for w in weights]
        keep = [
            lax.dynamic_slice_in_dim(w, self.core * h, h, 1) for w, h in zip(weights, half)
        ]
        give = [
            lax.dynamic_slice_in_dim(w, (1 - self.core) * h, h, 1) for w, h in zip(weights, half)
        ]
        return keep, give

    def finish_grad(self, own):
        rows = own.shape[0] // 2
        keep = lax.dynamic_slice_in_dim(own, self.core * rows, rows, 0)
        give = lax.dynamic_slice_in_dim(own, (1 - self.core) * rows, rows, 0)
        return keep, self.swap_core(give.astype(BF16)).astype(F32)

    def join(self, rows, near):
        both = jnp.concatenate([rows, near], axis=0)
        return jnp.concatenate([both, self.swap_core(both)], axis=0)

    def meet_core(self, left, right, dot):
        half = left.shape[0] // 2
        given = dot(left[half:], right).astype(BF16)
        got = self.swap_core(given)
        part = dot(after(left, given)[:half], right)
        return part, got


def after(value, *others):
    return lax.optimization_barrier((value,) + others)[0]


def after_all(values, *others):
    return lax.optimization_barrier(tuple(values) + others)[: len(values)]


def interleave(parts):
    starts = range(0, parts[0].shape[1], LANES)
    return jnp.concatenate([p[:, s : s + LANES] for s in starts for p in parts], axis=1)


def split_low(value):
    high = value.astype(BF16)
    return high, (value - high.astype(F32)).astype(BF16)


def paired_body(
    layer_in,
    segment_ids,
    norm1_gain,
    w_query,
    w_key,
    w_value,
    w_forget,
    forget_bias,
    w_output,
    norm2_gain,
    w_gate,
    w_up,
    w_down,
    clip_tau,
    out_grad,
):
    at = Place()
    rows_loc = layer_in.shape[0]
    pack = 2 * rows_loc
    width = layer_in.shape[1]
    heads = forget_bias.shape[0] // 2
    pairs = heads // 2
    y_index = at.y.astype(jnp.int32).reshape(1)
    d_rows = norm1_gain.shape[0]

    units = w_gate.shape[1] // 2
    keep, give = at.core_columns([w_query, w_key, w_value, w_output, w_forget])
    gains = jnp.stack([norm1_gain, norm2_gain], axis=1)
    pad = jnp.zeros((d_rows, LANES - 2 * heads - 2), BF16)

    def first_part(part):
        return jnp.concatenate(
            [interleave(part[:3]), part[4], part[4], gains, pad, part[3]], axis=1
        )

    attn_shard = at.by_core(first_part(keep)[None], at.swap_core(first_part(give))[None], 0)
    rows_near = at.swap_y(layer_in)
    grad_near = at.swap_y(after(out_grad, rows_near))
    qkv_cols = 3 * heads * HEAD_DIM
    in_cols = qkv_cols + LANES
    attn_ring = Gathering(at, attn_shard)
    moved = attn_ring.advance()
    keep, give = at.core_columns(after_all((w_gate, w_up, w_down), *moved))
    ffn_shard = at.by_core(
        jnp.concatenate(keep, axis=1)[None],
        at.swap_core(jnp.concatenate(give, axis=1))[None],
        0,
    )
    attn_ring.advance(rows_near)
    attn_ring.advance(grad_near)
    ffn_ring = Gathering(at, after(ffn_shard, *attn_ring.came))
    attn_all = attn_ring.finish()
    w_in, wo_all = attn_all[:, :in_cols], attn_all[:, in_cols:]
    rows_all = at.join(layer_in, rows_near)
    grad_rows = at.join(out_grad, grad_near)
    w_qkv = w_in[:, :qkv_cols]
    small = w_in[:, qkv_cols:].T
    forget_t = small[:heads]
    gain_one = small[2 * heads : 2 * heads + 1].astype(F32)
    gain_two = small[2 * heads + 1 : 2 * heads + 2].astype(F32)

    def first_norm(rows):
        rows = rows.astype(F32)
        return rows, lax.rsqrt(jnp.mean(rows * rows, axis=1, keepdims=True) + EPSILON)

    x_all, scale_all = first_norm(rows_all)
    normed_one = (x_all * scale_all * gain_one).astype(BF16)
    x_own, scale_one = first_norm(layer_in)
    unit_one = x_own * scale_one
    qkv = dot_nn(normed_one, w_qkv).astype(BF16)

    bias = lax.dynamic_slice_in_dim(forget_bias, at.core * heads, heads, 0)
    logits = dot_nt(forget_t, normed_one) + bias[:, None]
    logs = jax.nn.log_sigmoid(logits).reshape(heads, 2, 2, rows_loc)
    steps = jnp.arange(rows_loc, dtype=jnp.int32)
    upper = (steps[:, None] <= steps[None, :]).astype(F32)
    sums = jnp.einsum("hpbt,ts->hpbs", logs, upper, precision=HIGHEST)
    total = sums[..., -1:]
    later = at.y.astype(F32)
    cumul = jnp.stack(
        [sums[:, :, 0] + later * total[:, :, 1], sums[:, :, 1] + (1.0 - later) * total[:, :, 0]],
        axis=2,
    ).reshape(heads, 2 * pack)
    seg_own = segment_ids[0].reshape(2, rows_loc)
    seg_own = jnp.where(at.y == 0, seg_own, seg_own[::-1]).reshape(1, pack)
    seg_both = jnp.concatenate([seg_own, at.swap_core(seg_own)], axis=1).astype(F32)
    aux = jnp.concatenate(
        [
            cumul.reshape(pairs, 2, 2 * pack),
            jnp.broadcast_to(seg_both[None], (pairs, 6, 2 * pack)),
        ],
        axis=1,
    )
    mixed, inverse, expos, tops = attend(y_index, qkv, aux, 2, pairs)

    moved = ffn_ring.advance(mixed)
    part, got = at.meet_core(after(mixed, *moved), wo_all, dot_nt)
    mine = part + got.astype(F32)
    given = mine[rows_loc:].astype(BF16)
    got = at.swap_y(given)
    resid = x_own + (mine[:rows_loc] + got.astype(F32))
    scale_two = lax.rsqrt(jnp.mean(resid * resid, axis=1, keepdims=True) + EPSILON)
    unit_two = resid * scale_two
    normed_own = (unit_two * gain_two).astype(BF16)
    near = at.swap_y(normed_own)
    moved = ffn_ring.advance(normed_own)
    (near,) = after_all((near,), *moved)
    normed_two = at.join(normed_own, near)
    ffn_ring.advance(normed_two)
    ffn_all = ffn_ring.finish()
    gu_all, down_all = ffn_all[:, : 2 * units], ffn_all[:, 2 * units :]

    gate_up = dot_nn(normed_two, gu_all)
    gate_pre, up_pre = gate_up[:, :units], gate_up[:, units:]
    gate_sig = jax.nn.sigmoid(gate_pre)
    gate_act = gate_pre * gate_sig
    hidden = (gate_act * up_pre).astype(BF16)
    grad_hidden = dot_nn(grad_rows, down_all)
    grad_gate = (grad_hidden * up_pre * gate_sig * (1.0 + gate_pre * (1.0 - gate_sig))).astype(BF16)
    grad_up = (grad_hidden * gate_act).astype(BF16)
    grad_gu = jnp.concatenate([grad_gate, grad_up], axis=1)

    part, got = at.meet_core(grad_gu, gu_all, dot_nt)
    down_sum = Reduction(at, dot_tn(grad_rows, after(hidden, part)).astype(BF16))
    mine = part + after(got, down_sum.blocks).astype(F32)
    given = mine[rows_loc:].astype(BF16)
    got = at.swap_y(given)
    gu_sum = Reduction(at, dot_tn(normed_two, after(grad_gu, given)).astype(BF16))
    moved = down_sum.advance(gu_sum.blocks)

    (got,) = after_all((got,), *moved)
    grad_two = mine[:rows_loc] + got.astype(F32)
    weighted = gain_two * grad_two
    inner_two = jnp.mean(unit_two * weighted, axis=1, keepdims=True)
    norm2_part = jnp.sum(grad_two * unit_two, axis=0)
    grad_resid = out_grad.astype(F32) + scale_two * (weighted - unit_two * inner_two)
    grad_own = grad_resid.astype(BF16)
    near = at.swap_y(grad_own)
    moved = gu_sum.advance(grad_own)
    out_given = dot_nt(after(hidden, *moved)[pack:], down_all).astype(BF16)
    moved = down_sum.advance(out_given)
    out_part = dot_nt(after(hidden, *moved)[:pack], down_all)
    (near,) = after_all((near,), out_part)
    grad_attn = at.join(grad_own, near)

    grad_mixed = dot_nn(grad_attn, wo_all).astype(BF16)
    out_got = at.swap_core(after(out_given, grad_attn))
    moved = gu_sum.advance(grad_mixed)
    d_qkv, d_cum = attend_back(
        y_index, qkv, after(grad_mixed, *moved), inverse, expos, 2, pairs
    )

    def place(own):
        keep, got = at.finish_grad(own)
        return at.by_core(keep, got, 1)

    moved = down_sum.advance(d_qkv)
    moved = gu_sum.advance(*moved)
    middle = 7 * LANES
    low = dot_tn(normed_one, after(d_qkv, *moved)[:, :middle]).astype(BF16)
    d_cum = d_cum[:, :2].reshape(heads, 2, 2, rows_loc)
    back = jnp.einsum("hpbt,st->hpbs", d_cum, upper, precision=HIGHEST)
    ends = back[..., :1]
    d_log = jnp.stack(
        [back[:, :, 0] + (1.0 - later) * ends[:, :, 1], back[:, :, 1] + later * ends[:, :, 0]],
        axis=2,
    ).reshape(heads, 2 * pack)
    d_logit = d_log * jax.nn.sigmoid(-logits)
    bias_part = jnp.sum(d_logit, axis=1)
    d_split = jnp.concatenate(split_low(d_logit), axis=0).T
    d_split = jnp.pad(d_split, ((0, 0), (0, LANES - 2 * heads)))
    d_in = jnp.concatenate([d_qkv, d_split], axis=1)
    d_in_late, attn_late = after_all((d_in, grad_attn), low)
    high = jnp.concatenate(
        [dot_tn(normed_one, d_in_late[:, middle:]), dot_tn(attn_late, mixed)], axis=1
    ).astype(BF16)
    total = down_sum.finish(high)
    low_sum = Reduction(at, low, total)
    g_down = place(total)
    part, got = at.meet_core(after(d_in, *low_sum.sent), w_in, dot_nt)
    total = gu_sum.finish(part)
    high_sum = Reduction(at, high, total)
    mine = part + after(got, *high_sum.sent).astype(F32)
    given = mine[rows_loc:].astype(BF16)
    got = at.swap_y(given)
    moved = low_sum.advance(given)
    moved = high_sum.advance(*moved)
    moved = low_sum.advance(*moved)
    (got,) = after_all((got,), *moved)

    grad_one = mine[:rows_loc] + got.astype(F32)
    weighted = gain_one * grad_one
    inner_one = jnp.mean(unit_one * weighted, axis=1, keepdims=True)
    norm1_part = jnp.sum(grad_one * unit_one, axis=0)
    x_grad = (grad_resid + scale_one * (weighted - unit_one * inner_one)).astype(BF16)
    out_own = out_part + after(out_got, norm1_part).astype(F32)
    out_got = at.swap_y(out_own[rows_loc:].astype(BF16))
    layer_out = (resid + (out_own[:rows_loc] + out_got.astype(F32))).astype(BF16)
    moved = high_sum.advance(norm1_part)
    keep, other = at.finish_grad(total)
    g_gate = at.by_core(keep[:, :units], other[:, :units], 1)
    g_up = at.by_core(keep[:, units:], other[:, units:], 1)
    moved = low_sum.advance(*moved)
    moved = high_sum.advance(*moved)

    norms = after(jnp.stack([norm1_part, norm2_part]), *moved)
    norms = norms + at.swap_core(norms)
    cut = width // 2
    norms = lax.dynamic_slice_in_dim(norms, at.y * cut, cut, 1) + at.swap_y(
        lax.dynamic_slice_in_dim(norms, (1 - at.y) * cut, cut, 1)
    )
    maxima = jnp.max(tops[:, :, :2], axis=(0, 3)).reshape(heads)
    lone = jnp.pad(jnp.stack([bias_part, maxima]), ((0, 4), (0, cut - heads)))
    sums = at.sum_plane(
        jnp.concatenate([norms, lone], axis=0),
        lambda one, two: jnp.concatenate(
            [one[:3] + two[:3], jnp.maximum(one[3:], two[3:])], axis=0
        ),
    )
    lone = sums[2:4, :LANES]
    lone = at.by_core(lone[:, :heads], at.swap_core(lone)[:, :heads], 1)
    g_bias = lone[0]
    clip_factor = jnp.minimum(1.0, clip_tau / jnp.maximum(lone[1], 1.0))
    columns = jnp.repeat(jnp.sqrt(clip_factor), HEAD_DIM)
    clipped_query = (w_query.astype(F32) * columns[None, :]).astype(BF16)
    clipped_key = (w_key.astype(F32) * columns[None, :]).astype(BF16)

    g_in = jnp.concatenate([low_sum.finish(norms), high_sum.finish(norms)], axis=1)
    keep, got = at.finish_grad(g_in)

    def third(which):
        def pick(value):
            value = value[:, :qkv_cols].reshape(d_rows, pairs, 3, LANES)
            return value[:, :, which].reshape(d_rows, -1)

        return at.by_core(pick(keep), pick(got), 1)

    def forget(value):
        return value[:, qkv_cols : qkv_cols + heads] + value[:, qkv_cols + heads :][:, :heads]

    return (
        layer_out,
        x_grad,
        sums[0],
        third(0),
        third(1),
        third(2),
        at.by_core(forget(keep), forget(got), 1),
        g_bias,
        at.by_core(keep[:, in_cols:], got[:, in_cols:], 1),
        sums[1],
        g_gate,
        g_up,
        g_down,
        clip_factor,
        clipped_query,
        clipped_key,
    )


def pick_body(mesh):
    dp, tensor = mesh.shape["dp"], mesh.shape["tensor"]

    def body(*args):
        rows, heads = args[0].shape[0], args[7].shape[0]
        depth = dp // 4
        paired = (
            tensor == 2
            and dp % 4 == 0
            and depth & (depth - 1) == 0
            and rows == BLOCK
            and heads % 4 == 0
        )
        return (paired_body if paired else general_body)(*args)

    return body
def solution(mesh):
    return jax.shard_map(
        pick_body(mesh),
        mesh=mesh,
        in_specs=(
            P(("dp", "tensor"), None),
            P("dp", None),
            P("dp"),
            P("dp", "tensor"),
            P("dp", "tensor"),
            P("dp", "tensor"),
            P("dp", "tensor"),
            P("tensor"),
            P("dp", "tensor"),
            P("dp"),
            P("dp", "tensor"),
            P("dp", "tensor"),
            P("dp", "tensor"),
            P("tensor"),
            P(("dp", "tensor"), None),
        ),
        out_specs=(
            P(("dp", "tensor"), None),
            P(("dp", "tensor"), None),
            P("tensor"),
            P("dp", "tensor"),
            P("dp", "tensor"),
            P("dp", "tensor"),
            P("dp", "tensor"),
            P("tensor"),
            P("dp", "tensor"),
            P("tensor"),
            P("dp", "tensor"),
            P("dp", "tensor"),
            P("dp", "tensor"),
            P("tensor"),
            P("dp", "tensor"),
            P("dp", "tensor"),
        ),
        check_vma=False,
    )
```

```python
import math
from functools import partial

import jax
import jax.numpy as jnp
from jax import lax
from jax.experimental import pallas as pl
from jax.experimental.pallas import tpu as pltpu
from jax.sharding import PartitionSpec as P

HEAD_DIM = 64
BLOCK = 256
LANES = 128
EPSILON = 1e-06
HIGHEST = lax.Precision.HIGHEST
NEGATIVE = -1e30
F32 = jnp.float32
BF16 = jnp.bfloat16
def combined_all(part, axis, combine):
    gathered = jax.tree.map(lambda a: lax.all_gather(a, axis), part)

    def take(source):
        return jax.tree.map(lambda a: lax.dynamic_index_in_dim(a, source, 0, False), gathered)

    return lax.fori_loop(
        1, lax.axis_size(axis), lambda source, state: combine(state, take(source)), take(0)
    )


def contract_last(left_op, right_op):
    return lax.dot_general(
        left_op, right_op, (((1,), (1,)), ((), ())), preferred_element_type=jnp.float32
    )


def contract_first(left_op, right_op):
    return lax.dot_general(
        left_op, right_op, (((0,), (0,)), ((), ())), preferred_element_type=jnp.float32
    )


def block_terms(q_blk, keys_all, cumul, seg_row, offset, rows_blk):
    positions = jnp.arange(keys_all.shape[0], dtype=jnp.int32)
    q_pos = offset + jnp.arange(rows_blk, dtype=jnp.int32)
    allowed = (seg_row[:, None] == seg_row[None, :]) & (
        q_pos[:, None] // BLOCK >= positions[None, :] // BLOCK
    )
    signs = jnp.where(positions[None, :] <= q_pos[:, None], 1.0, -1.0).astype(jnp.float32)
    raw_blk = jnp.einsum("qhe,khe->hqk", q_blk, keys_all, preferred_element_type=jnp.float32) * (
        1.0 / math.sqrt(HEAD_DIM)
    )
    differ = cumul.T[:, :, None] - cumul.T[:, None, :]
    scores = jnp.where(allowed[None], raw_blk + signs[None] * differ, NEGATIVE)
    return (raw_blk, scores, allowed, signs)


def combine(former, latter):
    return (
        jnp.maximum(former[0], latter[0]),
        former[1] + latter[1],
        former[2] + latter[2],
        former[3] + latter[3],
    )


def general_body(
    layer_in,
    segment_ids,
    norm1_gain,
    w_query,
    w_key,
    w_value,
    w_forget,
    forget_bias,
    w_output,
    norm2_gain,
    w_gate,
    w_up,
    w_down,
    clip_tau,
    out_grad,
):
    gain_one, wq_all, wk_all, wv_all, wf_all, wo_all, gain_two, wg_all, wu_all, wd_all = (
        lax.all_gather(norm1_gain, "dp", axis=0, tiled=True),
        lax.all_gather(w_query, "dp", axis=0, tiled=True),
        lax.all_gather(w_key, "dp", axis=0, tiled=True),
        lax.all_gather(w_value, "dp", axis=0, tiled=True),
        lax.all_gather(w_forget, "dp", axis=0, tiled=True),
        lax.all_gather(w_output, "dp", axis=0, tiled=True),
        lax.all_gather(norm2_gain, "dp", axis=0, tiled=True),
        lax.all_gather(w_gate, "dp", axis=0, tiled=True),
        lax.all_gather(w_up, "dp", axis=0, tiled=True),
        lax.all_gather(w_down, "dp", axis=0, tiled=True),
    )
    gain_one = gain_one.astype(jnp.float32)
    gain_two = gain_two.astype(jnp.float32)
    tok_local = layer_in.shape[0]
    tokens = tok_local * lax.axis_size("tensor")
    heads_loc = forget_bias.shape[0]
    row_start = lax.axis_index("tensor") * tok_local
    seg_row = segment_ids[0]
    factor = 1.0 / math.sqrt(HEAD_DIM)
    rows_full = lax.all_gather(layer_in, "tensor", axis=0, tiled=True).astype(jnp.float32)
    scale_one = lax.rsqrt(jnp.mean(rows_full * rows_full, axis=1, keepdims=True) + EPSILON)
    unit_one = rows_full * scale_one
    normed_one = (unit_one * gain_one).astype(jnp.bfloat16)
    queries = (
        jnp.dot(normed_one, wq_all, preferred_element_type=jnp.float32)
        .astype(jnp.bfloat16)
        .reshape(tokens, heads_loc, HEAD_DIM)
    )
    keys_all = (
        jnp.dot(normed_one, wk_all, preferred_element_type=jnp.float32)
        .astype(jnp.bfloat16)
        .reshape(tokens, heads_loc, HEAD_DIM)
    )
    values_all = (
        jnp.dot(normed_one, wv_all, preferred_element_type=jnp.float32)
        .astype(jnp.bfloat16)
        .reshape(tokens, heads_loc, HEAD_DIM)
    )
    logits = jnp.dot(normed_one, wf_all, preferred_element_type=jnp.float32) + forget_bias
    cumul = jnp.cumsum(jax.nn.log_sigmoid(logits), axis=0)
    rows_blk = min(512, tokens)
    blocks = tokens // rows_blk
    numbers = jnp.arange(blocks, dtype=jnp.int32)

    def forward_block(number):
        offset = number * rows_blk
        raw_blk, scores, allowed, signs = block_terms(
            queries, keys_all, cumul, seg_row, offset, rows_blk
        )
        top_blk = jnp.max(jnp.where(allowed[None], raw_blk, NEGATIVE), axis=(1, 2))
        row_peak = jnp.max(scores, axis=2, keepdims=True)
        expo_blk = jnp.exp(scores - row_peak)
        totals = jnp.sum(expo_blk, axis=2, keepdims=True)
        weights = (expo_blk / totals).astype(jnp.bfloat16)
        mixed_out = jnp.einsum(
            "hqk,khe->qhe", weights, values_all, preferred_element_type=jnp.float32
        ).astype(jnp.bfloat16)
        return (mixed_out, (row_peak + jnp.log(totals))[:, :, 0], top_blk)

    mixed_out, log_sums, top_blk = lax.map(forward_block, numbers)
    mixed_flat = mixed_out.reshape(tokens, heads_loc * HEAD_DIM)
    maxima = jnp.max(top_blk, axis=0)
    attn_part = contract_last(mixed_flat, wo_all)
    resid_full = rows_full + lax.psum(attn_part.astype(jnp.bfloat16), "tensor").astype(jnp.float32)
    scale_full = lax.rsqrt(jnp.mean(resid_full * resid_full, axis=1, keepdims=True) + EPSILON)
    normed_two = (resid_full * scale_full * gain_two).astype(jnp.bfloat16)
    resid_part = lax.dynamic_slice_in_dim(resid_full, row_start, tok_local, 0)
    scale_two = lax.dynamic_slice_in_dim(scale_full, row_start, tok_local, 0)
    gate_pre = jnp.dot(normed_two, wg_all, preferred_element_type=jnp.float32)
    up_pre = jnp.dot(normed_two, wu_all, preferred_element_type=jnp.float32)
    gate_sig = jax.nn.sigmoid(gate_pre)
    gate_act = gate_pre * gate_sig
    hidden = (gate_act * up_pre).astype(jnp.bfloat16)
    ffn_part = lax.psum_scatter(
        contract_last(hidden, wd_all).astype(jnp.bfloat16),
        "tensor",
        scatter_dimension=0,
        tiled=True,
    ).astype(jnp.float32)
    layer_out = (resid_part + ffn_part).astype(jnp.bfloat16)
    grad_full = lax.all_gather(out_grad, "tensor", axis=0, tiled=True)
    grad_hidden = jnp.dot(grad_full, wd_all, preferred_element_type=jnp.float32)
    grad_gate = (grad_hidden * up_pre * gate_sig * (1.0 + gate_pre * (1.0 - gate_sig))).astype(
        jnp.bfloat16
    )
    grad_up = (grad_hidden * gate_act).astype(jnp.bfloat16)
    g_down = contract_first(grad_full, hidden)
    g_gate = contract_first(normed_two, grad_gate)
    g_up = contract_first(normed_two, grad_up)
    grad_normed = contract_last(grad_gate, wg_all) + contract_last(grad_up, wu_all)
    grad_two = lax.psum_scatter(
        grad_normed.astype(jnp.bfloat16), "tensor", scatter_dimension=0, tiled=True
    ).astype(jnp.float32)
    unit_two = resid_part * scale_two
    inner_two = jnp.mean(unit_two * gain_two * grad_two, axis=1, keepdims=True)
    norm2_part = jnp.sum(grad_two * unit_two, axis=0)
    grad_resid = out_grad.astype(jnp.float32) + scale_two * (
        gain_two * grad_two - unit_two * inner_two
    )
    grad_attn = lax.all_gather(grad_resid.astype(jnp.bfloat16), "tensor", axis=0, tiled=True)
    g_output = contract_first(grad_attn, mixed_flat)
    grad_mixed = jnp.dot(grad_attn, wo_all, preferred_element_type=jnp.float32).astype(jnp.bfloat16)
    grad_mixed = grad_mixed.reshape(blocks, rows_blk, heads_loc, HEAD_DIM)

    def backward_block(carried, block_in):
        key_acc, value_acc, column_acc = carried
        number, log_blk, grad_blk = block_in
        offset = number * rows_blk
        raw_blk, scores, allowed, signs = block_terms(
            queries, keys_all, cumul, seg_row, offset, rows_blk
        )
        prob_blk = jnp.exp(scores - log_blk[:, :, None])
        weights = prob_blk.astype(jnp.bfloat16)
        grad_prob = jnp.einsum(
            "qhe,khe->hqk", grad_blk, values_all, preferred_element_type=jnp.float32
        )
        inner = jnp.sum(prob_blk * grad_prob, axis=2, keepdims=True)
        grad_scores = (prob_blk * (grad_prob - inner)).astype(jnp.bfloat16)
        value_acc = value_acc + jnp.einsum(
            "hqk,qhe->khe", weights, grad_blk, preferred_element_type=jnp.float32
        )
        key_acc = key_acc + jnp.einsum(
            "hqk,qhe->khe", grad_scores, queries, preferred_element_type=jnp.float32
        )
        grad_query = (
            jnp.einsum("hqk,khe->qhe", grad_scores, keys_all, preferred_element_type=jnp.float32)
            * factor
        ).astype(jnp.bfloat16)
        signed = grad_scores.astype(jnp.float32) * signs[None]
        column_acc = column_acc - jnp.sum(signed, axis=1).T
        return ((key_acc, value_acc, column_acc), (grad_query, jnp.sum(signed, axis=2).T))

    start_acc = (
        jnp.zeros((tokens, heads_loc, HEAD_DIM), jnp.float32),
        jnp.zeros((tokens, heads_loc, HEAD_DIM), jnp.float32),
        jnp.zeros((tokens, heads_loc), jnp.float32),
    )
    (key_acc, value_acc, column_acc), (grad_query, row_parts) = lax.scan(
        backward_block, start_acc, (numbers, log_sums, grad_mixed)
    )
    grad_q = grad_query.reshape(tokens, heads_loc * HEAD_DIM)
    grad_k = (key_acc * factor).astype(jnp.bfloat16).reshape(tokens, heads_loc * HEAD_DIM)
    grad_v = value_acc.astype(jnp.bfloat16).reshape(tokens, heads_loc * HEAD_DIM)
    grad_cum = row_parts.reshape(tokens, heads_loc) + column_acc
    grad_logs = jnp.cumsum(grad_cum[::-1], axis=0)[::-1]
    grad_logit = grad_logs * jax.nn.sigmoid(-logits)
    g_bias = jnp.sum(grad_logit, axis=0)
    g_forget = jnp.einsum(
        "td,th->dh", normed_one, grad_logit, precision=HIGHEST, preferred_element_type=jnp.float32
    )
    g_query = contract_first(normed_one, grad_q)
    g_key = contract_first(normed_one, grad_k)
    g_value = contract_first(normed_one, grad_v)
    grad_one = (
        contract_last(grad_q, wq_all)
        + contract_last(grad_k, wk_all)
        + contract_last(grad_v, wv_all)
    )
    grad_one = grad_one + jnp.einsum(
        "th,dh->td", grad_logit, wf_all, precision=HIGHEST, preferred_element_type=jnp.float32
    )
    weighted = gain_one * grad_one
    grad_rows_one = scale_one * (
        weighted - unit_one * jnp.mean(unit_one * weighted, axis=1, keepdims=True)
    )
    norm1_part = jnp.sum(grad_one * unit_one, axis=0)
    grad_input, g_norm1_part, g_norm2_part = (
        lax.psum_scatter(
            grad_rows_one.astype(jnp.bfloat16), "tensor", scatter_dimension=0, tiled=True
        ).astype(jnp.float32),
        lax.psum_scatter(
            norm1_part.astype(jnp.bfloat16), "tensor", scatter_dimension=0, tiled=True
        ).astype(jnp.float32),
        lax.psum_scatter(
            norm2_part.astype(jnp.bfloat16), "tensor", scatter_dimension=0, tiled=True
        ).astype(jnp.float32),
    )
    x_grad = (grad_resid + grad_input).astype(jnp.bfloat16)
    g_query, g_key, g_value, g_forget, g_output, g_gate, g_up, g_down = (
        lax.psum_scatter(
            g_query.astype(jnp.bfloat16), "dp", scatter_dimension=0, tiled=True
        ).astype(jnp.float32),
        lax.psum_scatter(g_key.astype(jnp.bfloat16), "dp", scatter_dimension=0, tiled=True).astype(
            jnp.float32
        ),
        lax.psum_scatter(
            g_value.astype(jnp.bfloat16), "dp", scatter_dimension=0, tiled=True
        ).astype(jnp.float32),
        lax.psum_scatter(
            g_forget.astype(jnp.bfloat16), "dp", scatter_dimension=0, tiled=True
        ).astype(jnp.float32),
        lax.psum_scatter(
            g_output.astype(jnp.bfloat16), "dp", scatter_dimension=0, tiled=True
        ).astype(jnp.float32),
        lax.psum_scatter(g_gate.astype(jnp.bfloat16), "dp", scatter_dimension=0, tiled=True).astype(
            jnp.float32
        ),
        lax.psum_scatter(g_up.astype(jnp.bfloat16), "dp", scatter_dimension=0, tiled=True).astype(
            jnp.float32
        ),
        lax.psum_scatter(g_down.astype(jnp.bfloat16), "dp", scatter_dimension=0, tiled=True).astype(
            jnp.float32
        ),
    )
    maxima, g_bias, g_norm1, g_norm2 = combined_all(
        (maxima, g_bias, g_norm1_part, g_norm2_part), "dp", combine
    )
    clip_factor = jnp.minimum(1.0, clip_tau / jnp.maximum(maxima, 1.0))
    columns = jnp.repeat(jnp.sqrt(clip_factor), HEAD_DIM)
    clipped_query = (w_query.astype(jnp.float32) * columns[None, :]).astype(jnp.bfloat16)
    clipped_key = (w_key.astype(jnp.float32) * columns[None, :]).astype(jnp.bfloat16)
    return (
        layer_out,
        x_grad,
        g_norm1,
        g_query,
        g_key,
        g_value,
        g_forget,
        g_bias,
        g_output,
        g_norm2,
        g_gate,
        g_up,
        g_down,
        clip_factor,
        clipped_query,
        clipped_key,
    )


def dot_nt(left, right):
    return lax.dot_general(left, right, (((1,), (1,)), ((), ())), preferred_element_type=F32)


def dot_nn(left, right):
    return lax.dot_general(left, right, (((1,), (0,)), ((), ())), preferred_element_type=F32)


def dot_tn(left, right):
    return lax.dot_general(left, right, (((0,), (0,)), ((), ())), preferred_element_type=F32)


def attend_kernel(y_ref, qkv_ref, aux_ref, *refs):
    o_ref, inv_ref, exp_ref, top_ref = refs[-4:]
    y = y_ref[0]
    starts = (pl.multiple_of(y * BLOCK, BLOCK), pl.multiple_of((1 - y) * BLOCK, BLOCK))
    lane = lax.broadcasted_iota(jnp.int32, (1, LANES), 1)
    first = lane < HEAD_DIM
    aux = [aux_ref[0, :, pl.ds(start, BLOCK)] for start in starts]
    aux_col = [a.T for a in aux]
    q_blk = [qkv_ref[pl.ds(s, BLOCK), 0:LANES] * 0.125 for s in starts]
    k_blk = [qkv_ref[pl.ds(s, BLOCK), LANES : 2 * LANES] for s in starts]
    v_blk = [qkv_ref[pl.ds(s, BLOCK), 2 * LANES : 3 * LANES] for s in starts]
    same = {}
    for i, j in ((0, 0), (1, 0), (1, 1)):
        same[i, j] = aux_col[i][:, 2:3] == aux[j][2:3, :]
    tops = []
    results = [[], []]
    for head in range(2):
        mine = first if head == 0 else jnp.logical_not(first)
        top = None
        v_ext = [jnp.where(mine, v, jnp.ones_like(v)) for v in v_blk]
        k_head = [jnp.where(mine, k, jnp.zeros_like(k)) for k in k_blk]
        for i in range(2):
            scores = []
            for j in range(i + 1):
                raw = dot_nt(q_blk[i], k_head[j])
                seen = jnp.where(same[i, j], raw, NEGATIVE)
                high = jnp.max(seen, axis=0, keepdims=True)
                top = high if top is None else jnp.maximum(top, high)
                differ = aux_col[i][:, head : head + 1] - aux[j][head : head + 1, :]
                scores.append(seen - jnp.abs(differ))
            peak = jnp.max(scores[0], axis=1, keepdims=True)
            if i == 1:
                peak = jnp.maximum(peak, jnp.max(scores[1], axis=1, keepdims=True))
            acc = None
            for j in range(i + 1):
                weights = jnp.exp(scores[j] - peak).astype(BF16)
                exp_ref[0, 0, head, :, (i + j) * BLOCK : (i + j + 1) * BLOCK] = weights
                part = dot_nn(weights, v_ext[j])
                acc = part if acc is None else acc + part
            results[i].append(acc)
        tops.append(jnp.maximum(top[:, :LANES], top[:, LANES:]))
    for i in range(2):
        one, two = results[i]
        total = pltpu.roll(jnp.where(first, two, one), HEAD_DIM, 1)
        inverse = 1.0 / total
        inv_ref[pl.ds(starts[i], BLOCK), :] = inverse
        o_ref[pl.ds(starts[i], BLOCK), :] = (jnp.where(first, one, two) * inverse).astype(BF16)
    row = lax.broadcasted_iota(jnp.int32, (8, LANES), 0)
    top_ref[0, 0] = jnp.where(row == 0, tops[0], tops[1])


def attend(y_index, qkv, aux, packs, pairs, pack, kept=()):
    rows = qkv.shape[0] // packs
    wide = 3 * LANES
    grid_spec = pltpu.PrefetchScalarGridSpec(
        num_scalar_prefetch=1,
        grid=(pairs,),
        in_specs=[
            pl.BlockSpec((rows, wide), lambda h, y: (pack, h)),
            pl.BlockSpec((1, 8, rows), lambda h, y: (h, 0, pack)),
        ]
        + [pl.BlockSpec(memory_space=pl.ANY) for _ in kept],
        out_specs=[
            pl.BlockSpec((rows, LANES), lambda h, y: (0, h)),
            pl.BlockSpec((rows, LANES), lambda h, y: (pack, h)),
            pl.BlockSpec((1, 1, 2, BLOCK, 3 * BLOCK), lambda h, y: (pack, h, 0, 0, 0)),
            pl.BlockSpec((1, 1, 8, LANES), lambda h, y: (0, h, 0, 0)),
        ],
    )
    return pl.pallas_call(
        attend_kernel,
        grid_spec=grid_spec,
        out_shape=(
            jax.ShapeDtypeStruct((rows, pairs * LANES), BF16),
            jax.ShapeDtypeStruct((packs * rows, pairs * LANES), F32),
            jax.ShapeDtypeStruct((packs, pairs, 2, BLOCK, 3 * BLOCK), BF16),
            jax.ShapeDtypeStruct((1, pairs, 8, LANES), F32),
        ),
        input_output_aliases={3: 1, 4: 2} if kept else {},
        cost_estimate=pl.CostEstimate(
            flops=pairs * 2 * 6 * BLOCK * BLOCK * LANES * 2,
            bytes_accessed=10_000_000,
            transcendentals=pairs * 2 * 3 * BLOCK * BLOCK,
        ),
        name="attend",
    )(y_index, qkv, aux, *kept)


def attend_back_kernel(
    pairs, y_ref, qkv_ref, do_ref, inv_ref, exp_ref, aux_ref, dqkv_ref, split_ref
):
    y = y_ref[0]
    starts = (pl.multiple_of(y * BLOCK, BLOCK), pl.multiple_of((1 - y) * BLOCK, BLOCK))
    lane = lax.broadcasted_iota(jnp.int32, (1, LANES), 1)
    first = lane < HEAD_DIM
    ones = jnp.ones((8, BLOCK), BF16)
    lower = lax.broadcasted_iota(jnp.int32, (BLOCK, BLOCK), 1) <= lax.broadcasted_iota(
        jnp.int32, (BLOCK, BLOCK), 0
    )
    q_blk = [qkv_ref[pl.ds(s, BLOCK), 0:LANES] * 0.125 for s in starts]
    k_blk = [qkv_ref[pl.ds(s, BLOCK), LANES : 2 * LANES] for s in starts]
    v_blk = [qkv_ref[pl.ds(s, BLOCK), 2 * LANES : 3 * LANES] for s in starts]
    inv_blk = [inv_ref[pl.ds(s, BLOCK), :] for s in starts]
    do_blk = [
        (do_ref[pl.ds(s, BLOCK), :].astype(F32) * inv).astype(BF16)
        for s, inv in zip(starts, inv_blk)
    ]
    dq, dk, dv, dc = ([], []), ([], []), ([], []), ([], [])
    for head in range(2):
        mine = first if head == 0 else jnp.logical_not(first)
        v_head = [jnp.where(mine, v, jnp.zeros_like(v)) for v in v_blk]
        dk_acc, dv_acc, row_acc, col_acc = [None] * 2, [None] * 2, [None] * 2, [None] * 2
        for i in range(2):
            expos, probs, inner = [], [], None
            inv_col = inv_blk[i][:, head * HEAD_DIM : head * HEAD_DIM + 1]
            for j in range(i + 1):
                expo = exp_ref[0, 0, head, :, (i + j) * BLOCK : (i + j + 1) * BLOCK]
                grad_prob = dot_nt(do_blk[i], v_head[j])
                wide = expo.astype(F32)
                part = jnp.sum(wide * grad_prob, axis=1, keepdims=True)
                inner = part if inner is None else inner + part
                expos.append((expo, wide))
                probs.append(grad_prob)
            inner = inner * inv_col
            dq_acc = None
            for j in range(i + 1):
                expo, wide = expos[j]
                grad_score = wide * (probs[j] - inner)
                low = grad_score.astype(BF16)
                if i == j:
                    signed = jnp.where(lower, low, -low)
                else:
                    signed = low
                part = dot_nn(low, k_blk[j])
                dq_acc = part if dq_acc is None else dq_acc + part
                part = dot_tn(low, q_blk[i])
                dk_acc[j] = part if dk_acc[j] is None else dk_acc[j] + part
                part = dot_tn(expo, do_blk[i])
                dv_acc[j] = part if dv_acc[j] is None else dv_acc[j] + part
                part = dot_nt(ones, signed)
                row_acc[i] = part if row_acc[i] is None else row_acc[i] + part
                part = dot_nn(ones, signed)
                col_acc[j] = part if col_acc[j] is None else col_acc[j] + part
            dq[i].append(dq_acc)
        for j in range(2):
            dk[j].append(dk_acc[j])
            dv[j].append(dv_acc[j])
            dc[j].append(row_acc[j] - col_acc[j])
    for i in range(2):
        rows = pl.ds(starts[i], BLOCK)
        dqkv_ref[rows, 0:LANES] = (jnp.where(first, *dq[i]) * 0.125).astype(BF16)
        dqkv_ref[rows, LANES : 2 * LANES] = jnp.where(first, *dk[i]).astype(BF16)
        dqkv_ref[rows, 2 * LANES : 3 * LANES] = jnp.where(first, *dv[i]).astype(BF16)

    row = lax.broadcasted_iota(jnp.int32, (8, BLOCK), 0)
    until = jnp.where(lower, 1.0, 0.0).astype(BF16)
    d_cum = [jnp.where(row == 0, *dc[i]) for i in range(2)]
    ends = jnp.sum(d_cum[1], axis=1, keepdims=True)
    pair = pl.program_id(1)
    spot = lax.broadcasted_iota(jnp.int32, (8, LANES), 0)
    place = jnp.where(spot < 2, 2 * pair + spot, 2 * pairs + 2 * pair + spot - 2)
    hit = (lax.broadcasted_iota(jnp.int32, (8, LANES), 1) == place) & (spot < 4)
    hit = jnp.where(hit, 1.0, 0.0).astype(F32)

    @pl.when(pair == 0)
    def _():
        split_ref[...] = jnp.zeros_like(split_ref)

    for i in range(2):
        rows = pl.ds(starts[i], BLOCK)
        high = d_cum[i].astype(BF16).astype(F32)
        rest = d_cum[i] - high
        middle = rest.astype(BF16).astype(F32)
        low = pltpu.roll(rest - middle, 4, 0)
        parts = jnp.where(row < 4, pltpu.roll(middle, 2, 0), jnp.where(row < 6, low, 0.0))
        parts = jnp.where(row < 2, high, parts).astype(BF16)
        sums = dot_nn(parts, until)
        back = sums + pltpu.roll(sums, 6, 0) + pltpu.roll(sums, 4, 0)
        if i == 0:
            back = back + ends
        logit = pltpu.roll(aux_ref[0, :, rows], 4, 0)
        grad = back * jax.nn.sigmoid(-logit)
        high = grad.astype(BF16).astype(F32)
        rest = pltpu.roll((grad - high).astype(BF16).astype(F32), 2, 0)
        both = jnp.where(row < 2, high, jnp.where(row < 4, rest, 0.0))
        old = split_ref[rows, :].astype(F32)
        split_ref[rows, :] = (old + dot_tn(both, hit)).astype(BF16)


def attend_back(y_index, qkv, d_out, inverse, expos, aux, packs, pairs):
    rows = qkv.shape[0] // packs
    wide = 3 * LANES
    grid_spec = pltpu.PrefetchScalarGridSpec(
        num_scalar_prefetch=1,
        grid=(packs, pairs),
        in_specs=[
            pl.BlockSpec((rows, wide), lambda p, h, y: (p, h)),
            pl.BlockSpec((rows, LANES), lambda p, h, y: (p, h)),
            pl.BlockSpec((rows, LANES), lambda p, h, y: (p, h)),
            pl.BlockSpec((1, 1, 2, BLOCK, 3 * BLOCK), lambda p, h, y: (p, h, 0, 0, 0)),
            pl.BlockSpec((1, 8, rows), lambda p, h, y: (h, 0, p)),
        ],
        out_specs=[
            pl.BlockSpec((rows, wide), lambda p, h, y: (p, h)),
            pl.BlockSpec((rows, LANES), lambda p, h, y: (p, 0)),
        ],
    )
    return pl.pallas_call(
        partial(attend_back_kernel, pairs),
        grid_spec=grid_spec,
        out_shape=(
            jax.ShapeDtypeStruct((packs * rows, pairs * wide), BF16),
            jax.ShapeDtypeStruct((packs * rows, LANES), BF16),
        ),
        cost_estimate=pl.CostEstimate(
            flops=packs * pairs * 2 * 18 * BLOCK * BLOCK * LANES * 2,
            bytes_accessed=20_000_000,
            transcendentals=0,
        ),
        name="attend_back",
    )(y_index, qkv, d_out, inverse, expos, aux)


def assemble_kernel(core_ref, low_ref, got_low_ref, high_ref, got_high_ref, *outs):
    core = core_ref[0]
    rows = outs[0].shape[0]
    own = pl.ds(pl.multiple_of(core * rows, 8), rows)
    count = outs[0].shape[1] // (2 * LANES)
    middle = low_ref.shape[1]
    spots = [[3 * p + which for p in range(count)] for which in range(3)]
    spots.append([3 * count + 1 + p for p in range(count)])
    for out, chosen in zip(outs, spots):
        for p, spot in enumerate(chosen):
            start = spot * LANES
            mine_ref, got_ref = low_ref, got_low_ref
            if start >= middle:
                start -= middle
                mine_ref, got_ref = high_ref, got_high_ref
            lanes = slice(start, start + LANES)
            mine, got = mine_ref[own, lanes], got_ref[:, lanes].astype(F32)
            left = slice(p * LANES, (p + 1) * LANES)
            right = slice((count + p) * LANES, (count + p + 1) * LANES)
            out[:, left] = jnp.where(core == 0, mine, got)
            out[:, right] = jnp.where(core == 0, got, mine)


def assemble(core, low, got_low, high, got_high, pairs):
    shape = jax.ShapeDtypeStruct((got_low.shape[0], 2 * pairs * LANES), F32)
    spec = pl.BlockSpec(memory_space=pltpu.VMEM)
    return pl.pallas_call(
        assemble_kernel,
        in_specs=[pl.BlockSpec(memory_space=pltpu.SMEM)] + [spec] * 4,
        out_specs=[spec] * 4,
        out_shape=[shape] * 4,
        name="assemble",
    )(core.astype(jnp.int32).reshape(1), low, got_low, high, got_high)


class Gathering:
    def __init__(self, at, shard):
        self.at, self.step, self.half = at, 1, at.depth
        self.whole = None
        self.waiting = [(shard, 0, 0)]
        self.send(shard, shard)

    def store(self, *others):
        for part, step, side in self.waiting:
            if others:
                part = after(part, *others)
            if self.whole is None:
                self.whole = jnp.zeros((2 * self.half,) + part.shape, part.dtype)
                if others:
                    self.whole = after(self.whole, *others)
            start = (self.at.block_of(step), side, 0, 0)
            self.whole = lax.dynamic_update_slice(self.whole, part[None], start)
        self.waiting = []

    def send(self, up, down):
        if self.step == self.half:
            up, down = up[:1], down[1:]
        self.came = (self.at.ring(up, 1), self.at.ring(down, -1))

    def take(self, *others):
        up, down = after_all(self.came, *others)
        side = 1 if self.step == self.half else 0
        self.waiting += [(up, -self.step, 0), (down, self.step, side)]
        return up, down

    def advance(self, *others):
        up, down = self.take(*others)
        self.step += 1
        self.send(up, down)
        return up, down

    def finish(self, *others):
        self.take(*others)
        self.store()
        return self.whole.reshape(-1, self.whole.shape[-1])


class Reduction:
    def __init__(self, at, grad, *others):
        self.at, self.step, self.half = at, 1, at.depth
        count = 2 * at.depth
        self.blocks = grad.reshape(count, 2, grad.shape[0] // (2 * count), grad.shape[1])
        far = self.own(self.half)
        self.sent = after_all((far[:1], far[1:]), *others) if others else (far[:1], far[1:])
        self.send()

    def own(self, step):
        start = (self.at.block_of(step), 0, 0, 0)
        return lax.dynamic_slice(self.blocks, start, (1,) + self.blocks.shape[1:])[0]

    def send(self):
        self.came = (self.at.ring(self.sent[0], 1), self.at.ring(self.sent[1], -1))

    def advance(self, *others):
        up, down = after_all(self.came, *others)
        ahead, behind = self.own(self.half - self.step), self.own(self.step - self.half)
        if self.step == 1:
            first = (ahead[:1].astype(F32) + up.astype(F32)).astype(BF16)
            second = (behind[1:].astype(F32) + down.astype(F32)).astype(BF16)
            up = jnp.concatenate([first, ahead[1:]], axis=0)
            down = jnp.concatenate([behind[:1], second], axis=0)
        else:
            up = (ahead.astype(F32) + up.astype(F32)).astype(BF16)
            down = (behind.astype(F32) + down.astype(F32)).astype(BF16)
        self.sent = (up, down)
        self.step += 1
        self.send()
        return up, down

    def finish(self, *others):
        up, down = after_all(self.came, *others)
        total = self.own(0).astype(F32) + up.astype(F32) + down.astype(F32)
        return total.reshape(-1, total.shape[-1])


class Place:
    def __init__(self):
        self.dp = lax.axis_size("dp")
        self.depth = self.dp // 4
        index = lax.axis_index("dp")
        self.core = index % 2
        self.x = (index // 2) % 2
        self.z = index // 4
        self.y = lax.axis_index("tensor")

    def swap_core(self, value):
        return lax.ppermute(value, "dp", [(i, i ^ 1) for i in range(self.dp)])

    def swap_y(self, value):
        return lax.ppermute(value, "tensor", [(0, 1), (1, 0)])

    def ring(self, value, step):
        spots = [4 * z for z in range(self.depth)]
        spots += [4 * z + 2 for z in reversed(range(self.depth))]
        count = len(spots)
        pairs = [
            (spots[r] + core, spots[(r + step) % count] + core)
            for r in range(count)
            for core in (0, 1)
        ]
        return lax.ppermute(value, "dp", pairs)

    def block_of(self, step):
        count = 2 * self.depth
        spot = (jnp.where(self.x == 0, self.z, count - 1 - self.z) + step + count) % count
        return jnp.where(spot < self.depth, 2 * spot, 2 * (count - 1 - spot) + 1)

    def sum_plane(self, value, rings, combine):
        step = 2
        rings = list(rings)
        while step < self.dp:
            value = combine(
                value, lax.ppermute(value, "dp", [(i, i ^ step) for i in range(self.dp)])
            )
            if rings:
                value = after(value, *rings.pop(0).advance(value))
            step *= 2
        return value

    def by_core(self, mine, other, axis):
        return jnp.where(
            self.core == 0,
            jnp.concatenate([mine, other], axis=axis),
            jnp.concatenate([other, mine], axis=axis),
        )

    def core_columns(self, weights):
        half = [w.shape[1] // 2 for w in weights]
        keep = [
            lax.dynamic_slice_in_dim(w, self.core * h, h, 1) for w, h in zip(weights, half)
        ]
        give = [
            lax.dynamic_slice_in_dim(w, (1 - self.core) * h, h, 1) for w, h in zip(weights, half)
        ]
        return keep, give

    def finish_grad(self, own):
        rows = own.shape[0] // 2
        keep = lax.dynamic_slice_in_dim(own, self.core * rows, rows, 0)
        return keep, self.swap_core(self.theirs(own)).astype(F32)

    def theirs(self, own):
        rows = own.shape[0] // 2
        return lax.dynamic_slice_in_dim(own, (1 - self.core) * rows, rows, 0).astype(BF16)

    def join(self, rows, near):
        both = jnp.concatenate([rows, near], axis=0)
        return jnp.concatenate([both, self.swap_core(both)], axis=0)

    def meet_core(self, left, right, dot):
        half = left.shape[0] // 2
        given = dot(left[half:], right).astype(BF16)
        got = self.swap_core(given)
        part = dot(after(left, given)[:half], right)
        return part, got


def after(value, *others):
    return lax.optimization_barrier((value,) + others)[0]


def after_all(values, *others):
    return lax.optimization_barrier(tuple(values) + others)[: len(values)]


def interleave(parts):
    starts = range(0, parts[0].shape[1], LANES)
    return jnp.concatenate([p[:, s : s + LANES] for s in starts for p in parts], axis=1)


def split_low(value):
    high = value.astype(BF16)
    return high, (value - high.astype(F32)).astype(BF16)


def paired_body(
    layer_in,
    segment_ids,
    norm1_gain,
    w_query,
    w_key,
    w_value,
    w_forget,
    forget_bias,
    w_output,
    norm2_gain,
    w_gate,
    w_up,
    w_down,
    clip_tau,
    out_grad,
):
    at = Place()
    rows_loc = layer_in.shape[0]
    pack = 2 * rows_loc
    width = layer_in.shape[1]
    heads = forget_bias.shape[0] // 2
    pairs = heads // 2
    y_index = at.y.astype(jnp.int32).reshape(1)
    d_rows = norm1_gain.shape[0]

    units = w_gate.shape[1] // 2
    keep, give = at.core_columns([w_query, w_key, w_value, w_output, w_forget])
    gains = jnp.stack([norm1_gain, norm2_gain], axis=1)
    pad = jnp.zeros((d_rows, LANES - 2 * heads - 2), BF16)

    def first_part(part):
        return jnp.concatenate(
            [interleave(part[:3]), part[4], part[4], gains, pad, part[3]], axis=1
        )

    attn_shard = at.by_core(first_part(keep)[None], at.swap_core(first_part(give))[None], 0)
    rows_near = at.swap_y(layer_in)
    grad_near = at.swap_y(after(out_grad, rows_near))
    qkv_cols = 3 * heads * HEAD_DIM
    in_cols = qkv_cols + LANES
    attn_ring = Gathering(at, attn_shard)
    early = attn_ring.advance()
    attn_ring.store()
    keep, give = at.core_columns(after_all((w_gate, w_up, w_down), *early))
    ffn_shard = at.by_core(
        jnp.concatenate(keep, axis=1)[None],
        at.swap_core(jnp.concatenate(give, axis=1))[None],
        0,
    )
    attn_ring.advance(rows_near)
    attn_ring.store()
    attn_ring.advance(grad_near)
    attn_ring.store()
    ffn_ring = Gathering(at, after(ffn_shard, *attn_ring.came))
    attn_all = attn_ring.finish()
    w_in, wo_all = attn_all[:, :in_cols], attn_all[:, in_cols:]
    rows_all = at.join(layer_in, rows_near)
    grad_rows = at.join(out_grad, grad_near)
    w_qkv = w_in[:, :qkv_cols]
    small = w_in[:, qkv_cols:].T
    forget_t = small[:heads]
    gain_one = small[2 * heads : 2 * heads + 1].astype(F32)
    gain_two = small[2 * heads + 1 : 2 * heads + 2].astype(F32)

    def first_norm(rows):
        rows = rows.astype(F32)
        return rows, lax.rsqrt(jnp.mean(rows * rows, axis=1, keepdims=True) + EPSILON)

    x_all, scale_all = first_norm(rows_all)
    normed_one = (x_all * scale_all * gain_one).astype(BF16)
    x_own, scale_one = first_norm(layer_in)
    unit_one = x_own * scale_one
    qkv = dot_nn(normed_one, w_qkv).astype(BF16)

    bias = lax.dynamic_slice_in_dim(forget_bias, at.core * heads, heads, 0)
    logits = dot_nt(forget_t, normed_one) + bias[:, None]
    logs = jax.nn.log_sigmoid(logits).reshape(heads, 2, 2, rows_loc)
    steps = jnp.arange(rows_loc, dtype=jnp.int32)
    upper = (steps[:, None] <= steps[None, :]).astype(F32)
    sums = jnp.einsum("hpbt,ts->hpbs", logs, upper, precision=HIGHEST)
    total = sums[..., -1:]
    later = at.y.astype(F32)
    cumul = jnp.stack(
        [sums[:, :, 0] + later * total[:, :, 1], sums[:, :, 1] + (1.0 - later) * total[:, :, 0]],
        axis=2,
    ).reshape(heads, 2 * pack)
    seg_own = after(segment_ids, *early)[0].reshape(2, rows_loc)
    seg_own = jnp.where(at.y == 0, seg_own, seg_own[::-1]).reshape(1, pack)
    seg_both = jnp.concatenate([seg_own, at.swap_core(seg_own)], axis=1).astype(F32)
    aux = jnp.concatenate(
        [
            cumul.reshape(pairs, 2, 2 * pack),
            jnp.broadcast_to(seg_both[None], (pairs, 2, 2 * pack)),
            logits.reshape(pairs, 2, 2 * pack),
            jnp.zeros((pairs, 2, 2 * pack), F32),
        ],
        axis=1,
    )
    mixed_other, inverse, expos, tops_other = attend(y_index, qkv, aux, 2, pairs, 1)
    moved = ffn_ring.advance(mixed_other)

    given = dot_nt(after(mixed_other, *moved), wo_all).astype(BF16)
    got = at.swap_core(given)
    mixed_own, inverse, expos, tops = attend(
        y_index, after(qkv, given), aux, 2, pairs, 0, (inverse, expos)
    )
    tops = jnp.concatenate([tops, tops_other], axis=0)
    mixed = jnp.concatenate([mixed_own, mixed_other], axis=0)
    mine = dot_nt(mixed_own, wo_all) + after(got, mixed_own).astype(F32)
    given = mine[rows_loc:].astype(BF16)
    got = at.swap_y(given)
    ffn_ring.store(given)
    moved = ffn_ring.advance(given)
    (got,) = after_all((got,), *moved)
    resid = x_own + (mine[:rows_loc] + got.astype(F32))
    scale_two = lax.rsqrt(jnp.mean(resid * resid, axis=1, keepdims=True) + EPSILON)
    unit_two = resid * scale_two
    normed_own = (unit_two * gain_two).astype(BF16)
    near = at.swap_y(normed_own)
    ffn_ring.store(normed_own)
    moved = ffn_ring.advance(normed_own)
    (near,) = after_all((near,), *moved)
    normed_two = at.join(normed_own, near)
    ffn_ring.store(near)
    ffn_all = ffn_ring.finish()
    gu_all, down_all = ffn_all[:, : 2 * units], ffn_all[:, 2 * units :]

    gate_up = dot_nn(normed_two, gu_all)
    gate_pre, up_pre = gate_up[:, :units], gate_up[:, units:]
    gate_sig = jax.nn.sigmoid(gate_pre)
    gate_act = gate_pre * gate_sig
    hidden = (gate_act * up_pre).astype(BF16)
    grad_hidden = dot_nn(grad_rows, down_all)
    grad_gate = (grad_hidden * up_pre * gate_sig * (1.0 + gate_pre * (1.0 - gate_sig))).astype(BF16)
    grad_up = (grad_hidden * gate_act).astype(BF16)
    grad_gu = jnp.concatenate([grad_gate, grad_up], axis=1)

    part, got = at.meet_core(grad_gu, gu_all, dot_nt)
    down_sum = Reduction(at, dot_tn(grad_rows, after(hidden, part)).astype(BF16))
    mine = part + after(got, down_sum.blocks).astype(F32)
    given = mine[rows_loc:].astype(BF16)
    got = at.swap_y(given)
    gu_sum = Reduction(at, dot_tn(normed_two, after(grad_gu, given)).astype(BF16))
    moved = down_sum.advance(gu_sum.blocks)

    (got,) = after_all((got,), *moved)
    grad_two = mine[:rows_loc] + got.astype(F32)
    weighted = gain_two * grad_two
    inner_two = jnp.mean(unit_two * weighted, axis=1, keepdims=True)
    norm2_part = jnp.sum(grad_two * unit_two, axis=0)
    grad_resid = out_grad.astype(F32) + scale_two * (weighted - unit_two * inner_two)
    grad_own = grad_resid.astype(BF16)
    near = at.swap_y(grad_own)
    moved = gu_sum.advance(grad_own)
    out_given = dot_nt(after(hidden, *moved)[pack:], down_all).astype(BF16)
    moved = down_sum.advance(out_given)
    out_part = dot_nt(after(hidden, *moved)[:pack], down_all)
    moved = gu_sum.advance(out_part)
    (near,) = after_all((near,), *moved)
    grad_attn = at.join(grad_own, near)

    out_got = at.swap_core(after(out_given, grad_attn))
    grad_mixed = dot_nn(grad_attn, wo_all).astype(BF16)
    out_own = out_part + after(out_got, grad_mixed).astype(F32)
    out_given = out_own[rows_loc:].astype(BF16)
    out_got = at.swap_y(out_given)
    moved = down_sum.advance(out_given)
    d_qkv, d_split = attend_back(
        y_index, qkv, after(grad_mixed, *moved), inverse, expos, aux, 2, pairs
    )
    moved = gu_sum.advance(d_qkv)
    middle = 7 * LANES
    low = dot_tn(normed_one, after(d_qkv, *moved)[:, :middle]).astype(BF16)
    total_down = down_sum.finish(low)
    low_sum = Reduction(at, low, total_down)
    d_in = jnp.concatenate([d_qkv, after(d_split, *low_sum.sent)], axis=1)
    bias_part = jnp.sum(d_split.astype(F32), axis=0)
    bias_part = bias_part[:heads] + bias_part[heads : 2 * heads]
    given = dot_nt(d_in[pack:], w_in).astype(BF16)
    got = at.swap_core(given)
    d_in_late, attn_late = after_all((d_in, grad_attn), given)
    high = jnp.concatenate(
        [dot_tn(normed_one, d_in_late[:, middle:]), dot_tn(attn_late, mixed)], axis=1
    ).astype(BF16)
    part = dot_nt(after(d_in, high)[:pack], w_in)
    mine = part + after(got, part).astype(F32)
    given = mine[rows_loc:].astype(BF16)
    got = at.swap_y(given)
    total_gu = gu_sum.finish(given)
    high_sum = Reduction(at, high, total_gu)
    layer_out = resid + (out_own[:rows_loc] + after(out_got, low).astype(F32))
    layer_out = layer_out.astype(BF16)
    moved = low_sum.advance(layer_out, *high_sum.sent)
    moved = high_sum.advance(*moved)
    (got,) = after_all((got,), *moved)

    grad_one = mine[:rows_loc] + got.astype(F32)
    weighted = gain_one * grad_one
    inner_one = jnp.mean(unit_one * weighted, axis=1, keepdims=True)
    norm1_part = jnp.sum(grad_one * unit_one, axis=0)
    x_grad = (grad_resid + scale_one * (weighted - unit_one * inner_one)).astype(BF16)
    moved = low_sum.advance(norm1_part)
    moved = high_sum.advance(*moved)

    maxima = jnp.max(tops[:, :, :2], axis=(0, 3)).reshape(heads)
    lone = jnp.pad(jnp.stack([bias_part, maxima]), ((0, 4), (0, width - heads)))
    sums = at.sum_plane(
        jnp.concatenate([jnp.stack([norm1_part, norm2_part]), lone], axis=0),
        (low_sum, high_sum),
        lambda one, two: jnp.concatenate(
            [one[:3] + two[:3], jnp.maximum(one[3:], two[3:])], axis=0
        ),
    )
    other = at.swap_core(sums)
    cut = width // 2
    norms = sums[:2] + other[:2]
    norms = lax.dynamic_slice_in_dim(norms, at.y * cut, cut, 1) + at.swap_y(
        lax.dynamic_slice_in_dim(norms, (1 - at.y) * cut, cut, 1)
    )
    lone = at.by_core(sums[2:4, :heads], other[2:4, :heads], 1)
    g_bias = lone[0]
    clip_factor = jnp.minimum(1.0, clip_tau / jnp.maximum(lone[1], 1.0))
    columns = jnp.repeat(jnp.sqrt(clip_factor), HEAD_DIM)
    clipped_query = (w_query.astype(F32) * columns[None, :]).astype(BF16)
    clipped_key = (w_key.astype(F32) * columns[None, :]).astype(BF16)

    def place(own):
        keep, got = at.finish_grad(own)
        return at.by_core(keep, got, 1)

    g_down = place(total_down)
    keep, got = at.finish_grad(total_gu)
    g_gate = at.by_core(keep[:, :units], got[:, :units], 1)
    g_up = at.by_core(keep[:, units:], got[:, units:], 1)
    low, high = low_sum.finish(), high_sum.finish()
    got_low, got_high = at.swap_core(at.theirs(low)), at.swap_core(at.theirs(high))
    g_query, g_key, g_value, g_output = assemble(at.core, low, got_low, high, got_high, pairs)
    start = qkv_cols - middle
    mine = lax.dynamic_slice(high, (at.core * d_rows, start), (d_rows, 2 * heads))
    both = at.by_core(mine[None], got_high[None, :, start : start + 2 * heads].astype(F32), 0)
    g_forget = both[..., :heads] + both[..., heads:]
    g_forget = jnp.concatenate([g_forget[0], g_forget[1]], axis=1)

    return (
        layer_out,
        x_grad,
        norms[0],
        g_query,
        g_key,
        g_value,
        g_forget,
        g_bias,
        g_output,
        norms[1],
        g_gate,
        g_up,
        g_down,
        clip_factor,
        clipped_query,
        clipped_key,
    )


def pick_body(mesh):
    dp, tensor = mesh.shape["dp"], mesh.shape["tensor"]

    def body(*args):
        rows, heads = args[0].shape[0], args[7].shape[0]
        depth = dp // 4
        paired = (
            tensor == 2
            and dp % 4 == 0
            and depth & (depth - 1) == 0
            and rows == BLOCK
            and heads % 4 == 0
        )
        return (paired_body if paired else general_body)(*args)

    return body
def solution(mesh):
    return jax.shard_map(
        pick_body(mesh),
        mesh=mesh,
        in_specs=(
            P(("dp", "tensor"), None),
            P("dp", None),
            P("dp"),
            P("dp", "tensor"),
            P("dp", "tensor"),
            P("dp", "tensor"),
            P("dp", "tensor"),
            P("tensor"),
            P("dp", "tensor"),
            P("dp"),
            P("dp", "tensor"),
            P("dp", "tensor"),
            P("dp", "tensor"),
            P("tensor"),
            P(("dp", "tensor"), None),
        ),
        out_specs=(
            P(("dp", "tensor"), None),
            P(("dp", "tensor"), None),
            P("tensor"),
            P("dp", "tensor"),
            P("dp", "tensor"),
            P("dp", "tensor"),
            P("dp", "tensor"),
            P("tensor"),
            P("dp", "tensor"),
            P("tensor"),
            P("dp", "tensor"),
            P("dp", "tensor"),
            P("dp", "tensor"),
            P("tensor"),
            P("dp", "tensor"),
            P("dp", "tensor"),
        ),
        check_vma=False,
    )
```

```python
import math
from functools import partial

import jax
import jax.numpy as jnp
from jax import lax
from jax.experimental import pallas as pl
from jax.experimental.pallas import tpu as pltpu
from jax.sharding import PartitionSpec as P

HEAD_DIM = 64
BLOCK = 256
LANES = 128
EPSILON = 1e-06
HIGHEST = lax.Precision.HIGHEST
NEGATIVE = -1e30
F32 = jnp.float32
BF16 = jnp.bfloat16
def combined_all(part, axis, combine):
    gathered = jax.tree.map(lambda a: lax.all_gather(a, axis), part)

    def take(source):
        return jax.tree.map(lambda a: lax.dynamic_index_in_dim(a, source, 0, False), gathered)

    return lax.fori_loop(
        1, lax.axis_size(axis), lambda source, state: combine(state, take(source)), take(0)
    )


def contract_last(left_op, right_op):
    return lax.dot_general(
        left_op, right_op, (((1,), (1,)), ((), ())), preferred_element_type=jnp.float32
    )


def contract_first(left_op, right_op):
    return lax.dot_general(
        left_op, right_op, (((0,), (0,)), ((), ())), preferred_element_type=jnp.float32
    )


def block_terms(q_blk, keys_all, cumul, seg_row, offset, rows_blk):
    positions = jnp.arange(keys_all.shape[0], dtype=jnp.int32)
    q_pos = offset + jnp.arange(rows_blk, dtype=jnp.int32)
    allowed = (seg_row[:, None] == seg_row[None, :]) & (
        q_pos[:, None] // BLOCK >= positions[None, :] // BLOCK
    )
    signs = jnp.where(positions[None, :] <= q_pos[:, None], 1.0, -1.0).astype(jnp.float32)
    raw_blk = jnp.einsum("qhe,khe->hqk", q_blk, keys_all, preferred_element_type=jnp.float32) * (
        1.0 / math.sqrt(HEAD_DIM)
    )
    differ = cumul.T[:, :, None] - cumul.T[:, None, :]
    scores = jnp.where(allowed[None], raw_blk + signs[None] * differ, NEGATIVE)
    return (raw_blk, scores, allowed, signs)


def combine(former, latter):
    return (
        jnp.maximum(former[0], latter[0]),
        former[1] + latter[1],
        former[2] + latter[2],
        former[3] + latter[3],
    )


def general_body(
    layer_in,
    segment_ids,
    norm1_gain,
    w_query,
    w_key,
    w_value,
    w_forget,
    forget_bias,
    w_output,
    norm2_gain,
    w_gate,
    w_up,
    w_down,
    clip_tau,
    out_grad,
):
    gain_one, wq_all, wk_all, wv_all, wf_all, wo_all, gain_two, wg_all, wu_all, wd_all = (
        lax.all_gather(norm1_gain, "dp", axis=0, tiled=True),
        lax.all_gather(w_query, "dp", axis=0, tiled=True),
        lax.all_gather(w_key, "dp", axis=0, tiled=True),
        lax.all_gather(w_value, "dp", axis=0, tiled=True),
        lax.all_gather(w_forget, "dp", axis=0, tiled=True),
        lax.all_gather(w_output, "dp", axis=0, tiled=True),
        lax.all_gather(norm2_gain, "dp", axis=0, tiled=True),
        lax.all_gather(w_gate, "dp", axis=0, tiled=True),
        lax.all_gather(w_up, "dp", axis=0, tiled=True),
        lax.all_gather(w_down, "dp", axis=0, tiled=True),
    )
    gain_one = gain_one.astype(jnp.float32)
    gain_two = gain_two.astype(jnp.float32)
    tok_local = layer_in.shape[0]
    tokens = tok_local * lax.axis_size("tensor")
    heads_loc = forget_bias.shape[0]
    row_start = lax.axis_index("tensor") * tok_local
    seg_row = segment_ids[0]
    factor = 1.0 / math.sqrt(HEAD_DIM)
    rows_full = lax.all_gather(layer_in, "tensor", axis=0, tiled=True).astype(jnp.float32)
    scale_one = lax.rsqrt(jnp.mean(rows_full * rows_full, axis=1, keepdims=True) + EPSILON)
    unit_one = rows_full * scale_one
    normed_one = (unit_one * gain_one).astype(jnp.bfloat16)
    queries = (
        jnp.dot(normed_one, wq_all, preferred_element_type=jnp.float32)
        .astype(jnp.bfloat16)
        .reshape(tokens, heads_loc, HEAD_DIM)
    )
    keys_all = (
        jnp.dot(normed_one, wk_all, preferred_element_type=jnp.float32)
        .astype(jnp.bfloat16)
        .reshape(tokens, heads_loc, HEAD_DIM)
    )
    values_all = (
        jnp.dot(normed_one, wv_all, preferred_element_type=jnp.float32)
        .astype(jnp.bfloat16)
        .reshape(tokens, heads_loc, HEAD_DIM)
    )
    logits = jnp.dot(normed_one, wf_all, preferred_element_type=jnp.float32) + forget_bias
    cumul = jnp.cumsum(jax.nn.log_sigmoid(logits), axis=0)
    rows_blk = min(512, tokens)
    blocks = tokens // rows_blk
    numbers = jnp.arange(blocks, dtype=jnp.int32)

    def forward_block(number):
        offset = number * rows_blk
        raw_blk, scores, allowed, signs = block_terms(
            queries, keys_all, cumul, seg_row, offset, rows_blk
        )
        top_blk = jnp.max(jnp.where(allowed[None], raw_blk, NEGATIVE), axis=(1, 2))
        row_peak = jnp.max(scores, axis=2, keepdims=True)
        expo_blk = jnp.exp(scores - row_peak)
        totals = jnp.sum(expo_blk, axis=2, keepdims=True)
        weights = (expo_blk / totals).astype(jnp.bfloat16)
        mixed_out = jnp.einsum(
            "hqk,khe->qhe", weights, values_all, preferred_element_type=jnp.float32
        ).astype(jnp.bfloat16)
        return (mixed_out, (row_peak + jnp.log(totals))[:, :, 0], top_blk)

    mixed_out, log_sums, top_blk = lax.map(forward_block, numbers)
    mixed_flat = mixed_out.reshape(tokens, heads_loc * HEAD_DIM)
    maxima = jnp.max(top_blk, axis=0)
    attn_part = contract_last(mixed_flat, wo_all)
    resid_full = rows_full + lax.psum(attn_part.astype(jnp.bfloat16), "tensor").astype(jnp.float32)
    scale_full = lax.rsqrt(jnp.mean(resid_full * resid_full, axis=1, keepdims=True) + EPSILON)
    normed_two = (resid_full * scale_full * gain_two).astype(jnp.bfloat16)
    resid_part = lax.dynamic_slice_in_dim(resid_full, row_start, tok_local, 0)
    scale_two = lax.dynamic_slice_in_dim(scale_full, row_start, tok_local, 0)
    gate_pre = jnp.dot(normed_two, wg_all, preferred_element_type=jnp.float32)
    up_pre = jnp.dot(normed_two, wu_all, preferred_element_type=jnp.float32)
    gate_sig = jax.nn.sigmoid(gate_pre)
    gate_act = gate_pre * gate_sig
    hidden = (gate_act * up_pre).astype(jnp.bfloat16)
    ffn_part = lax.psum_scatter(
        contract_last(hidden, wd_all).astype(jnp.bfloat16),
        "tensor",
        scatter_dimension=0,
        tiled=True,
    ).astype(jnp.float32)
    layer_out = (resid_part + ffn_part).astype(jnp.bfloat16)
    grad_full = lax.all_gather(out_grad, "tensor", axis=0, tiled=True)
    grad_hidden = jnp.dot(grad_full, wd_all, preferred_element_type=jnp.float32)
    grad_gate = (grad_hidden * up_pre * gate_sig * (1.0 + gate_pre * (1.0 - gate_sig))).astype(
        jnp.bfloat16
    )
    grad_up = (grad_hidden * gate_act).astype(jnp.bfloat16)
    g_down = contract_first(grad_full, hidden)
    g_gate = contract_first(normed_two, grad_gate)
    g_up = contract_first(normed_two, grad_up)
    grad_normed = contract_last(grad_gate, wg_all) + contract_last(grad_up, wu_all)
    grad_two = lax.psum_scatter(
        grad_normed.astype(jnp.bfloat16), "tensor", scatter_dimension=0, tiled=True
    ).astype(jnp.float32)
    unit_two = resid_part * scale_two
    inner_two = jnp.mean(unit_two * gain_two * grad_two, axis=1, keepdims=True)
    norm2_part = jnp.sum(grad_two * unit_two, axis=0)
    grad_resid = out_grad.astype(jnp.float32) + scale_two * (
        gain_two * grad_two - unit_two * inner_two
    )
    grad_attn = lax.all_gather(grad_resid.astype(jnp.bfloat16), "tensor", axis=0, tiled=True)
    g_output = contract_first(grad_attn, mixed_flat)
    grad_mixed = jnp.dot(grad_attn, wo_all, preferred_element_type=jnp.float32).astype(jnp.bfloat16)
    grad_mixed = grad_mixed.reshape(blocks, rows_blk, heads_loc, HEAD_DIM)

    def backward_block(carried, block_in):
        key_acc, value_acc, column_acc = carried
        number, log_blk, grad_blk = block_in
        offset = number * rows_blk
        raw_blk, scores, allowed, signs = block_terms(
            queries, keys_all, cumul, seg_row, offset, rows_blk
        )
        prob_blk = jnp.exp(scores - log_blk[:, :, None])
        weights = prob_blk.astype(jnp.bfloat16)
        grad_prob = jnp.einsum(
            "qhe,khe->hqk", grad_blk, values_all, preferred_element_type=jnp.float32
        )
        inner = jnp.sum(prob_blk * grad_prob, axis=2, keepdims=True)
        grad_scores = (prob_blk * (grad_prob - inner)).astype(jnp.bfloat16)
        value_acc = value_acc + jnp.einsum(
            "hqk,qhe->khe", weights, grad_blk, preferred_element_type=jnp.float32
        )
        key_acc = key_acc + jnp.einsum(
            "hqk,qhe->khe", grad_scores, queries, preferred_element_type=jnp.float32
        )
        grad_query = (
            jnp.einsum("hqk,khe->qhe", grad_scores, keys_all, preferred_element_type=jnp.float32)
            * factor
        ).astype(jnp.bfloat16)
        signed = grad_scores.astype(jnp.float32) * signs[None]
        column_acc = column_acc - jnp.sum(signed, axis=1).T
        return ((key_acc, value_acc, column_acc), (grad_query, jnp.sum(signed, axis=2).T))

    start_acc = (
        jnp.zeros((tokens, heads_loc, HEAD_DIM), jnp.float32),
        jnp.zeros((tokens, heads_loc, HEAD_DIM), jnp.float32),
        jnp.zeros((tokens, heads_loc), jnp.float32),
    )
    (key_acc, value_acc, column_acc), (grad_query, row_parts) = lax.scan(
        backward_block, start_acc, (numbers, log_sums, grad_mixed)
    )
    grad_q = grad_query.reshape(tokens, heads_loc * HEAD_DIM)
    grad_k = (key_acc * factor).astype(jnp.bfloat16).reshape(tokens, heads_loc * HEAD_DIM)
    grad_v = value_acc.astype(jnp.bfloat16).reshape(tokens, heads_loc * HEAD_DIM)
    grad_cum = row_parts.reshape(tokens, heads_loc) + column_acc
    grad_logs = jnp.cumsum(grad_cum[::-1], axis=0)[::-1]
    grad_logit = grad_logs * jax.nn.sigmoid(-logits)
    g_bias = jnp.sum(grad_logit, axis=0)
    g_forget = jnp.einsum(
        "td,th->dh", normed_one, grad_logit, precision=HIGHEST, preferred_element_type=jnp.float32
    )
    g_query = contract_first(normed_one, grad_q)
    g_key = contract_first(normed_one, grad_k)
    g_value = contract_first(normed_one, grad_v)
    grad_one = (
        contract_last(grad_q, wq_all)
        + contract_last(grad_k, wk_all)
        + contract_last(grad_v, wv_all)
    )
    grad_one = grad_one + jnp.einsum(
        "th,dh->td", grad_logit, wf_all, precision=HIGHEST, preferred_element_type=jnp.float32
    )
    weighted = gain_one * grad_one
    grad_rows_one = scale_one * (
        weighted - unit_one * jnp.mean(unit_one * weighted, axis=1, keepdims=True)
    )
    norm1_part = jnp.sum(grad_one * unit_one, axis=0)
    grad_input, g_norm1_part, g_norm2_part = (
        lax.psum_scatter(
            grad_rows_one.astype(jnp.bfloat16), "tensor", scatter_dimension=0, tiled=True
        ).astype(jnp.float32),
        lax.psum_scatter(
            norm1_part.astype(jnp.bfloat16), "tensor", scatter_dimension=0, tiled=True
        ).astype(jnp.float32),
        lax.psum_scatter(
            norm2_part.astype(jnp.bfloat16), "tensor", scatter_dimension=0, tiled=True
        ).astype(jnp.float32),
    )
    x_grad = (grad_resid + grad_input).astype(jnp.bfloat16)
    g_query, g_key, g_value, g_forget, g_output, g_gate, g_up, g_down = (
        lax.psum_scatter(
            g_query.astype(jnp.bfloat16), "dp", scatter_dimension=0, tiled=True
        ).astype(jnp.float32),
        lax.psum_scatter(g_key.astype(jnp.bfloat16), "dp", scatter_dimension=0, tiled=True).astype(
            jnp.float32
        ),
        lax.psum_scatter(
            g_value.astype(jnp.bfloat16), "dp", scatter_dimension=0, tiled=True
        ).astype(jnp.float32),
        lax.psum_scatter(
            g_forget.astype(jnp.bfloat16), "dp", scatter_dimension=0, tiled=True
        ).astype(jnp.float32),
        lax.psum_scatter(
            g_output.astype(jnp.bfloat16), "dp", scatter_dimension=0, tiled=True
        ).astype(jnp.float32),
        lax.psum_scatter(g_gate.astype(jnp.bfloat16), "dp", scatter_dimension=0, tiled=True).astype(
            jnp.float32
        ),
        lax.psum_scatter(g_up.astype(jnp.bfloat16), "dp", scatter_dimension=0, tiled=True).astype(
            jnp.float32
        ),
        lax.psum_scatter(g_down.astype(jnp.bfloat16), "dp", scatter_dimension=0, tiled=True).astype(
            jnp.float32
        ),
    )
    maxima, g_bias, g_norm1, g_norm2 = combined_all(
        (maxima, g_bias, g_norm1_part, g_norm2_part), "dp", combine
    )
    clip_factor = jnp.minimum(1.0, clip_tau / jnp.maximum(maxima, 1.0))
    columns = jnp.repeat(jnp.sqrt(clip_factor), HEAD_DIM)
    clipped_query = (w_query.astype(jnp.float32) * columns[None, :]).astype(jnp.bfloat16)
    clipped_key = (w_key.astype(jnp.float32) * columns[None, :]).astype(jnp.bfloat16)
    return (
        layer_out,
        x_grad,
        g_norm1,
        g_query,
        g_key,
        g_value,
        g_forget,
        g_bias,
        g_output,
        g_norm2,
        g_gate,
        g_up,
        g_down,
        clip_factor,
        clipped_query,
        clipped_key,
    )


def dot_nt(left, right):
    return lax.dot_general(left, right, (((1,), (1,)), ((), ())), preferred_element_type=F32)


def dot_nn(left, right):
    return lax.dot_general(left, right, (((1,), (0,)), ((), ())), preferred_element_type=F32)


def dot_tn(left, right):
    return lax.dot_general(left, right, (((0,), (0,)), ((), ())), preferred_element_type=F32)


def attend_kernel(y_ref, qkv_ref, aux_ref, *refs):
    o_ref, inv_ref, exp_ref, top_ref = refs[-4:]
    y = y_ref[0]
    starts = (pl.multiple_of(y * BLOCK, BLOCK), pl.multiple_of((1 - y) * BLOCK, BLOCK))
    lane = lax.broadcasted_iota(jnp.int32, (1, LANES), 1)
    first = lane < HEAD_DIM
    aux = [aux_ref[0, :, pl.ds(start, BLOCK)] for start in starts]
    aux_col = [a.T for a in aux]
    q_blk = [qkv_ref[pl.ds(s, BLOCK), 0:LANES] * 0.125 for s in starts]
    k_blk = [qkv_ref[pl.ds(s, BLOCK), LANES : 2 * LANES] for s in starts]
    v_blk = [qkv_ref[pl.ds(s, BLOCK), 2 * LANES : 3 * LANES] for s in starts]
    same = {}
    for i, j in ((0, 0), (1, 0), (1, 1)):
        same[i, j] = aux_col[i][:, 2:3] == aux[j][2:3, :]
    tops = []
    results = [[], []]
    for head in range(2):
        mine = first if head == 0 else jnp.logical_not(first)
        top = None
        v_ext = [jnp.where(mine, v, jnp.ones_like(v)) for v in v_blk]
        k_head = [jnp.where(mine, k, jnp.zeros_like(k)) for k in k_blk]
        for i in range(2):
            scores = []
            for j in range(i + 1):
                raw = dot_nt(q_blk[i], k_head[j])
                seen = jnp.where(same[i, j], raw, NEGATIVE)
                high = jnp.max(seen, axis=0, keepdims=True)
                top = high if top is None else jnp.maximum(top, high)
                differ = aux_col[i][:, head : head + 1] - aux[j][head : head + 1, :]
                scores.append(seen - jnp.abs(differ))
            peak = jnp.max(scores[0], axis=1, keepdims=True)
            if i == 1:
                peak = jnp.maximum(peak, jnp.max(scores[1], axis=1, keepdims=True))
            acc = None
            for j in range(i + 1):
                weights = jnp.exp(scores[j] - peak).astype(BF16)
                exp_ref[0, 0, head, :, (i + j) * BLOCK : (i + j + 1) * BLOCK] = weights
                part = dot_nn(weights, v_ext[j])
                acc = part if acc is None else acc + part
            results[i].append(acc)
        tops.append(jnp.maximum(top[:, :LANES], top[:, LANES:]))
    for i in range(2):
        one, two = results[i]
        total = pltpu.roll(jnp.where(first, two, one), HEAD_DIM, 1)
        inverse = 1.0 / total
        inv_ref[pl.ds(starts[i], BLOCK), :] = inverse
        o_ref[pl.ds(starts[i], BLOCK), :] = (jnp.where(first, one, two) * inverse).astype(BF16)
    row = lax.broadcasted_iota(jnp.int32, (8, LANES), 0)
    top_ref[0, 0] = jnp.where(row == 0, tops[0], tops[1])


def attend(y_index, qkv, aux, packs, pairs, pack, kept=()):
    rows = qkv.shape[0] // packs
    wide = 3 * LANES
    grid_spec = pltpu.PrefetchScalarGridSpec(
        num_scalar_prefetch=1,
        grid=(pairs,),
        in_specs=[
            pl.BlockSpec((rows, wide), lambda h, y: (pack, h)),
            pl.BlockSpec((1, 8, rows), lambda h, y: (h, 0, pack)),
        ]
        + [pl.BlockSpec(memory_space=pl.ANY) for _ in kept],
        out_specs=[
            pl.BlockSpec((rows, LANES), lambda h, y: (0, h)),
            pl.BlockSpec((rows, LANES), lambda h, y: (pack, h)),
            pl.BlockSpec((1, 1, 2, BLOCK, 3 * BLOCK), lambda h, y: (pack, h, 0, 0, 0)),
            pl.BlockSpec((1, 1, 8, LANES), lambda h, y: (0, h, 0, 0)),
        ],
    )
    return pl.pallas_call(
        attend_kernel,
        grid_spec=grid_spec,
        out_shape=(
            jax.ShapeDtypeStruct((rows, pairs * LANES), BF16),
            jax.ShapeDtypeStruct((packs * rows, pairs * LANES), F32),
            jax.ShapeDtypeStruct((packs, pairs, 2, BLOCK, 3 * BLOCK), BF16),
            jax.ShapeDtypeStruct((1, pairs, 8, LANES), F32),
        ),
        input_output_aliases={3: 1, 4: 2} if kept else {},
        cost_estimate=pl.CostEstimate(
            flops=pairs * 2 * 6 * BLOCK * BLOCK * LANES * 2,
            bytes_accessed=10_000_000,
            transcendentals=pairs * 2 * 3 * BLOCK * BLOCK,
        ),
        name="attend",
    )(y_index, qkv, aux, *kept)


def attend_back_kernel(
    pairs, y_ref, qkv_ref, do_ref, inv_ref, exp_ref, aux_ref, dqkv_ref, split_ref
):
    y = y_ref[0]
    starts = (pl.multiple_of(y * BLOCK, BLOCK), pl.multiple_of((1 - y) * BLOCK, BLOCK))
    lane = lax.broadcasted_iota(jnp.int32, (1, LANES), 1)
    first = lane < HEAD_DIM
    ones = jnp.ones((8, BLOCK), BF16)
    lower = lax.broadcasted_iota(jnp.int32, (BLOCK, BLOCK), 1) <= lax.broadcasted_iota(
        jnp.int32, (BLOCK, BLOCK), 0
    )
    q_blk = [qkv_ref[pl.ds(s, BLOCK), 0:LANES] * 0.125 for s in starts]
    k_blk = [qkv_ref[pl.ds(s, BLOCK), LANES : 2 * LANES] for s in starts]
    v_blk = [qkv_ref[pl.ds(s, BLOCK), 2 * LANES : 3 * LANES] for s in starts]
    inv_blk = [inv_ref[pl.ds(s, BLOCK), :] for s in starts]
    do_blk = [
        (do_ref[pl.ds(s, BLOCK), :].astype(F32) * inv).astype(BF16)
        for s, inv in zip(starts, inv_blk)
    ]
    dq, dk, dv, dc = ([], []), ([], []), ([], []), ([], [])
    for head in range(2):
        mine = first if head == 0 else jnp.logical_not(first)
        v_head = [jnp.where(mine, v, jnp.zeros_like(v)) for v in v_blk]
        dk_acc, dv_acc, row_acc, col_acc = [None] * 2, [None] * 2, [None] * 2, [None] * 2
        for i in range(2):
            expos, probs, inner = [], [], None
            inv_col = inv_blk[i][:, head * HEAD_DIM : head * HEAD_DIM + 1]
            for j in range(i + 1):
                expo = exp_ref[0, 0, head, :, (i + j) * BLOCK : (i + j + 1) * BLOCK]
                grad_prob = dot_nt(do_blk[i], v_head[j])
                wide = expo.astype(F32)
                part = jnp.sum(wide * grad_prob, axis=1, keepdims=True)
                inner = part if inner is None else inner + part
                expos.append((expo, wide))
                probs.append(grad_prob)
            inner = inner * inv_col
            dq_acc = None
            for j in range(i + 1):
                expo, wide = expos[j]
                grad_score = wide * (probs[j] - inner)
                low = grad_score.astype(BF16)
                if i == j:
                    signed = jnp.where(lower, low, -low)
                else:
                    signed = low
                part = dot_nn(low, k_blk[j])
                dq_acc = part if dq_acc is None else dq_acc + part
                part = dot_tn(low, q_blk[i])
                dk_acc[j] = part if dk_acc[j] is None else dk_acc[j] + part
                part = dot_tn(expo, do_blk[i])
                dv_acc[j] = part if dv_acc[j] is None else dv_acc[j] + part
                part = dot_nt(ones, signed)
                row_acc[i] = part if row_acc[i] is None else row_acc[i] + part
                part = dot_nn(ones, signed)
                col_acc[j] = part if col_acc[j] is None else col_acc[j] + part
            dq[i].append(dq_acc)
        for j in range(2):
            dk[j].append(dk_acc[j])
            dv[j].append(dv_acc[j])
            dc[j].append(row_acc[j] - col_acc[j])
    for i in range(2):
        rows = pl.ds(starts[i], BLOCK)
        dqkv_ref[rows, 0:LANES] = (jnp.where(first, *dq[i]) * 0.125).astype(BF16)
        dqkv_ref[rows, LANES : 2 * LANES] = jnp.where(first, *dk[i]).astype(BF16)
        dqkv_ref[rows, 2 * LANES : 3 * LANES] = jnp.where(first, *dv[i]).astype(BF16)

    row = lax.broadcasted_iota(jnp.int32, (8, BLOCK), 0)
    until = jnp.where(lower, 1.0, 0.0).astype(BF16)
    d_cum = [jnp.where(row == 0, *dc[i]) for i in range(2)]
    ends = jnp.sum(d_cum[1], axis=1, keepdims=True)
    pair = pl.program_id(1)
    spot = lax.broadcasted_iota(jnp.int32, (8, LANES), 0)
    place = jnp.where(spot < 2, 2 * pair + spot, 2 * pairs + 2 * pair + spot - 2)
    hit = (lax.broadcasted_iota(jnp.int32, (8, LANES), 1) == place) & (spot < 4)
    hit = jnp.where(hit, 1.0, 0.0).astype(F32)

    @pl.when(pair == 0)
    def _():
        split_ref[...] = jnp.zeros_like(split_ref)

    for i in range(2):
        rows = pl.ds(starts[i], BLOCK)
        high = d_cum[i].astype(BF16).astype(F32)
        rest = d_cum[i] - high
        middle = rest.astype(BF16).astype(F32)
        low = pltpu.roll(rest - middle, 4, 0)
        parts = jnp.where(row < 4, pltpu.roll(middle, 2, 0), jnp.where(row < 6, low, 0.0))
        parts = jnp.where(row < 2, high, parts).astype(BF16)
        sums = dot_nn(parts, until)
        back = sums + pltpu.roll(sums, 6, 0) + pltpu.roll(sums, 4, 0)
        if i == 0:
            back = back + ends
        logit = pltpu.roll(aux_ref[0, :, rows], 4, 0)
        grad = back * jax.nn.sigmoid(-logit)
        high = grad.astype(BF16).astype(F32)
        rest = pltpu.roll((grad - high).astype(BF16).astype(F32), 2, 0)
        both = jnp.where(row < 2, high, jnp.where(row < 4, rest, 0.0))
        old = split_ref[rows, :].astype(F32)
        split_ref[rows, :] = (old + dot_tn(both, hit)).astype(BF16)


def attend_back(y_index, qkv, d_out, inverse, expos, aux, packs, pairs):
    rows = qkv.shape[0] // packs
    wide = 3 * LANES
    grid_spec = pltpu.PrefetchScalarGridSpec(
        num_scalar_prefetch=1,
        grid=(packs, pairs),
        in_specs=[
            pl.BlockSpec((rows, wide), lambda p, h, y: (p, h)),
            pl.BlockSpec((rows, LANES), lambda p, h, y: (p, h)),
            pl.BlockSpec((rows, LANES), lambda p, h, y: (p, h)),
            pl.BlockSpec((1, 1, 2, BLOCK, 3 * BLOCK), lambda p, h, y: (p, h, 0, 0, 0)),
            pl.BlockSpec((1, 8, rows), lambda p, h, y: (h, 0, p)),
        ],
        out_specs=[
            pl.BlockSpec((rows, wide), lambda p, h, y: (p, h)),
            pl.BlockSpec((rows, LANES), lambda p, h, y: (p, 0)),
        ],
    )
    return pl.pallas_call(
        partial(attend_back_kernel, pairs),
        grid_spec=grid_spec,
        out_shape=(
            jax.ShapeDtypeStruct((packs * rows, pairs * wide), BF16),
            jax.ShapeDtypeStruct((packs * rows, LANES), BF16),
        ),
        cost_estimate=pl.CostEstimate(
            flops=packs * pairs * 2 * 18 * BLOCK * BLOCK * LANES * 2,
            bytes_accessed=20_000_000,
            transcendentals=0,
        ),
        name="attend_back",
    )(y_index, qkv, d_out, inverse, expos, aux)


def assemble_kernel(core_ref, low_ref, got_low_ref, high_ref, got_high_ref, *outs):
    core = core_ref[0]
    rows = outs[0].shape[0]
    own = pl.ds(pl.multiple_of(core * rows, 8), rows)
    count = outs[0].shape[1] // (2 * LANES)
    middle = low_ref.shape[1]
    spots = [[3 * p + which for p in range(count)] for which in range(3)]
    spots.append([3 * count + 1 + p for p in range(count)])
    for out, chosen in zip(outs, spots):
        for p, spot in enumerate(chosen):
            start = spot * LANES
            mine_ref, got_ref = low_ref, got_low_ref
            if start >= middle:
                start -= middle
                mine_ref, got_ref = high_ref, got_high_ref
            lanes = slice(start, start + LANES)
            mine, got = mine_ref[own, lanes], got_ref[:, lanes].astype(F32)
            left = slice(p * LANES, (p + 1) * LANES)
            right = slice((count + p) * LANES, (count + p + 1) * LANES)
            out[:, left] = jnp.where(core == 0, mine, got)
            out[:, right] = jnp.where(core == 0, got, mine)


def assemble(core, low, got_low, high, got_high, pairs):
    shape = jax.ShapeDtypeStruct((got_low.shape[0], 2 * pairs * LANES), F32)
    spec = pl.BlockSpec(memory_space=pltpu.VMEM)
    return pl.pallas_call(
        assemble_kernel,
        in_specs=[pl.BlockSpec(memory_space=pltpu.SMEM)] + [spec] * 4,
        out_specs=[spec] * 4,
        out_shape=[shape] * 4,
        name="assemble",
    )(core.astype(jnp.int32).reshape(1), low, got_low, high, got_high)


class Gathering:
    def __init__(self, at, shard):
        self.at, self.step, self.half = at, 1, at.depth
        self.whole = None
        self.waiting = [(shard, 0, 0)]
        self.send(shard, shard)

    def store(self, *others):
        for part, step, side in self.waiting:
            if others:
                part = after(part, *others)
            if self.whole is None:
                self.whole = jnp.zeros((2 * self.half,) + part.shape, part.dtype)
                if others:
                    self.whole = after(self.whole, *others)
            start = (self.at.block_of(step), side, 0, 0)
            self.whole = lax.dynamic_update_slice(self.whole, part[None], start)
        self.waiting = []

    def send(self, up, down):
        if self.step == self.half:
            up, down = up[:1], down[1:]
        self.came = (self.at.ring(up, 1), self.at.ring(down, -1))

    def take(self, *others):
        up, down = after_all(self.came, *others)
        side = 1 if self.step == self.half else 0
        self.waiting += [(up, -self.step, 0), (down, self.step, side)]
        return up, down

    def advance(self, *others):
        up, down = self.take(*others)
        self.step += 1
        self.send(up, down)
        return up, down

    def finish(self, *others):
        self.take(*others)
        self.store()
        return self.whole.reshape(-1, self.whole.shape[-1])


class Reduction:
    def __init__(self, at, grad, *others):
        self.at, self.step, self.half = at, 1, at.depth
        count = 2 * at.depth
        self.blocks = grad.reshape(count, 2, grad.shape[0] // (2 * count), grad.shape[1])
        far = self.own(self.half)
        self.sent = after_all((far[:1], far[1:]), *others) if others else (far[:1], far[1:])
        self.send()

    def own(self, step):
        start = (self.at.block_of(step), 0, 0, 0)
        return lax.dynamic_slice(self.blocks, start, (1,) + self.blocks.shape[1:])[0]

    def send(self):
        self.came = (self.at.ring(self.sent[0], 1), self.at.ring(self.sent[1], -1))

    def advance(self, *others):
        up, down = after_all(self.came, *others)
        ahead, behind = self.own(self.half - self.step), self.own(self.step - self.half)
        if self.step == 1:
            first = (ahead[:1].astype(F32) + up.astype(F32)).astype(BF16)
            second = (behind[1:].astype(F32) + down.astype(F32)).astype(BF16)
            up = jnp.concatenate([first, ahead[1:]], axis=0)
            down = jnp.concatenate([behind[:1], second], axis=0)
        else:
            up = (ahead.astype(F32) + up.astype(F32)).astype(BF16)
            down = (behind.astype(F32) + down.astype(F32)).astype(BF16)
        self.sent = (up, down)
        self.step += 1
        self.send()
        return up, down

    def finish(self, *others):
        up, down = after_all(self.came, *others)
        total = self.own(0).astype(F32) + up.astype(F32) + down.astype(F32)
        return total.reshape(-1, total.shape[-1])


class Place:
    def __init__(self):
        self.dp = lax.axis_size("dp")
        self.depth = self.dp // 4
        index = lax.axis_index("dp")
        self.core = index % 2
        self.x = (index // 2) % 2
        self.z = index // 4
        self.y = lax.axis_index("tensor")

    def swap_core(self, value):
        return lax.ppermute(value, "dp", [(i, i ^ 1) for i in range(self.dp)])

    def swap_y(self, value):
        return lax.ppermute(value, "tensor", [(0, 1), (1, 0)])

    def ring(self, value, step):
        spots = [4 * z for z in range(self.depth)]
        spots += [4 * z + 2 for z in reversed(range(self.depth))]
        count = len(spots)
        pairs = [
            (spots[r] + core, spots[(r + step) % count] + core)
            for r in range(count)
            for core in (0, 1)
        ]
        return lax.ppermute(value, "dp", pairs)

    def block_of(self, step):
        count = 2 * self.depth
        spot = (jnp.where(self.x == 0, self.z, count - 1 - self.z) + step + count) % count
        return jnp.where(spot < self.depth, 2 * spot, 2 * (count - 1 - spot) + 1)

    def sum_plane(self, value, rings, combine):
        step = 2
        rings = list(rings)
        while step < self.dp:
            value = combine(
                value, lax.ppermute(value, "dp", [(i, i ^ step) for i in range(self.dp)])
            )
            if rings:
                value = after(value, *rings.pop(0).advance(value))
            step *= 2
        return value

    def by_core(self, mine, other, axis):
        return jnp.where(
            self.core == 0,
            jnp.concatenate([mine, other], axis=axis),
            jnp.concatenate([other, mine], axis=axis),
        )

    def core_columns(self, weights):
        half = [w.shape[1] // 2 for w in weights]
        keep = [
            lax.dynamic_slice_in_dim(w, self.core * h, h, 1) for w, h in zip(weights, half)
        ]
        give = [
            lax.dynamic_slice_in_dim(w, (1 - self.core) * h, h, 1) for w, h in zip(weights, half)
        ]
        return keep, give

    def finish_grad(self, own):
        rows = own.shape[0] // 2
        keep = lax.dynamic_slice_in_dim(own, self.core * rows, rows, 0)
        return keep, self.swap_core(self.theirs(own)).astype(F32)

    def theirs(self, own):
        rows = own.shape[0] // 2
        return lax.dynamic_slice_in_dim(own, (1 - self.core) * rows, rows, 0).astype(BF16)

    def join(self, rows, near):
        both = jnp.concatenate([rows, near], axis=0)
        return jnp.concatenate([both, self.swap_core(both)], axis=0)

    def meet_core(self, left, right, dot):
        half = left.shape[0] // 2
        given = dot(left[half:], right).astype(BF16)
        got = self.swap_core(given)
        part = dot(after(left, given)[:half], right)
        return part, got


def after(value, *others):
    return lax.optimization_barrier((value,) + others)[0]


def after_all(values, *others):
    return lax.optimization_barrier(tuple(values) + others)[: len(values)]


def interleave(parts):
    starts = range(0, parts[0].shape[1], LANES)
    return jnp.concatenate([p[:, s : s + LANES] for s in starts for p in parts], axis=1)


def split_low(value):
    high = value.astype(BF16)
    return high, (value - high.astype(F32)).astype(BF16)


def paired_body(
    layer_in,
    segment_ids,
    norm1_gain,
    w_query,
    w_key,
    w_value,
    w_forget,
    forget_bias,
    w_output,
    norm2_gain,
    w_gate,
    w_up,
    w_down,
    clip_tau,
    out_grad,
):
    at = Place()
    rows_loc = layer_in.shape[0]
    pack = 2 * rows_loc
    width = layer_in.shape[1]
    heads = forget_bias.shape[0] // 2
    pairs = heads // 2
    y_index = at.y.astype(jnp.int32).reshape(1)
    d_rows = norm1_gain.shape[0]

    units = w_gate.shape[1] // 2
    keep, give = at.core_columns([w_query, w_key, w_value, w_output, w_forget])
    gains = jnp.stack([norm1_gain, norm2_gain], axis=1)
    pad = jnp.zeros((d_rows, LANES - 2 * heads - 2), BF16)

    def first_part(part):
        return jnp.concatenate(
            [interleave(part[:3]), part[4], part[4], gains, pad, part[3]], axis=1
        )

    attn_shard = at.by_core(first_part(keep)[None], at.swap_core(first_part(give))[None], 0)
    rows_near = at.swap_y(layer_in)
    qkv_cols = 3 * heads * HEAD_DIM
    in_cols = qkv_cols + LANES
    attn_ring = Gathering(at, attn_shard)
    keep, give = at.core_columns(after_all((w_gate, w_up, w_down), attn_shard))
    keep, give = jnp.concatenate(keep, axis=1), jnp.concatenate(give, axis=1)
    early = attn_ring.advance(keep, give)
    ffn_shard = at.by_core(after(keep, *early)[None], at.swap_core(after(give, *early))[None], 0)
    moved = attn_ring.advance(rows_near)
    attn_ring.store()
    grad_near = at.swap_y(after(out_grad, *moved))
    attn_ring.advance(ffn_shard)
    attn_ring.store()
    ffn_ring = Gathering(at, after(ffn_shard, *attn_ring.came))
    attn_all = attn_ring.finish()
    w_in, wo_all = attn_all[:, :in_cols], attn_all[:, in_cols:]
    rows_all = at.join(layer_in, rows_near)
    grad_rows = at.join(out_grad, grad_near)
    w_qkv = w_in[:, :qkv_cols]
    small = w_in[:, qkv_cols:].T
    forget_t = small[:heads]
    gain_one = small[2 * heads : 2 * heads + 1].astype(F32)
    gain_two = small[2 * heads + 1 : 2 * heads + 2].astype(F32)

    def first_norm(rows):
        rows = rows.astype(F32)
        return rows, lax.rsqrt(jnp.mean(rows * rows, axis=1, keepdims=True) + EPSILON)

    x_all, scale_all = first_norm(rows_all)
    normed_one = (x_all * scale_all * gain_one).astype(BF16)
    x_own, scale_one = first_norm(layer_in)
    unit_one = x_own * scale_one
    qkv = dot_nn(normed_one, w_qkv).astype(BF16)

    bias = lax.dynamic_slice_in_dim(forget_bias, at.core * heads, heads, 0)
    logits = dot_nt(forget_t, normed_one) + bias[:, None]
    logs = jax.nn.log_sigmoid(logits).reshape(heads, 2, 2, rows_loc)
    steps = jnp.arange(rows_loc, dtype=jnp.int32)
    upper = (steps[:, None] <= steps[None, :]).astype(F32)
    sums = jnp.einsum("hpbt,ts->hpbs", logs, upper, precision=HIGHEST)
    total = sums[..., -1:]
    later = at.y.astype(F32)
    cumul = jnp.stack(
        [sums[:, :, 0] + later * total[:, :, 1], sums[:, :, 1] + (1.0 - later) * total[:, :, 0]],
        axis=2,
    ).reshape(heads, 2 * pack)
    seg_own = after(segment_ids, *early)[0].reshape(2, rows_loc)
    seg_own = jnp.where(at.y == 0, seg_own, seg_own[::-1]).reshape(1, pack)
    seg_both = jnp.concatenate([seg_own, at.swap_core(seg_own)], axis=1).astype(F32)
    aux = jnp.concatenate(
        [
            cumul.reshape(pairs, 2, 2 * pack),
            jnp.broadcast_to(seg_both[None], (pairs, 2, 2 * pack)),
            logits.reshape(pairs, 2, 2 * pack),
            jnp.zeros((pairs, 2, 2 * pack), F32),
        ],
        axis=1,
    )
    aux = after(aux, grad_near)
    mixed_other, inverse, expos, tops_other = attend(y_index, qkv, aux, 2, pairs, 1)
    moved = ffn_ring.advance(mixed_other)

    given = dot_nt(after(mixed_other, *moved), wo_all).astype(BF16)
    got = at.swap_core(given)
    mixed_own, inverse, expos, tops = attend(
        y_index, after(qkv, given), aux, 2, pairs, 0, (inverse, expos)
    )
    tops = jnp.concatenate([tops, tops_other], axis=0)
    maxima = jnp.max(tops[:, :, :2], axis=(0, 3)).reshape(heads)
    mixed = jnp.concatenate([mixed_own, mixed_other], axis=0)
    mine = dot_nt(mixed_own, wo_all) + after(got, mixed_own).astype(F32)
    given = mine[rows_loc:].astype(BF16)
    got = at.swap_y(given)
    ffn_ring.store(given)
    moved = ffn_ring.advance(given)
    (got,) = after_all((got,), *moved)
    resid = x_own + (mine[:rows_loc] + got.astype(F32))
    scale_two = lax.rsqrt(jnp.mean(resid * resid, axis=1, keepdims=True) + EPSILON)
    unit_two = resid * scale_two
    normed_own = (unit_two * gain_two).astype(BF16)
    near = at.swap_y(normed_own)
    ffn_ring.store(normed_own)
    moved = ffn_ring.advance(normed_own)
    (near,) = after_all((near,), maxima, *moved)
    normed_two = at.join(normed_own, near)
    ffn_ring.store(near)
    ffn_all = ffn_ring.finish()
    gu_all, down_all = ffn_all[:, : 2 * units], ffn_all[:, 2 * units :]

    gate_up = dot_nn(normed_two, gu_all)
    gate_pre, up_pre = gate_up[:, :units], gate_up[:, units:]
    gate_sig = jax.nn.sigmoid(gate_pre)
    gate_act = gate_pre * gate_sig
    hidden = (gate_act * up_pre).astype(BF16)
    grad_hidden = dot_nn(grad_rows, down_all)
    grad_gate = (grad_hidden * up_pre * gate_sig * (1.0 + gate_pre * (1.0 - gate_sig))).astype(BF16)
    grad_up = (grad_hidden * gate_act).astype(BF16)
    grad_gu = jnp.concatenate([grad_gate, grad_up], axis=1)

    down_sum = Reduction(at, dot_tn(grad_rows, hidden).astype(BF16))
    part, got = at.meet_core(after(grad_gu, *down_sum.sent), gu_all, dot_nt)
    mine = part + after(got, part).astype(F32)
    given = mine[rows_loc:].astype(BF16)
    got = at.swap_y(given)
    gu_sum = Reduction(at, dot_tn(normed_two, after(grad_gu, given)).astype(BF16))
    moved = down_sum.advance(gu_sum.blocks)

    (got,) = after_all((got,), *moved)
    grad_two = mine[:rows_loc] + got.astype(F32)
    weighted = gain_two * grad_two
    inner_two = jnp.mean(unit_two * weighted, axis=1, keepdims=True)
    norm2_part = jnp.sum(grad_two * unit_two, axis=0)
    grad_resid = out_grad.astype(F32) + scale_two * (weighted - unit_two * inner_two)
    grad_own = grad_resid.astype(BF16)
    near = at.swap_y(grad_own)
    moved = gu_sum.advance(grad_own)
    out_given = dot_nt(after(hidden, *moved)[pack:], down_all).astype(BF16)
    moved = down_sum.advance(out_given)
    out_part = dot_nt(after(hidden, *moved)[:pack], down_all)
    moved = gu_sum.advance(out_part)
    (near,) = after_all((near,), *moved)
    grad_attn = at.join(grad_own, near)

    out_got = at.swap_core(after(out_given, grad_attn))
    grad_mixed = dot_nn(grad_attn, wo_all).astype(BF16)
    out_own = out_part + after(out_got, grad_mixed).astype(F32)
    out_given = out_own[rows_loc:].astype(BF16)
    out_got = at.swap_y(out_given)
    moved = down_sum.advance(out_given)
    d_qkv, d_split = attend_back(
        y_index, qkv, after(grad_mixed, *moved), inverse, expos, aux, 2, pairs
    )
    moved = gu_sum.advance(d_qkv)
    middle = 7 * LANES
    low = dot_tn(normed_one, after(d_qkv, *moved)[:, :middle]).astype(BF16)
    total_down = down_sum.finish(low)
    low_sum = Reduction(at, low, total_down)
    d_in = jnp.concatenate([d_qkv, after(d_split, *low_sum.sent)], axis=1)
    bias_part = jnp.sum(d_split.astype(F32), axis=0)
    bias_part = bias_part[:heads] + bias_part[heads : 2 * heads]
    high = jnp.concatenate(
        [dot_tn(normed_one, d_in[:, middle:]), dot_tn(grad_attn, mixed)], axis=1
    ).astype(BF16)
    given = dot_nt(after(d_in, high)[pack:], w_in).astype(BF16)
    got = at.swap_core(given)
    total_gu = gu_sum.finish(given)
    high_sum = Reduction(at, high, total_gu)
    part = dot_nt(after(d_in, *high_sum.sent)[:pack], w_in)
    mine = part + after(got, part).astype(F32)
    given = mine[rows_loc:].astype(BF16)
    got = at.swap_y(given)
    layer_out = resid + (out_own[:rows_loc] + after(out_got, low).astype(F32))
    layer_out = layer_out.astype(BF16)
    moved = low_sum.advance(layer_out, *high_sum.sent)
    moved = high_sum.advance(*moved)
    (got,) = after_all((got,), *moved)

    grad_one = mine[:rows_loc] + got.astype(F32)
    weighted = gain_one * grad_one
    inner_one = jnp.mean(unit_one * weighted, axis=1, keepdims=True)
    norm1_part = jnp.sum(grad_one * unit_one, axis=0)
    x_grad = (grad_resid + scale_one * (weighted - unit_one * inner_one)).astype(BF16)
    moved = low_sum.advance(norm1_part)
    moved = high_sum.advance(*moved)

    lone = jnp.pad(jnp.stack([bias_part, maxima]), ((0, 4), (0, width - heads)))
    sums = at.sum_plane(
        jnp.concatenate([jnp.stack([norm1_part, norm2_part]), lone], axis=0),
        (low_sum, high_sum),
        lambda one, two: jnp.concatenate(
            [one[:3] + two[:3], jnp.maximum(one[3:], two[3:])], axis=0
        ),
    )
    other = at.swap_core(sums)
    cut = width // 2
    norms = sums[:2] + other[:2]
    norms = lax.dynamic_slice_in_dim(norms, at.y * cut, cut, 1) + at.swap_y(
        lax.dynamic_slice_in_dim(norms, (1 - at.y) * cut, cut, 1)
    )
    lone = at.by_core(sums[2:4, :heads], other[2:4, :heads], 1)
    g_bias = lone[0]
    clip_factor = jnp.minimum(1.0, clip_tau / jnp.maximum(lone[1], 1.0))
    columns = jnp.repeat(jnp.sqrt(clip_factor), HEAD_DIM)
    clipped_query = (w_query.astype(F32) * columns[None, :]).astype(BF16)
    clipped_key = (w_key.astype(F32) * columns[None, :]).astype(BF16)

    def place(own):
        keep, got = at.finish_grad(own)
        return at.by_core(keep, got, 1)

    g_down = place(total_down)
    keep, got = at.finish_grad(total_gu)
    g_gate = at.by_core(keep[:, :units], got[:, :units], 1)
    g_up = at.by_core(keep[:, units:], got[:, units:], 1)
    low, high = low_sum.finish(), high_sum.finish()
    got_low, got_high = at.swap_core(at.theirs(low)), at.swap_core(at.theirs(high))
    g_query, g_key, g_value, g_output = assemble(at.core, low, got_low, high, got_high, pairs)
    start = qkv_cols - middle
    mine = lax.dynamic_slice(high, (at.core * d_rows, start), (d_rows, 2 * heads))
    both = at.by_core(mine[None], got_high[None, :, start : start + 2 * heads].astype(F32), 0)
    g_forget = both[..., :heads] + both[..., heads:]
    g_forget = jnp.concatenate([g_forget[0], g_forget[1]], axis=1)

    return (
        layer_out,
        x_grad,
        norms[0],
        g_query,
        g_key,
        g_value,
        g_forget,
        g_bias,
        g_output,
        norms[1],
        g_gate,
        g_up,
        g_down,
        clip_factor,
        clipped_query,
        clipped_key,
    )


def pick_body(mesh):
    dp, tensor = mesh.shape["dp"], mesh.shape["tensor"]

    def body(*args):
        rows, heads = args[0].shape[0], args[7].shape[0]
        depth = dp // 4
        paired = (
            tensor == 2
            and dp % 4 == 0
            and depth & (depth - 1) == 0
            and rows == BLOCK
            and heads % 4 == 0
        )
        return (paired_body if paired else general_body)(*args)

    return body
def solution(mesh):
    return jax.shard_map(
        pick_body(mesh),
        mesh=mesh,
        in_specs=(
            P(("dp", "tensor"), None),
            P("dp", None),
            P("dp"),
            P("dp", "tensor"),
            P("dp", "tensor"),
            P("dp", "tensor"),
            P("dp", "tensor"),
            P("tensor"),
            P("dp", "tensor"),
            P("dp"),
            P("dp", "tensor"),
            P("dp", "tensor"),
            P("dp", "tensor"),
            P("tensor"),
            P(("dp", "tensor"), None),
        ),
        out_specs=(
            P(("dp", "tensor"), None),
            P(("dp", "tensor"), None),
            P("tensor"),
            P("dp", "tensor"),
            P("dp", "tensor"),
            P("dp", "tensor"),
            P("dp", "tensor"),
            P("tensor"),
            P("dp", "tensor"),
            P("tensor"),
            P("dp", "tensor"),
            P("dp", "tensor"),
            P("dp", "tensor"),
            P("tensor"),
            P("dp", "tensor"),
            P("dp", "tensor"),
        ),
        check_vma=False,
    )
```

```python
import math
from functools import partial

import jax
import jax.numpy as jnp
from jax import lax
from jax.experimental import pallas as pl
from jax.experimental.pallas import tpu as pltpu
from jax.sharding import PartitionSpec as P

HEAD_DIM = 64
BLOCK = 256
LANES = 128
EPSILON = 1e-06
HIGHEST = lax.Precision.HIGHEST
NEGATIVE = -1e30
F32 = jnp.float32
BF16 = jnp.bfloat16
def combined_all(part, axis, combine):
    gathered = jax.tree.map(lambda a: lax.all_gather(a, axis), part)

    def take(source):
        return jax.tree.map(lambda a: lax.dynamic_index_in_dim(a, source, 0, False), gathered)

    return lax.fori_loop(
        1, lax.axis_size(axis), lambda source, state: combine(state, take(source)), take(0)
    )


def contract_last(left_op, right_op):
    return lax.dot_general(
        left_op, right_op, (((1,), (1,)), ((), ())), preferred_element_type=jnp.float32
    )


def contract_first(left_op, right_op):
    return lax.dot_general(
        left_op, right_op, (((0,), (0,)), ((), ())), preferred_element_type=jnp.float32
    )


def block_terms(q_blk, keys_all, cumul, seg_row, offset, rows_blk):
    positions = jnp.arange(keys_all.shape[0], dtype=jnp.int32)
    q_pos = offset + jnp.arange(rows_blk, dtype=jnp.int32)
    allowed = (seg_row[:, None] == seg_row[None, :]) & (
        q_pos[:, None] // BLOCK >= positions[None, :] // BLOCK
    )
    signs = jnp.where(positions[None, :] <= q_pos[:, None], 1.0, -1.0).astype(jnp.float32)
    raw_blk = jnp.einsum("qhe,khe->hqk", q_blk, keys_all, preferred_element_type=jnp.float32) * (
        1.0 / math.sqrt(HEAD_DIM)
    )
    differ = cumul.T[:, :, None] - cumul.T[:, None, :]
    scores = jnp.where(allowed[None], raw_blk + signs[None] * differ, NEGATIVE)
    return (raw_blk, scores, allowed, signs)


def combine(former, latter):
    return (
        jnp.maximum(former[0], latter[0]),
        former[1] + latter[1],
        former[2] + latter[2],
        former[3] + latter[3],
    )


def general_body(
    layer_in,
    segment_ids,
    norm1_gain,
    w_query,
    w_key,
    w_value,
    w_forget,
    forget_bias,
    w_output,
    norm2_gain,
    w_gate,
    w_up,
    w_down,
    clip_tau,
    out_grad,
):
    gain_one, wq_all, wk_all, wv_all, wf_all, wo_all, gain_two, wg_all, wu_all, wd_all = (
        lax.all_gather(norm1_gain, "dp", axis=0, tiled=True),
        lax.all_gather(w_query, "dp", axis=0, tiled=True),
        lax.all_gather(w_key, "dp", axis=0, tiled=True),
        lax.all_gather(w_value, "dp", axis=0, tiled=True),
        lax.all_gather(w_forget, "dp", axis=0, tiled=True),
        lax.all_gather(w_output, "dp", axis=0, tiled=True),
        lax.all_gather(norm2_gain, "dp", axis=0, tiled=True),
        lax.all_gather(w_gate, "dp", axis=0, tiled=True),
        lax.all_gather(w_up, "dp", axis=0, tiled=True),
        lax.all_gather(w_down, "dp", axis=0, tiled=True),
    )
    gain_one = gain_one.astype(jnp.float32)
    gain_two = gain_two.astype(jnp.float32)
    tok_local = layer_in.shape[0]
    tokens = tok_local * lax.axis_size("tensor")
    heads_loc = forget_bias.shape[0]
    row_start = lax.axis_index("tensor") * tok_local
    seg_row = segment_ids[0]
    factor = 1.0 / math.sqrt(HEAD_DIM)
    rows_full = lax.all_gather(layer_in, "tensor", axis=0, tiled=True).astype(jnp.float32)
    scale_one = lax.rsqrt(jnp.mean(rows_full * rows_full, axis=1, keepdims=True) + EPSILON)
    unit_one = rows_full * scale_one
    normed_one = (unit_one * gain_one).astype(jnp.bfloat16)
    queries = (
        jnp.dot(normed_one, wq_all, preferred_element_type=jnp.float32)
        .astype(jnp.bfloat16)
        .reshape(tokens, heads_loc, HEAD_DIM)
    )
    keys_all = (
        jnp.dot(normed_one, wk_all, preferred_element_type=jnp.float32)
        .astype(jnp.bfloat16)
        .reshape(tokens, heads_loc, HEAD_DIM)
    )
    values_all = (
        jnp.dot(normed_one, wv_all, preferred_element_type=jnp.float32)
        .astype(jnp.bfloat16)
        .reshape(tokens, heads_loc, HEAD_DIM)
    )
    logits = jnp.dot(normed_one, wf_all, preferred_element_type=jnp.float32) + forget_bias
    cumul = jnp.cumsum(jax.nn.log_sigmoid(logits), axis=0)
    rows_blk = min(512, tokens)
    blocks = tokens // rows_blk
    numbers = jnp.arange(blocks, dtype=jnp.int32)

    def forward_block(number):
        offset = number * rows_blk
        raw_blk, scores, allowed, signs = block_terms(
            queries, keys_all, cumul, seg_row, offset, rows_blk
        )
        top_blk = jnp.max(jnp.where(allowed[None], raw_blk, NEGATIVE), axis=(1, 2))
        row_peak = jnp.max(scores, axis=2, keepdims=True)
        expo_blk = jnp.exp(scores - row_peak)
        totals = jnp.sum(expo_blk, axis=2, keepdims=True)
        weights = (expo_blk / totals).astype(jnp.bfloat16)
        mixed_out = jnp.einsum(
            "hqk,khe->qhe", weights, values_all, preferred_element_type=jnp.float32
        ).astype(jnp.bfloat16)
        return (mixed_out, (row_peak + jnp.log(totals))[:, :, 0], top_blk)

    mixed_out, log_sums, top_blk = lax.map(forward_block, numbers)
    mixed_flat = mixed_out.reshape(tokens, heads_loc * HEAD_DIM)
    maxima = jnp.max(top_blk, axis=0)
    attn_part = contract_last(mixed_flat, wo_all)
    resid_full = rows_full + lax.psum(attn_part.astype(jnp.bfloat16), "tensor").astype(jnp.float32)
    scale_full = lax.rsqrt(jnp.mean(resid_full * resid_full, axis=1, keepdims=True) + EPSILON)
    normed_two = (resid_full * scale_full * gain_two).astype(jnp.bfloat16)
    resid_part = lax.dynamic_slice_in_dim(resid_full, row_start, tok_local, 0)
    scale_two = lax.dynamic_slice_in_dim(scale_full, row_start, tok_local, 0)
    gate_pre = jnp.dot(normed_two, wg_all, preferred_element_type=jnp.float32)
    up_pre = jnp.dot(normed_two, wu_all, preferred_element_type=jnp.float32)
    gate_sig = jax.nn.sigmoid(gate_pre)
    gate_act = gate_pre * gate_sig
    hidden = (gate_act * up_pre).astype(jnp.bfloat16)
    ffn_part = lax.psum_scatter(
        contract_last(hidden, wd_all).astype(jnp.bfloat16),
        "tensor",
        scatter_dimension=0,
        tiled=True,
    ).astype(jnp.float32)
    layer_out = (resid_part + ffn_part).astype(jnp.bfloat16)
    grad_full = lax.all_gather(out_grad, "tensor", axis=0, tiled=True)
    grad_hidden = jnp.dot(grad_full, wd_all, preferred_element_type=jnp.float32)
    grad_gate = (grad_hidden * up_pre * gate_sig * (1.0 + gate_pre * (1.0 - gate_sig))).astype(
        jnp.bfloat16
    )
    grad_up = (grad_hidden * gate_act).astype(jnp.bfloat16)
    g_down = contract_first(grad_full, hidden)
    g_gate = contract_first(normed_two, grad_gate)
    g_up = contract_first(normed_two, grad_up)
    grad_normed = contract_last(grad_gate, wg_all) + contract_last(grad_up, wu_all)
    grad_two = lax.psum_scatter(
        grad_normed.astype(jnp.bfloat16), "tensor", scatter_dimension=0, tiled=True
    ).astype(jnp.float32)
    unit_two = resid_part * scale_two
    inner_two = jnp.mean(unit_two * gain_two * grad_two, axis=1, keepdims=True)
    norm2_part = jnp.sum(grad_two * unit_two, axis=0)
    grad_resid = out_grad.astype(jnp.float32) + scale_two * (
        gain_two * grad_two - unit_two * inner_two
    )
    grad_attn = lax.all_gather(grad_resid.astype(jnp.bfloat16), "tensor", axis=0, tiled=True)
    g_output = contract_first(grad_attn, mixed_flat)
    grad_mixed = jnp.dot(grad_attn, wo_all, preferred_element_type=jnp.float32).astype(jnp.bfloat16)
    grad_mixed = grad_mixed.reshape(blocks, rows_blk, heads_loc, HEAD_DIM)

    def backward_block(carried, block_in):
        key_acc, value_acc, column_acc = carried
        number, log_blk, grad_blk = block_in
        offset = number * rows_blk
        raw_blk, scores, allowed, signs = block_terms(
            queries, keys_all, cumul, seg_row, offset, rows_blk
        )
        prob_blk = jnp.exp(scores - log_blk[:, :, None])
        weights = prob_blk.astype(jnp.bfloat16)
        grad_prob = jnp.einsum(
            "qhe,khe->hqk", grad_blk, values_all, preferred_element_type=jnp.float32
        )
        inner = jnp.sum(prob_blk * grad_prob, axis=2, keepdims=True)
        grad_scores = (prob_blk * (grad_prob - inner)).astype(jnp.bfloat16)
        value_acc = value_acc + jnp.einsum(
            "hqk,qhe->khe", weights, grad_blk, preferred_element_type=jnp.float32
        )
        key_acc = key_acc + jnp.einsum(
            "hqk,qhe->khe", grad_scores, queries, preferred_element_type=jnp.float32
        )
        grad_query = (
            jnp.einsum("hqk,khe->qhe", grad_scores, keys_all, preferred_element_type=jnp.float32)
            * factor
        ).astype(jnp.bfloat16)
        signed = grad_scores.astype(jnp.float32) * signs[None]
        column_acc = column_acc - jnp.sum(signed, axis=1).T
        return ((key_acc, value_acc, column_acc), (grad_query, jnp.sum(signed, axis=2).T))

    start_acc = (
        jnp.zeros((tokens, heads_loc, HEAD_DIM), jnp.float32),
        jnp.zeros((tokens, heads_loc, HEAD_DIM), jnp.float32),
        jnp.zeros((tokens, heads_loc), jnp.float32),
    )
    (key_acc, value_acc, column_acc), (grad_query, row_parts) = lax.scan(
        backward_block, start_acc, (numbers, log_sums, grad_mixed)
    )
    grad_q = grad_query.reshape(tokens, heads_loc * HEAD_DIM)
    grad_k = (key_acc * factor).astype(jnp.bfloat16).reshape(tokens, heads_loc * HEAD_DIM)
    grad_v = value_acc.astype(jnp.bfloat16).reshape(tokens, heads_loc * HEAD_DIM)
    grad_cum = row_parts.reshape(tokens, heads_loc) + column_acc
    grad_logs = jnp.cumsum(grad_cum[::-1], axis=0)[::-1]
    grad_logit = grad_logs * jax.nn.sigmoid(-logits)
    g_bias = jnp.sum(grad_logit, axis=0)
    g_forget = jnp.einsum(
        "td,th->dh", normed_one, grad_logit, precision=HIGHEST, preferred_element_type=jnp.float32
    )
    g_query = contract_first(normed_one, grad_q)
    g_key = contract_first(normed_one, grad_k)
    g_value = contract_first(normed_one, grad_v)
    grad_one = (
        contract_last(grad_q, wq_all)
        + contract_last(grad_k, wk_all)
        + contract_last(grad_v, wv_all)
    )
    grad_one = grad_one + jnp.einsum(
        "th,dh->td", grad_logit, wf_all, precision=HIGHEST, preferred_element_type=jnp.float32
    )
    weighted = gain_one * grad_one
    grad_rows_one = scale_one * (
        weighted - unit_one * jnp.mean(unit_one * weighted, axis=1, keepdims=True)
    )
    norm1_part = jnp.sum(grad_one * unit_one, axis=0)
    grad_input, g_norm1_part, g_norm2_part = (
        lax.psum_scatter(
            grad_rows_one.astype(jnp.bfloat16), "tensor", scatter_dimension=0, tiled=True
        ).astype(jnp.float32),
        lax.psum_scatter(
            norm1_part.astype(jnp.bfloat16), "tensor", scatter_dimension=0, tiled=True
        ).astype(jnp.float32),
        lax.psum_scatter(
            norm2_part.astype(jnp.bfloat16), "tensor", scatter_dimension=0, tiled=True
        ).astype(jnp.float32),
    )
    x_grad = (grad_resid + grad_input).astype(jnp.bfloat16)
    g_query, g_key, g_value, g_forget, g_output, g_gate, g_up, g_down = (
        lax.psum_scatter(
            g_query.astype(jnp.bfloat16), "dp", scatter_dimension=0, tiled=True
        ).astype(jnp.float32),
        lax.psum_scatter(g_key.astype(jnp.bfloat16), "dp", scatter_dimension=0, tiled=True).astype(
            jnp.float32
        ),
        lax.psum_scatter(
            g_value.astype(jnp.bfloat16), "dp", scatter_dimension=0, tiled=True
        ).astype(jnp.float32),
        lax.psum_scatter(
            g_forget.astype(jnp.bfloat16), "dp", scatter_dimension=0, tiled=True
        ).astype(jnp.float32),
        lax.psum_scatter(
            g_output.astype(jnp.bfloat16), "dp", scatter_dimension=0, tiled=True
        ).astype(jnp.float32),
        lax.psum_scatter(g_gate.astype(jnp.bfloat16), "dp", scatter_dimension=0, tiled=True).astype(
            jnp.float32
        ),
        lax.psum_scatter(g_up.astype(jnp.bfloat16), "dp", scatter_dimension=0, tiled=True).astype(
            jnp.float32
        ),
        lax.psum_scatter(g_down.astype(jnp.bfloat16), "dp", scatter_dimension=0, tiled=True).astype(
            jnp.float32
        ),
    )
    maxima, g_bias, g_norm1, g_norm2 = combined_all(
        (maxima, g_bias, g_norm1_part, g_norm2_part), "dp", combine
    )
    clip_factor = jnp.minimum(1.0, clip_tau / jnp.maximum(maxima, 1.0))
    columns = jnp.repeat(jnp.sqrt(clip_factor), HEAD_DIM)
    clipped_query = (w_query.astype(jnp.float32) * columns[None, :]).astype(jnp.bfloat16)
    clipped_key = (w_key.astype(jnp.float32) * columns[None, :]).astype(jnp.bfloat16)
    return (
        layer_out,
        x_grad,
        g_norm1,
        g_query,
        g_key,
        g_value,
        g_forget,
        g_bias,
        g_output,
        g_norm2,
        g_gate,
        g_up,
        g_down,
        clip_factor,
        clipped_query,
        clipped_key,
    )


def dot_nt(left, right):
    return lax.dot_general(left, right, (((1,), (1,)), ((), ())), preferred_element_type=F32)


def dot_nn(left, right):
    return lax.dot_general(left, right, (((1,), (0,)), ((), ())), preferred_element_type=F32)


def dot_tn(left, right):
    return lax.dot_general(left, right, (((0,), (0,)), ((), ())), preferred_element_type=F32)


def attend_kernel(y_ref, qkv_ref, aux_ref, *refs):
    o_ref, inv_ref, exp_ref, top_ref = refs[-4:]
    y = y_ref[0]
    starts = (pl.multiple_of(y * BLOCK, BLOCK), pl.multiple_of((1 - y) * BLOCK, BLOCK))
    lane = lax.broadcasted_iota(jnp.int32, (1, LANES), 1)
    first = lane < HEAD_DIM
    aux = [aux_ref[0, :, pl.ds(start, BLOCK)] for start in starts]
    aux_col = [a.T for a in aux]
    q_blk = [qkv_ref[pl.ds(s, BLOCK), 0:LANES] * 0.125 for s in starts]
    k_blk = [qkv_ref[pl.ds(s, BLOCK), LANES : 2 * LANES] for s in starts]
    v_blk = [qkv_ref[pl.ds(s, BLOCK), 2 * LANES : 3 * LANES] for s in starts]
    same = {}
    for i, j in ((0, 0), (1, 0), (1, 1)):
        same[i, j] = aux_col[i][:, 2:3] == aux[j][2:3, :]
    tops = []
    results = [[], []]
    for head in range(2):
        mine = first if head == 0 else jnp.logical_not(first)
        top = None
        v_ext = [jnp.where(mine, v, jnp.ones_like(v)) for v in v_blk]
        k_head = [jnp.where(mine, k, jnp.zeros_like(k)) for k in k_blk]
        for i in range(2):
            scores = []
            for j in range(i + 1):
                raw = dot_nt(q_blk[i], k_head[j])
                seen = jnp.where(same[i, j], raw, NEGATIVE)
                high = jnp.max(seen, axis=0, keepdims=True)
                top = high if top is None else jnp.maximum(top, high)
                differ = aux_col[i][:, head : head + 1] - aux[j][head : head + 1, :]
                scores.append(seen - jnp.abs(differ))
            peak = jnp.max(scores[0], axis=1, keepdims=True)
            if i == 1:
                peak = jnp.maximum(peak, jnp.max(scores[1], axis=1, keepdims=True))
            acc = None
            for j in range(i + 1):
                weights = jnp.exp(scores[j] - peak).astype(BF16)
                exp_ref[0, 0, head, :, (i + j) * BLOCK : (i + j + 1) * BLOCK] = weights
                part = dot_nn(weights, v_ext[j])
                acc = part if acc is None else acc + part
            results[i].append(acc)
        tops.append(jnp.maximum(top[:, :LANES], top[:, LANES:]))
    for i in range(2):
        one, two = results[i]
        total = pltpu.roll(jnp.where(first, two, one), HEAD_DIM, 1)
        inverse = 1.0 / total
        inv_ref[pl.ds(starts[i], BLOCK), :] = inverse
        o_ref[pl.ds(starts[i], BLOCK), :] = (jnp.where(first, one, two) * inverse).astype(BF16)
    row = lax.broadcasted_iota(jnp.int32, (8, LANES), 0)
    top_ref[0, 0] = jnp.where(row == 0, tops[0], tops[1])


def attend(y_index, qkv, aux, packs, pairs, pack, kept=()):
    rows = qkv.shape[0] // packs
    wide = 3 * LANES
    grid_spec = pltpu.PrefetchScalarGridSpec(
        num_scalar_prefetch=1,
        grid=(pairs,),
        in_specs=[
            pl.BlockSpec((rows, wide), lambda h, y: (pack, h)),
            pl.BlockSpec((1, 8, rows), lambda h, y: (h, 0, pack)),
        ]
        + [pl.BlockSpec(memory_space=pl.ANY) for _ in kept],
        out_specs=[
            pl.BlockSpec((rows, LANES), lambda h, y: (0, h)),
            pl.BlockSpec((rows, LANES), lambda h, y: (pack, h)),
            pl.BlockSpec((1, 1, 2, BLOCK, 3 * BLOCK), lambda h, y: (pack, h, 0, 0, 0)),
            pl.BlockSpec((1, 1, 8, LANES), lambda h, y: (0, h, 0, 0)),
        ],
    )
    return pl.pallas_call(
        attend_kernel,
        grid_spec=grid_spec,
        out_shape=(
            jax.ShapeDtypeStruct((rows, pairs * LANES), BF16),
            jax.ShapeDtypeStruct((packs * rows, pairs * LANES), F32),
            jax.ShapeDtypeStruct((packs, pairs, 2, BLOCK, 3 * BLOCK), BF16),
            jax.ShapeDtypeStruct((1, pairs, 8, LANES), F32),
        ),
        input_output_aliases={3: 1, 4: 2} if kept else {},
        cost_estimate=pl.CostEstimate(
            flops=pairs * 2 * 6 * BLOCK * BLOCK * LANES * 2,
            bytes_accessed=10_000_000,
            transcendentals=pairs * 2 * 3 * BLOCK * BLOCK,
        ),
        name="attend",
    )(y_index, qkv, aux, *kept)


def attend_back_kernel(
    pairs, y_ref, qkv_ref, do_ref, inv_ref, exp_ref, aux_ref, dqkv_ref, split_ref
):
    y = y_ref[0]
    starts = (pl.multiple_of(y * BLOCK, BLOCK), pl.multiple_of((1 - y) * BLOCK, BLOCK))
    lane = lax.broadcasted_iota(jnp.int32, (1, LANES), 1)
    first = lane < HEAD_DIM
    ones = jnp.ones((8, BLOCK), BF16)
    lower = lax.broadcasted_iota(jnp.int32, (BLOCK, BLOCK), 1) <= lax.broadcasted_iota(
        jnp.int32, (BLOCK, BLOCK), 0
    )
    q_blk = [qkv_ref[pl.ds(s, BLOCK), 0:LANES] * 0.125 for s in starts]
    k_blk = [qkv_ref[pl.ds(s, BLOCK), LANES : 2 * LANES] for s in starts]
    v_blk = [qkv_ref[pl.ds(s, BLOCK), 2 * LANES : 3 * LANES] for s in starts]
    inv_blk = [inv_ref[pl.ds(s, BLOCK), :] for s in starts]
    do_blk = [
        (do_ref[pl.ds(s, BLOCK), :].astype(F32) * inv).astype(BF16)
        for s, inv in zip(starts, inv_blk)
    ]
    dq, dk, dv, dc = ([], []), ([], []), ([], []), ([], [])
    for head in range(2):
        mine = first if head == 0 else jnp.logical_not(first)
        v_head = [jnp.where(mine, v, jnp.zeros_like(v)) for v in v_blk]
        dk_acc, dv_acc, row_acc, col_acc = [None] * 2, [None] * 2, [None] * 2, [None] * 2
        for i in range(2):
            expos, probs, inner = [], [], None
            inv_col = inv_blk[i][:, head * HEAD_DIM : head * HEAD_DIM + 1]
            for j in range(i + 1):
                expo = exp_ref[0, 0, head, :, (i + j) * BLOCK : (i + j + 1) * BLOCK]
                grad_prob = dot_nt(do_blk[i], v_head[j])
                wide = expo.astype(F32)
                part = jnp.sum(wide * grad_prob, axis=1, keepdims=True)
                inner = part if inner is None else inner + part
                expos.append((expo, wide))
                probs.append(grad_prob)
            inner = inner * inv_col
            dq_acc = None
            for j in range(i + 1):
                expo, wide = expos[j]
                grad_score = wide * (probs[j] - inner)
                low = grad_score.astype(BF16)
                if i == j:
                    signed = jnp.where(lower, low, -low)
                else:
                    signed = low
                part = dot_nn(low, k_blk[j])
                dq_acc = part if dq_acc is None else dq_acc + part
                part = dot_tn(low, q_blk[i])
                dk_acc[j] = part if dk_acc[j] is None else dk_acc[j] + part
                part = dot_tn(expo, do_blk[i])
                dv_acc[j] = part if dv_acc[j] is None else dv_acc[j] + part
                part = dot_nt(ones, signed)
                row_acc[i] = part if row_acc[i] is None else row_acc[i] + part
                part = dot_nn(ones, signed)
                col_acc[j] = part if col_acc[j] is None else col_acc[j] + part
            dq[i].append(dq_acc)
        for j in range(2):
            dk[j].append(dk_acc[j])
            dv[j].append(dv_acc[j])
            dc[j].append(row_acc[j] - col_acc[j])
    for i in range(2):
        rows = pl.ds(starts[i], BLOCK)
        dqkv_ref[rows, 0:LANES] = (jnp.where(first, *dq[i]) * 0.125).astype(BF16)
        dqkv_ref[rows, LANES : 2 * LANES] = jnp.where(first, *dk[i]).astype(BF16)
        dqkv_ref[rows, 2 * LANES : 3 * LANES] = jnp.where(first, *dv[i]).astype(BF16)

    row = lax.broadcasted_iota(jnp.int32, (8, BLOCK), 0)
    until = jnp.where(lower, 1.0, 0.0).astype(BF16)
    d_cum = [jnp.where(row == 0, *dc[i]) for i in range(2)]
    ends = jnp.sum(d_cum[1], axis=1, keepdims=True)
    pair = pl.program_id(1)
    spot = lax.broadcasted_iota(jnp.int32, (8, LANES), 0)
    place = jnp.where(spot < 2, 2 * pair + spot, 2 * pairs + 2 * pair + spot - 2)
    hit = (lax.broadcasted_iota(jnp.int32, (8, LANES), 1) == place) & (spot < 4)
    hit = jnp.where(hit, 1.0, 0.0).astype(F32)

    @pl.when(pair == 0)
    def _():
        split_ref[...] = jnp.zeros_like(split_ref)

    for i in range(2):
        rows = pl.ds(starts[i], BLOCK)
        high = d_cum[i].astype(BF16).astype(F32)
        rest = d_cum[i] - high
        middle = rest.astype(BF16).astype(F32)
        low = pltpu.roll(rest - middle, 4, 0)
        parts = jnp.where(row < 4, pltpu.roll(middle, 2, 0), jnp.where(row < 6, low, 0.0))
        parts = jnp.where(row < 2, high, parts).astype(BF16)
        sums = dot_nn(parts, until)
        back = sums + pltpu.roll(sums, 6, 0) + pltpu.roll(sums, 4, 0)
        if i == 0:
            back = back + ends
        logit = pltpu.roll(aux_ref[0, :, rows], 4, 0)
        grad = back * jax.nn.sigmoid(-logit)
        high = grad.astype(BF16).astype(F32)
        rest = pltpu.roll((grad - high).astype(BF16).astype(F32), 2, 0)
        both = jnp.where(row < 2, high, jnp.where(row < 4, rest, 0.0))
        old = split_ref[rows, :].astype(F32)
        split_ref[rows, :] = (old + dot_tn(both, hit)).astype(BF16)


def attend_back(y_index, qkv, d_out, inverse, expos, aux, packs, pairs):
    rows = qkv.shape[0] // packs
    wide = 3 * LANES
    grid_spec = pltpu.PrefetchScalarGridSpec(
        num_scalar_prefetch=1,
        grid=(packs, pairs),
        in_specs=[
            pl.BlockSpec((rows, wide), lambda p, h, y: (p, h)),
            pl.BlockSpec((rows, LANES), lambda p, h, y: (p, h)),
            pl.BlockSpec((rows, LANES), lambda p, h, y: (p, h)),
            pl.BlockSpec((1, 1, 2, BLOCK, 3 * BLOCK), lambda p, h, y: (p, h, 0, 0, 0)),
            pl.BlockSpec((1, 8, rows), lambda p, h, y: (h, 0, p)),
        ],
        out_specs=[
            pl.BlockSpec((rows, wide), lambda p, h, y: (p, h)),
            pl.BlockSpec((rows, LANES), lambda p, h, y: (p, 0)),
        ],
    )
    return pl.pallas_call(
        partial(attend_back_kernel, pairs),
        grid_spec=grid_spec,
        out_shape=(
            jax.ShapeDtypeStruct((packs * rows, pairs * wide), BF16),
            jax.ShapeDtypeStruct((packs * rows, LANES), BF16),
        ),
        cost_estimate=pl.CostEstimate(
            flops=packs * pairs * 2 * 18 * BLOCK * BLOCK * LANES * 2,
            bytes_accessed=20_000_000,
            transcendentals=0,
        ),
        name="attend_back",
    )(y_index, qkv, d_out, inverse, expos, aux)


def assemble_kernel(core_ref, low_ref, got_low_ref, high_ref, got_high_ref, *outs):
    core = core_ref[0]
    rows = outs[0].shape[0]
    own = pl.ds(pl.multiple_of(core * rows, 8), rows)
    count = outs[0].shape[1] // (2 * LANES)
    middle = low_ref.shape[1]
    spots = [[3 * p + which for p in range(count)] for which in range(3)]
    spots.append([3 * count + 1 + p for p in range(count)])
    for out, chosen in zip(outs, spots):
        for p, spot in enumerate(chosen):
            start = spot * LANES
            mine_ref, got_ref = low_ref, got_low_ref
            if start >= middle:
                start -= middle
                mine_ref, got_ref = high_ref, got_high_ref
            lanes = slice(start, start + LANES)
            mine, got = mine_ref[own, lanes], got_ref[:, lanes].astype(F32)
            left = slice(p * LANES, (p + 1) * LANES)
            right = slice((count + p) * LANES, (count + p + 1) * LANES)
            out[:, left] = jnp.where(core == 0, mine, got)
            out[:, right] = jnp.where(core == 0, got, mine)


def assemble(core, low, got_low, high, got_high, pairs):
    shape = jax.ShapeDtypeStruct((got_low.shape[0], 2 * pairs * LANES), F32)
    spec = pl.BlockSpec(memory_space=pltpu.VMEM)
    return pl.pallas_call(
        assemble_kernel,
        in_specs=[pl.BlockSpec(memory_space=pltpu.SMEM)] + [spec] * 4,
        out_specs=[spec] * 4,
        out_shape=[shape] * 4,
        name="assemble",
    )(core.astype(jnp.int32).reshape(1), low, got_low, high, got_high)


class Gathering:
    def __init__(self, at, shard):
        self.at, self.step, self.half = at, 1, at.depth
        self.whole = None
        self.waiting = [(shard, 0, 0)]
        self.send(shard, shard)

    def store(self, *others):
        for part, step, side in self.waiting:
            if others:
                part = after(part, *others)
            if self.whole is None:
                self.whole = jnp.zeros((2 * self.half,) + part.shape, part.dtype)
                if others:
                    self.whole = after(self.whole, *others)
            start = (self.at.block_of(step), side, 0, 0)
            self.whole = lax.dynamic_update_slice(self.whole, part[None], start)
        self.waiting = []

    def send(self, up, down):
        if self.step == self.half:
            up, down = up[:1], down[1:]
        self.came = (self.at.ring(up, 1), self.at.ring(down, -1))

    def take(self, *others):
        up, down = after_all(self.came, *others)
        side = 1 if self.step == self.half else 0
        self.waiting += [(up, -self.step, 0), (down, self.step, side)]
        return up, down

    def advance(self, *others):
        up, down = self.take(*others)
        self.step += 1
        self.send(up, down)
        return up, down

    def finish(self, *others):
        self.take(*others)
        self.store()
        return self.whole.reshape(-1, self.whole.shape[-1])


class Reduction:
    def __init__(self, at, grad, *others):
        self.at, self.step, self.half = at, 1, at.depth
        count = 2 * at.depth
        self.blocks = grad.reshape(count, 2, grad.shape[0] // (2 * count), grad.shape[1])
        far = self.own(self.half)
        self.sent = after_all((far[:1], far[1:]), *others) if others else (far[:1], far[1:])
        self.send()

    def own(self, step):
        start = (self.at.block_of(step), 0, 0, 0)
        return lax.dynamic_slice(self.blocks, start, (1,) + self.blocks.shape[1:])[0]

    def send(self):
        self.came = (self.at.ring(self.sent[0], 1), self.at.ring(self.sent[1], -1))

    def advance(self, *others):
        up, down = after_all(self.came, *others)
        ahead, behind = self.own(self.half - self.step), self.own(self.step - self.half)
        if self.step == 1:
            first = (ahead[:1].astype(F32) + up.astype(F32)).astype(BF16)
            second = (behind[1:].astype(F32) + down.astype(F32)).astype(BF16)
            up = jnp.concatenate([first, ahead[1:]], axis=0)
            down = jnp.concatenate([behind[:1], second], axis=0)
        else:
            up = (ahead.astype(F32) + up.astype(F32)).astype(BF16)
            down = (behind.astype(F32) + down.astype(F32)).astype(BF16)
        self.sent = (up, down)
        self.step += 1
        self.send()
        return up, down

    def finish(self, *others):
        up, down = after_all(self.came, *others)
        total = self.own(0).astype(F32) + up.astype(F32) + down.astype(F32)
        return total.reshape(-1, total.shape[-1])


class Place:
    def __init__(self):
        self.dp = lax.axis_size("dp")
        self.depth = self.dp // 4
        index = lax.axis_index("dp")
        self.core = index % 2
        self.x = (index // 2) % 2
        self.z = index // 4
        self.y = lax.axis_index("tensor")

    def swap_core(self, value):
        return lax.ppermute(value, "dp", [(i, i ^ 1) for i in range(self.dp)])

    def swap_y(self, value):
        return lax.ppermute(value, "tensor", [(0, 1), (1, 0)])

    def ring(self, value, step):
        spots = [4 * z for z in range(self.depth)]
        spots += [4 * z + 2 for z in reversed(range(self.depth))]
        count = len(spots)
        pairs = [
            (spots[r] + core, spots[(r + step) % count] + core)
            for r in range(count)
            for core in (0, 1)
        ]
        return lax.ppermute(value, "dp", pairs)

    def block_of(self, step):
        count = 2 * self.depth
        spot = (jnp.where(self.x == 0, self.z, count - 1 - self.z) + step + count) % count
        return jnp.where(spot < self.depth, 2 * spot, 2 * (count - 1 - spot) + 1)

    def sum_plane(self, value, rings, combine):
        step = 2
        rings = list(rings)
        while step < self.dp:
            value = combine(
                value, lax.ppermute(value, "dp", [(i, i ^ step) for i in range(self.dp)])
            )
            if rings:
                value = after(value, *rings.pop(0).advance(value))
            step *= 2
        return value

    def by_core(self, mine, other, axis):
        return jnp.where(
            self.core == 0,
            jnp.concatenate([mine, other], axis=axis),
            jnp.concatenate([other, mine], axis=axis),
        )

    def core_columns(self, weights):
        half = [w.shape[1] // 2 for w in weights]
        keep = [
            lax.dynamic_slice_in_dim(w, self.core * h, h, 1) for w, h in zip(weights, half)
        ]
        give = [
            lax.dynamic_slice_in_dim(w, (1 - self.core) * h, h, 1) for w, h in zip(weights, half)
        ]
        return keep, give

    def finish_grad(self, own):
        rows = own.shape[0] // 2
        keep = lax.dynamic_slice_in_dim(own, self.core * rows, rows, 0)
        return keep, self.swap_core(self.theirs(own)).astype(F32)

    def theirs(self, own):
        rows = own.shape[0] // 2
        return lax.dynamic_slice_in_dim(own, (1 - self.core) * rows, rows, 0).astype(BF16)

    def join(self, rows, near):
        both = jnp.concatenate([rows, near], axis=0)
        return jnp.concatenate([both, self.swap_core(both)], axis=0)

    def meet_core(self, left, right, dot):
        half = left.shape[0] // 2
        given = dot(left[half:], right).astype(BF16)
        got = self.swap_core(given)
        part = dot(after(left, given)[:half], right)
        return part, got


def after(value, *others):
    return lax.optimization_barrier((value,) + others)[0]


def after_all(values, *others):
    return lax.optimization_barrier(tuple(values) + others)[: len(values)]


def interleave(parts):
    starts = range(0, parts[0].shape[1], LANES)
    return jnp.concatenate([p[:, s : s + LANES] for s in starts for p in parts], axis=1)


def split_low(value):
    high = value.astype(BF16)
    return high, (value - high.astype(F32)).astype(BF16)


def paired_body(
    layer_in,
    segment_ids,
    norm1_gain,
    w_query,
    w_key,
    w_value,
    w_forget,
    forget_bias,
    w_output,
    norm2_gain,
    w_gate,
    w_up,
    w_down,
    clip_tau,
    out_grad,
):
    at = Place()
    rows_loc = layer_in.shape[0]
    pack = 2 * rows_loc
    width = layer_in.shape[1]
    heads = forget_bias.shape[0] // 2
    pairs = heads // 2
    y_index = at.y.astype(jnp.int32).reshape(1)
    d_rows = norm1_gain.shape[0]

    units = w_gate.shape[1] // 2
    keep, give = at.core_columns([w_query, w_key, w_value, w_output, w_forget])
    gains = jnp.stack([norm1_gain, norm2_gain], axis=1)
    pad = jnp.zeros((d_rows, LANES - 2 * heads - 2), BF16)

    def first_part(part):
        return jnp.concatenate(
            [interleave(part[:3]), part[4], part[4], gains, pad, part[3]], axis=1
        )

    attn_shard = at.by_core(first_part(keep)[None], at.swap_core(first_part(give))[None], 0)
    rows_near = at.swap_y(layer_in)
    qkv_cols = 3 * heads * HEAD_DIM
    in_cols = qkv_cols + LANES
    attn_ring = Gathering(at, attn_shard)
    keep, give = at.core_columns(after_all((w_gate, w_up, w_down), attn_shard))
    keep, give = jnp.concatenate(keep, axis=1), jnp.concatenate(give, axis=1)
    early = attn_ring.advance(keep, give)
    ffn_shard = at.by_core(after(keep, *early)[None], at.swap_core(after(give, *early))[None], 0)
    moved = attn_ring.advance(rows_near)
    attn_ring.store()
    grad_near = at.swap_y(after(out_grad, *moved))
    def first_norm(rows):
        rows = rows.astype(F32)
        return rows, lax.rsqrt(jnp.mean(rows * rows, axis=1, keepdims=True) + EPSILON)

    rows_all = at.join(layer_in, rows_near)
    x_all, scale_all = first_norm(rows_all)
    unit_all = x_all * scale_all
    attn_ring.advance(ffn_shard, unit_all)
    unit_all = after(unit_all, *attn_ring.came)
    attn_ring.store()
    ffn_ring = Gathering(at, after(ffn_shard, *attn_ring.came))
    attn_all = attn_ring.finish()
    w_in, wo_all = attn_all[:, :in_cols], attn_all[:, in_cols:]
    grad_rows = at.join(out_grad, grad_near)
    w_qkv = w_in[:, :qkv_cols]
    small = w_in[:, qkv_cols:].T
    forget_t = small[:heads]
    gain_one = small[2 * heads : 2 * heads + 1].astype(F32)
    gain_two = small[2 * heads + 1 : 2 * heads + 2].astype(F32)

    normed_one = (unit_all * gain_one).astype(BF16)
    x_own, scale_one = first_norm(layer_in)
    unit_one = x_own * scale_one
    qkv = dot_nn(normed_one, w_qkv).astype(BF16)

    bias = lax.dynamic_slice_in_dim(forget_bias, at.core * heads, heads, 0)
    logits = dot_nt(after(forget_t, qkv), normed_one) + bias[:, None]
    logs = jax.nn.log_sigmoid(logits).reshape(heads, 2, 2, rows_loc)
    steps = jnp.arange(rows_loc, dtype=jnp.int32)
    upper = (steps[:, None] <= steps[None, :]).astype(F32)
    sums = jnp.einsum("hpbt,ts->hpbs", logs, upper, precision=HIGHEST)
    total = sums[..., -1:]
    later = at.y.astype(F32)
    cumul = jnp.stack(
        [sums[:, :, 0] + later * total[:, :, 1], sums[:, :, 1] + (1.0 - later) * total[:, :, 0]],
        axis=2,
    ).reshape(heads, 2 * pack)
    seg_own = after(segment_ids, *early)[0].reshape(2, rows_loc)
    seg_own = jnp.where(at.y == 0, seg_own, seg_own[::-1]).reshape(1, pack)
    seg_both = jnp.concatenate([seg_own, at.swap_core(seg_own)], axis=1).astype(F32)
    aux = jnp.concatenate(
        [
            cumul.reshape(pairs, 2, 2 * pack),
            jnp.broadcast_to(seg_both[None], (pairs, 2, 2 * pack)),
            logits.reshape(pairs, 2, 2 * pack),
            jnp.zeros((pairs, 2, 2 * pack), F32),
        ],
        axis=1,
    )
    aux = after(aux, grad_near)
    mixed_other, inverse, expos, tops_other = attend(y_index, qkv, aux, 2, pairs, 1)
    moved = ffn_ring.advance(mixed_other)

    given = dot_nt(after(mixed_other, *moved), wo_all).astype(BF16)
    got = at.swap_core(given)
    mixed_own, inverse, expos, tops = attend(
        y_index, after(qkv, given), aux, 2, pairs, 0, (inverse, expos)
    )
    tops = jnp.concatenate([tops, tops_other], axis=0)
    maxima = jnp.max(tops[:, :, :2], axis=(0, 3)).reshape(heads)
    mixed = jnp.concatenate([mixed_own, mixed_other], axis=0)
    mine = dot_nt(mixed_own, wo_all) + after(got, mixed_own).astype(F32)
    given = mine[rows_loc:].astype(BF16)
    got = at.swap_y(given)
    ffn_ring.store(given)
    moved = ffn_ring.advance(given)
    (got,) = after_all((got,), *moved)
    resid = x_own + (mine[:rows_loc] + got.astype(F32))
    scale_two = lax.rsqrt(jnp.mean(resid * resid, axis=1, keepdims=True) + EPSILON)
    unit_two = resid * scale_two
    normed_own = (unit_two * gain_two).astype(BF16)
    near = at.swap_y(normed_own)
    ffn_ring.store(normed_own)
    moved = ffn_ring.advance(normed_own)
    (near,) = after_all((near,), maxima, *moved)
    normed_two = at.join(normed_own, near)
    ffn_ring.store(near)
    ffn_all = ffn_ring.finish()
    gu_all, down_all = ffn_all[:, : 2 * units], ffn_all[:, 2 * units :]

    gate_up = dot_nn(normed_two, gu_all)
    gate_pre, up_pre = gate_up[:, :units], gate_up[:, units:]
    gate_sig = jax.nn.sigmoid(gate_pre)
    gate_act = gate_pre * gate_sig
    hidden = (gate_act * up_pre).astype(BF16)
    grad_hidden = dot_nn(grad_rows, down_all)
    grad_gate = (grad_hidden * up_pre * gate_sig * (1.0 + gate_pre * (1.0 - gate_sig))).astype(BF16)
    grad_up = (grad_hidden * gate_act).astype(BF16)
    grad_gu = jnp.concatenate([grad_gate, grad_up], axis=1)

    down_sum = Reduction(at, dot_tn(grad_rows, hidden).astype(BF16))
    part, got = at.meet_core(after(grad_gu, *down_sum.sent), gu_all, dot_nt)
    mine = part + after(got, part).astype(F32)
    given = mine[rows_loc:].astype(BF16)
    got = at.swap_y(given)
    gu_sum = Reduction(at, dot_tn(normed_two, after(grad_gu, given)).astype(BF16))
    moved = down_sum.advance(gu_sum.blocks)

    (got,) = after_all((got,), *moved)
    grad_two = mine[:rows_loc] + got.astype(F32)
    weighted = gain_two * grad_two
    inner_two = jnp.mean(unit_two * weighted, axis=1, keepdims=True)
    norm2_part = jnp.sum(grad_two * unit_two, axis=0)
    grad_resid = out_grad.astype(F32) + scale_two * (weighted - unit_two * inner_two)
    grad_own = grad_resid.astype(BF16)
    near = at.swap_y(grad_own)
    moved = gu_sum.advance(grad_own)
    out_given = dot_nt(after(hidden, *moved)[pack:], down_all).astype(BF16)
    moved = down_sum.advance(out_given)
    out_part = dot_nt(after(hidden, *moved)[:pack], down_all)
    moved = gu_sum.advance(out_part)
    (near,) = after_all((near,), *moved)
    grad_attn = at.join(grad_own, near)

    out_got = at.swap_core(after(out_given, grad_attn))
    grad_mixed = dot_nn(grad_attn, wo_all).astype(BF16)
    out_own = out_part + after(out_got, grad_mixed).astype(F32)
    out_given = out_own[rows_loc:].astype(BF16)
    out_got = at.swap_y(out_given)
    moved = down_sum.advance(out_given)
    d_qkv, d_split = attend_back(
        y_index, qkv, after(grad_mixed, *moved), inverse, expos, aux, 2, pairs
    )
    moved = gu_sum.advance(d_qkv)
    middle = 7 * LANES
    low = dot_tn(normed_one, after(d_qkv, *moved)[:, :middle]).astype(BF16)
    total_down = down_sum.finish(low)
    low_sum = Reduction(at, low, total_down)
    d_in = jnp.concatenate([d_qkv, after(d_split, *low_sum.sent)], axis=1)
    bias_part = jnp.sum(d_split.astype(F32), axis=0)
    bias_part = bias_part[:heads] + bias_part[heads : 2 * heads]
    high = jnp.concatenate(
        [dot_tn(normed_one, d_in[:, middle:]), dot_tn(grad_attn, mixed)], axis=1
    ).astype(BF16)
    given = dot_nt(after(d_in, high)[pack:], w_in).astype(BF16)
    got = at.swap_core(given)
    total_gu = gu_sum.finish(given)
    high_sum = Reduction(at, high, total_gu)
    part = dot_nt(after(d_in, *high_sum.sent)[:pack], w_in)
    mine = part + after(got, part).astype(F32)
    given = mine[rows_loc:].astype(BF16)
    got = at.swap_y(given)
    layer_out = resid + (out_own[:rows_loc] + after(out_got, low).astype(F32))
    layer_out = layer_out.astype(BF16)
    moved = low_sum.advance(layer_out, *high_sum.sent)
    moved = high_sum.advance(*moved)
    (got,) = after_all((got,), *moved)

    grad_one = mine[:rows_loc] + got.astype(F32)
    weighted = gain_one * grad_one
    inner_one = jnp.mean(unit_one * weighted, axis=1, keepdims=True)
    norm1_part = jnp.sum(grad_one * unit_one, axis=0)
    x_grad = (grad_resid + scale_one * (weighted - unit_one * inner_one)).astype(BF16)
    moved = low_sum.advance(norm1_part)
    moved = high_sum.advance(*moved)

    lone = jnp.pad(jnp.stack([bias_part, maxima]), ((0, 4), (0, width - heads)))
    sums = at.sum_plane(
        jnp.concatenate([jnp.stack([norm1_part, norm2_part]), lone], axis=0),
        (low_sum, high_sum),
        lambda one, two: jnp.concatenate(
            [one[:3] + two[:3], jnp.maximum(one[3:], two[3:])], axis=0
        ),
    )
    other = at.swap_core(sums)
    cut = width // 2
    norms = sums[:2] + other[:2]
    norms = lax.dynamic_slice_in_dim(norms, at.y * cut, cut, 1) + at.swap_y(
        lax.dynamic_slice_in_dim(norms, (1 - at.y) * cut, cut, 1)
    )
    lone = at.by_core(sums[2:4, :heads], other[2:4, :heads], 1)
    g_bias = lone[0]
    clip_factor = jnp.minimum(1.0, clip_tau / jnp.maximum(lone[1], 1.0))
    columns = jnp.repeat(jnp.sqrt(clip_factor), HEAD_DIM)
    clipped_query = (w_query.astype(F32) * columns[None, :]).astype(BF16)
    clipped_key = (w_key.astype(F32) * columns[None, :]).astype(BF16)

    def place(own):
        keep, got = at.finish_grad(own)
        return at.by_core(keep, got, 1)

    g_down = place(total_down)
    keep, got = at.finish_grad(total_gu)
    g_gate = at.by_core(keep[:, :units], got[:, :units], 1)
    g_up = at.by_core(keep[:, units:], got[:, units:], 1)
    low, high = low_sum.finish(), high_sum.finish()
    got_low, got_high = at.swap_core(at.theirs(low)), at.swap_core(at.theirs(high))
    g_query, g_key, g_value, g_output = assemble(at.core, low, got_low, high, got_high, pairs)
    start = qkv_cols - middle
    mine = lax.dynamic_slice(high, (at.core * d_rows, start), (d_rows, 2 * heads))
    both = at.by_core(mine[None], got_high[None, :, start : start + 2 * heads].astype(F32), 0)
    g_forget = both[..., :heads] + both[..., heads:]
    g_forget = jnp.concatenate([g_forget[0], g_forget[1]], axis=1)

    return (
        layer_out,
        x_grad,
        norms[0],
        g_query,
        g_key,
        g_value,
        g_forget,
        g_bias,
        g_output,
        norms[1],
        g_gate,
        g_up,
        g_down,
        clip_factor,
        clipped_query,
        clipped_key,
    )


def pick_body(mesh):
    dp, tensor = mesh.shape["dp"], mesh.shape["tensor"]

    def body(*args):
        rows, heads = args[0].shape[0], args[7].shape[0]
        depth = dp // 4
        paired = (
            tensor == 2
            and dp % 4 == 0
            and depth & (depth - 1) == 0
            and rows == BLOCK
            and heads % 4 == 0
        )
        return (paired_body if paired else general_body)(*args)

    return body
def solution(mesh):
    return jax.shard_map(
        pick_body(mesh),
        mesh=mesh,
        in_specs=(
            P(("dp", "tensor"), None),
            P("dp", None),
            P("dp"),
            P("dp", "tensor"),
            P("dp", "tensor"),
            P("dp", "tensor"),
            P("dp", "tensor"),
            P("tensor"),
            P("dp", "tensor"),
            P("dp"),
            P("dp", "tensor"),
            P("dp", "tensor"),
            P("dp", "tensor"),
            P("tensor"),
            P(("dp", "tensor"), None),
        ),
        out_specs=(
            P(("dp", "tensor"), None),
            P(("dp", "tensor"), None),
            P("tensor"),
            P("dp", "tensor"),
            P("dp", "tensor"),
            P("dp", "tensor"),
            P("dp", "tensor"),
            P("tensor"),
            P("dp", "tensor"),
            P("tensor"),
            P("dp", "tensor"),
            P("dp", "tensor"),
            P("dp", "tensor"),
            P("tensor"),
            P("dp", "tensor"),
            P("dp", "tensor"),
        ),
        check_vma=False,
    )
```

```python
import math
from functools import partial

import jax
import jax.numpy as jnp
from jax import lax
from jax.experimental import pallas as pl
from jax.experimental.pallas import tpu as pltpu
from jax.sharding import PartitionSpec as P

HEAD_DIM = 64
BLOCK = 256
LANES = 128
EPSILON = 1e-06
HIGHEST = lax.Precision.HIGHEST
NEGATIVE = -1e30
F32 = jnp.float32
BF16 = jnp.bfloat16
def combined_all(part, axis, combine):
    gathered = jax.tree.map(lambda a: lax.all_gather(a, axis), part)

    def take(source):
        return jax.tree.map(lambda a: lax.dynamic_index_in_dim(a, source, 0, False), gathered)

    return lax.fori_loop(
        1, lax.axis_size(axis), lambda source, state: combine(state, take(source)), take(0)
    )


def contract_last(left_op, right_op):
    return lax.dot_general(
        left_op, right_op, (((1,), (1,)), ((), ())), preferred_element_type=jnp.float32
    )


def contract_first(left_op, right_op):
    return lax.dot_general(
        left_op, right_op, (((0,), (0,)), ((), ())), preferred_element_type=jnp.float32
    )


def block_terms(q_blk, keys_all, cumul, seg_row, offset, rows_blk):
    positions = jnp.arange(keys_all.shape[0], dtype=jnp.int32)
    q_pos = offset + jnp.arange(rows_blk, dtype=jnp.int32)
    allowed = (seg_row[:, None] == seg_row[None, :]) & (
        q_pos[:, None] // BLOCK >= positions[None, :] // BLOCK
    )
    signs = jnp.where(positions[None, :] <= q_pos[:, None], 1.0, -1.0).astype(jnp.float32)
    raw_blk = jnp.einsum("qhe,khe->hqk", q_blk, keys_all, preferred_element_type=jnp.float32) * (
        1.0 / math.sqrt(HEAD_DIM)
    )
    differ = cumul.T[:, :, None] - cumul.T[:, None, :]
    scores = jnp.where(allowed[None], raw_blk + signs[None] * differ, NEGATIVE)
    return (raw_blk, scores, allowed, signs)


def combine(former, latter):
    return (
        jnp.maximum(former[0], latter[0]),
        former[1] + latter[1],
        former[2] + latter[2],
        former[3] + latter[3],
    )


def general_body(
    layer_in,
    segment_ids,
    norm1_gain,
    w_query,
    w_key,
    w_value,
    w_forget,
    forget_bias,
    w_output,
    norm2_gain,
    w_gate,
    w_up,
    w_down,
    clip_tau,
    out_grad,
):
    gain_one, wq_all, wk_all, wv_all, wf_all, wo_all, gain_two, wg_all, wu_all, wd_all = (
        lax.all_gather(norm1_gain, "dp", axis=0, tiled=True),
        lax.all_gather(w_query, "dp", axis=0, tiled=True),
        lax.all_gather(w_key, "dp", axis=0, tiled=True),
        lax.all_gather(w_value, "dp", axis=0, tiled=True),
        lax.all_gather(w_forget, "dp", axis=0, tiled=True),
        lax.all_gather(w_output, "dp", axis=0, tiled=True),
        lax.all_gather(norm2_gain, "dp", axis=0, tiled=True),
        lax.all_gather(w_gate, "dp", axis=0, tiled=True),
        lax.all_gather(w_up, "dp", axis=0, tiled=True),
        lax.all_gather(w_down, "dp", axis=0, tiled=True),
    )
    gain_one = gain_one.astype(jnp.float32)
    gain_two = gain_two.astype(jnp.float32)
    tok_local = layer_in.shape[0]
    tokens = tok_local * lax.axis_size("tensor")
    heads_loc = forget_bias.shape[0]
    row_start = lax.axis_index("tensor") * tok_local
    seg_row = segment_ids[0]
    factor = 1.0 / math.sqrt(HEAD_DIM)
    rows_full = lax.all_gather(layer_in, "tensor", axis=0, tiled=True).astype(jnp.float32)
    scale_one = lax.rsqrt(jnp.mean(rows_full * rows_full, axis=1, keepdims=True) + EPSILON)
    unit_one = rows_full * scale_one
    normed_one = (unit_one * gain_one).astype(jnp.bfloat16)
    queries = (
        jnp.dot(normed_one, wq_all, preferred_element_type=jnp.float32)
        .astype(jnp.bfloat16)
        .reshape(tokens, heads_loc, HEAD_DIM)
    )
    keys_all = (
        jnp.dot(normed_one, wk_all, preferred_element_type=jnp.float32)
        .astype(jnp.bfloat16)
        .reshape(tokens, heads_loc, HEAD_DIM)
    )
    values_all = (
        jnp.dot(normed_one, wv_all, preferred_element_type=jnp.float32)
        .astype(jnp.bfloat16)
        .reshape(tokens, heads_loc, HEAD_DIM)
    )
    logits = jnp.dot(normed_one, wf_all, preferred_element_type=jnp.float32) + forget_bias
    cumul = jnp.cumsum(jax.nn.log_sigmoid(logits), axis=0)
    rows_blk = min(512, tokens)
    blocks = tokens // rows_blk
    numbers = jnp.arange(blocks, dtype=jnp.int32)

    def forward_block(number):
        offset = number * rows_blk
        raw_blk, scores, allowed, signs = block_terms(
            queries, keys_all, cumul, seg_row, offset, rows_blk
        )
        top_blk = jnp.max(jnp.where(allowed[None], raw_blk, NEGATIVE), axis=(1, 2))
        row_peak = jnp.max(scores, axis=2, keepdims=True)
        expo_blk = jnp.exp(scores - row_peak)
        totals = jnp.sum(expo_blk, axis=2, keepdims=True)
        weights = (expo_blk / totals).astype(jnp.bfloat16)
        mixed_out = jnp.einsum(
            "hqk,khe->qhe", weights, values_all, preferred_element_type=jnp.float32
        ).astype(jnp.bfloat16)
        return (mixed_out, (row_peak + jnp.log(totals))[:, :, 0], top_blk)

    mixed_out, log_sums, top_blk = lax.map(forward_block, numbers)
    mixed_flat = mixed_out.reshape(tokens, heads_loc * HEAD_DIM)
    maxima = jnp.max(top_blk, axis=0)
    attn_part = contract_last(mixed_flat, wo_all)
    resid_full = rows_full + lax.psum(attn_part.astype(jnp.bfloat16), "tensor").astype(jnp.float32)
    scale_full = lax.rsqrt(jnp.mean(resid_full * resid_full, axis=1, keepdims=True) + EPSILON)
    normed_two = (resid_full * scale_full * gain_two).astype(jnp.bfloat16)
    resid_part = lax.dynamic_slice_in_dim(resid_full, row_start, tok_local, 0)
    scale_two = lax.dynamic_slice_in_dim(scale_full, row_start, tok_local, 0)
    gate_pre = jnp.dot(normed_two, wg_all, preferred_element_type=jnp.float32)
    up_pre = jnp.dot(normed_two, wu_all, preferred_element_type=jnp.float32)
    gate_sig = jax.nn.sigmoid(gate_pre)
    gate_act = gate_pre * gate_sig
    hidden = (gate_act * up_pre).astype(jnp.bfloat16)
    ffn_part = lax.psum_scatter(
        contract_last(hidden, wd_all).astype(jnp.bfloat16),
        "tensor",
        scatter_dimension=0,
        tiled=True,
    ).astype(jnp.float32)
    layer_out = (resid_part + ffn_part).astype(jnp.bfloat16)
    grad_full = lax.all_gather(out_grad, "tensor", axis=0, tiled=True)
    grad_hidden = jnp.dot(grad_full, wd_all, preferred_element_type=jnp.float32)
    grad_gate = (grad_hidden * up_pre * gate_sig * (1.0 + gate_pre * (1.0 - gate_sig))).astype(
        jnp.bfloat16
    )
    grad_up = (grad_hidden * gate_act).astype(jnp.bfloat16)
    g_down = contract_first(grad_full, hidden)
    g_gate = contract_first(normed_two, grad_gate)
    g_up = contract_first(normed_two, grad_up)
    grad_normed = contract_last(grad_gate, wg_all) + contract_last(grad_up, wu_all)
    grad_two = lax.psum_scatter(
        grad_normed.astype(jnp.bfloat16), "tensor", scatter_dimension=0, tiled=True
    ).astype(jnp.float32)
    unit_two = resid_part * scale_two
    inner_two = jnp.mean(unit_two * gain_two * grad_two, axis=1, keepdims=True)
    norm2_part = jnp.sum(grad_two * unit_two, axis=0)
    grad_resid = out_grad.astype(jnp.float32) + scale_two * (
        gain_two * grad_two - unit_two * inner_two
    )
    grad_attn = lax.all_gather(grad_resid.astype(jnp.bfloat16), "tensor", axis=0, tiled=True)
    g_output = contract_first(grad_attn, mixed_flat)
    grad_mixed = jnp.dot(grad_attn, wo_all, preferred_element_type=jnp.float32).astype(jnp.bfloat16)
    grad_mixed = grad_mixed.reshape(blocks, rows_blk, heads_loc, HEAD_DIM)

    def backward_block(carried, block_in):
        key_acc, value_acc, column_acc = carried
        number, log_blk, grad_blk = block_in
        offset = number * rows_blk
        raw_blk, scores, allowed, signs = block_terms(
            queries, keys_all, cumul, seg_row, offset, rows_blk
        )
        prob_blk = jnp.exp(scores - log_blk[:, :, None])
        weights = prob_blk.astype(jnp.bfloat16)
        grad_prob = jnp.einsum(
            "qhe,khe->hqk", grad_blk, values_all, preferred_element_type=jnp.float32
        )
        inner = jnp.sum(prob_blk * grad_prob, axis=2, keepdims=True)
        grad_scores = (prob_blk * (grad_prob - inner)).astype(jnp.bfloat16)
        value_acc = value_acc + jnp.einsum(
            "hqk,qhe->khe", weights, grad_blk, preferred_element_type=jnp.float32
        )
        key_acc = key_acc + jnp.einsum(
            "hqk,qhe->khe", grad_scores, queries, preferred_element_type=jnp.float32
        )
        grad_query = (
            jnp.einsum("hqk,khe->qhe", grad_scores, keys_all, preferred_element_type=jnp.float32)
            * factor
        ).astype(jnp.bfloat16)
        signed = grad_scores.astype(jnp.float32) * signs[None]
        column_acc = column_acc - jnp.sum(signed, axis=1).T
        return ((key_acc, value_acc, column_acc), (grad_query, jnp.sum(signed, axis=2).T))

    start_acc = (
        jnp.zeros((tokens, heads_loc, HEAD_DIM), jnp.float32),
        jnp.zeros((tokens, heads_loc, HEAD_DIM), jnp.float32),
        jnp.zeros((tokens, heads_loc), jnp.float32),
    )
    (key_acc, value_acc, column_acc), (grad_query, row_parts) = lax.scan(
        backward_block, start_acc, (numbers, log_sums, grad_mixed)
    )
    grad_q = grad_query.reshape(tokens, heads_loc * HEAD_DIM)
    grad_k = (key_acc * factor).astype(jnp.bfloat16).reshape(tokens, heads_loc * HEAD_DIM)
    grad_v = value_acc.astype(jnp.bfloat16).reshape(tokens, heads_loc * HEAD_DIM)
    grad_cum = row_parts.reshape(tokens, heads_loc) + column_acc
    grad_logs = jnp.cumsum(grad_cum[::-1], axis=0)[::-1]
    grad_logit = grad_logs * jax.nn.sigmoid(-logits)
    g_bias = jnp.sum(grad_logit, axis=0)
    g_forget = jnp.einsum(
        "td,th->dh", normed_one, grad_logit, precision=HIGHEST, preferred_element_type=jnp.float32
    )
    g_query = contract_first(normed_one, grad_q)
    g_key = contract_first(normed_one, grad_k)
    g_value = contract_first(normed_one, grad_v)
    grad_one = (
        contract_last(grad_q, wq_all)
        + contract_last(grad_k, wk_all)
        + contract_last(grad_v, wv_all)
    )
    grad_one = grad_one + jnp.einsum(
        "th,dh->td", grad_logit, wf_all, precision=HIGHEST, preferred_element_type=jnp.float32
    )
    weighted = gain_one * grad_one
    grad_rows_one = scale_one * (
        weighted - unit_one * jnp.mean(unit_one * weighted, axis=1, keepdims=True)
    )
    norm1_part = jnp.sum(grad_one * unit_one, axis=0)
    grad_input, g_norm1_part, g_norm2_part = (
        lax.psum_scatter(
            grad_rows_one.astype(jnp.bfloat16), "tensor", scatter_dimension=0, tiled=True
        ).astype(jnp.float32),
        lax.psum_scatter(
            norm1_part.astype(jnp.bfloat16), "tensor", scatter_dimension=0, tiled=True
        ).astype(jnp.float32),
        lax.psum_scatter(
            norm2_part.astype(jnp.bfloat16), "tensor", scatter_dimension=0, tiled=True
        ).astype(jnp.float32),
    )
    x_grad = (grad_resid + grad_input).astype(jnp.bfloat16)
    g_query, g_key, g_value, g_forget, g_output, g_gate, g_up, g_down = (
        lax.psum_scatter(
            g_query.astype(jnp.bfloat16), "dp", scatter_dimension=0, tiled=True
        ).astype(jnp.float32),
        lax.psum_scatter(g_key.astype(jnp.bfloat16), "dp", scatter_dimension=0, tiled=True).astype(
            jnp.float32
        ),
        lax.psum_scatter(
            g_value.astype(jnp.bfloat16), "dp", scatter_dimension=0, tiled=True
        ).astype(jnp.float32),
        lax.psum_scatter(
            g_forget.astype(jnp.bfloat16), "dp", scatter_dimension=0, tiled=True
        ).astype(jnp.float32),
        lax.psum_scatter(
            g_output.astype(jnp.bfloat16), "dp", scatter_dimension=0, tiled=True
        ).astype(jnp.float32),
        lax.psum_scatter(g_gate.astype(jnp.bfloat16), "dp", scatter_dimension=0, tiled=True).astype(
            jnp.float32
        ),
        lax.psum_scatter(g_up.astype(jnp.bfloat16), "dp", scatter_dimension=0, tiled=True).astype(
            jnp.float32
        ),
        lax.psum_scatter(g_down.astype(jnp.bfloat16), "dp", scatter_dimension=0, tiled=True).astype(
            jnp.float32
        ),
    )
    maxima, g_bias, g_norm1, g_norm2 = combined_all(
        (maxima, g_bias, g_norm1_part, g_norm2_part), "dp", combine
    )
    clip_factor = jnp.minimum(1.0, clip_tau / jnp.maximum(maxima, 1.0))
    columns = jnp.repeat(jnp.sqrt(clip_factor), HEAD_DIM)
    clipped_query = (w_query.astype(jnp.float32) * columns[None, :]).astype(jnp.bfloat16)
    clipped_key = (w_key.astype(jnp.float32) * columns[None, :]).astype(jnp.bfloat16)
    return (
        layer_out,
        x_grad,
        g_norm1,
        g_query,
        g_key,
        g_value,
        g_forget,
        g_bias,
        g_output,
        g_norm2,
        g_gate,
        g_up,
        g_down,
        clip_factor,
        clipped_query,
        clipped_key,
    )


def dot_nt(left, right):
    return lax.dot_general(left, right, (((1,), (1,)), ((), ())), preferred_element_type=F32)


def dot_nn(left, right):
    return lax.dot_general(left, right, (((1,), (0,)), ((), ())), preferred_element_type=F32)


def dot_tn(left, right):
    return lax.dot_general(left, right, (((0,), (0,)), ((), ())), preferred_element_type=F32)


def attend_kernel(y_ref, qkv_ref, aux_ref, *refs):
    o_ref, inv_ref, exp_ref, top_ref = refs[-4:]
    y = y_ref[0]
    starts = (pl.multiple_of(y * BLOCK, BLOCK), pl.multiple_of((1 - y) * BLOCK, BLOCK))
    lane = lax.broadcasted_iota(jnp.int32, (1, LANES), 1)
    first = lane < HEAD_DIM
    aux = [aux_ref[0, :, pl.ds(start, BLOCK)] for start in starts]
    aux_col = [a.T for a in aux]
    q_blk = [qkv_ref[pl.ds(s, BLOCK), 0:LANES] * 0.125 for s in starts]
    k_blk = [qkv_ref[pl.ds(s, BLOCK), LANES : 2 * LANES] for s in starts]
    v_blk = [qkv_ref[pl.ds(s, BLOCK), 2 * LANES : 3 * LANES] for s in starts]
    same = {}
    for i, j in ((0, 0), (1, 0), (1, 1)):
        same[i, j] = aux_col[i][:, 2:3] == aux[j][2:3, :]
    tops = []
    results = [[], []]
    for head in range(2):
        mine = first if head == 0 else jnp.logical_not(first)
        top = None
        v_ext = [jnp.where(mine, v, jnp.ones_like(v)) for v in v_blk]
        k_head = [jnp.where(mine, k, jnp.zeros_like(k)) for k in k_blk]
        for i in range(2):
            scores = []
            for j in range(i + 1):
                raw = dot_nt(q_blk[i], k_head[j])
                seen = jnp.where(same[i, j], raw, NEGATIVE)
                high = jnp.max(seen, axis=0, keepdims=True)
                top = high if top is None else jnp.maximum(top, high)
                differ = aux_col[i][:, head : head + 1] - aux[j][head : head + 1, :]
                scores.append(seen - jnp.abs(differ))
            peak = jnp.max(scores[0], axis=1, keepdims=True)
            if i == 1:
                peak = jnp.maximum(peak, jnp.max(scores[1], axis=1, keepdims=True))
            acc = None
            for j in range(i + 1):
                weights = jnp.exp(scores[j] - peak).astype(BF16)
                exp_ref[0, 0, head, :, (i + j) * BLOCK : (i + j + 1) * BLOCK] = weights
                part = dot_nn(weights, v_ext[j])
                acc = part if acc is None else acc + part
            results[i].append(acc)
        tops.append(jnp.maximum(top[:, :LANES], top[:, LANES:]))
    for i in range(2):
        one, two = results[i]
        total = pltpu.roll(jnp.where(first, two, one), HEAD_DIM, 1)
        inverse = 1.0 / total
        inv_ref[pl.ds(starts[i], BLOCK), :] = inverse
        o_ref[pl.ds(starts[i], BLOCK), :] = (jnp.where(first, one, two) * inverse).astype(BF16)
    row = lax.broadcasted_iota(jnp.int32, (8, LANES), 0)
    top_ref[0, 0] = jnp.where(row == 0, tops[0], tops[1])


def attend(y_index, qkv, aux, packs, pairs, pack, kept=()):
    rows = qkv.shape[0] // packs
    wide = 3 * LANES
    grid_spec = pltpu.PrefetchScalarGridSpec(
        num_scalar_prefetch=1,
        grid=(pairs,),
        in_specs=[
            pl.BlockSpec((rows, wide), lambda h, y: (pack, h)),
            pl.BlockSpec((1, 8, rows), lambda h, y: (h, 0, pack)),
        ]
        + [pl.BlockSpec(memory_space=pl.ANY) for _ in kept],
        out_specs=[
            pl.BlockSpec((rows, LANES), lambda h, y: (0, h)),
            pl.BlockSpec((rows, LANES), lambda h, y: (pack, h)),
            pl.BlockSpec((1, 1, 2, BLOCK, 3 * BLOCK), lambda h, y: (pack, h, 0, 0, 0)),
            pl.BlockSpec((1, 1, 8, LANES), lambda h, y: (0, h, 0, 0)),
        ],
    )
    return pl.pallas_call(
        attend_kernel,
        grid_spec=grid_spec,
        out_shape=(
            jax.ShapeDtypeStruct((rows, pairs * LANES), BF16),
            jax.ShapeDtypeStruct((packs * rows, pairs * LANES), F32),
            jax.ShapeDtypeStruct((packs, pairs, 2, BLOCK, 3 * BLOCK), BF16),
            jax.ShapeDtypeStruct((1, pairs, 8, LANES), F32),
        ),
        input_output_aliases={3: 1, 4: 2} if kept else {},
        cost_estimate=pl.CostEstimate(
            flops=pairs * 2 * 6 * BLOCK * BLOCK * LANES * 2,
            bytes_accessed=10_000_000,
            transcendentals=pairs * 2 * 3 * BLOCK * BLOCK,
        ),
        name="attend",
    )(y_index, qkv, aux, *kept)


def attend_back_kernel(
    pairs, y_ref, qkv_ref, do_ref, inv_ref, exp_ref, aux_ref, dqkv_ref, split_ref
):
    y = y_ref[0]
    starts = (pl.multiple_of(y * BLOCK, BLOCK), pl.multiple_of((1 - y) * BLOCK, BLOCK))
    lane = lax.broadcasted_iota(jnp.int32, (1, LANES), 1)
    first = lane < HEAD_DIM
    ones = jnp.ones((8, BLOCK), BF16)
    lower = lax.broadcasted_iota(jnp.int32, (BLOCK, BLOCK), 1) <= lax.broadcasted_iota(
        jnp.int32, (BLOCK, BLOCK), 0
    )
    q_blk = [qkv_ref[pl.ds(s, BLOCK), 0:LANES] * 0.125 for s in starts]
    k_blk = [qkv_ref[pl.ds(s, BLOCK), LANES : 2 * LANES] for s in starts]
    v_blk = [qkv_ref[pl.ds(s, BLOCK), 2 * LANES : 3 * LANES] for s in starts]
    inv_blk = [inv_ref[pl.ds(s, BLOCK), :] for s in starts]
    do_blk = [
        (do_ref[pl.ds(s, BLOCK), :].astype(F32) * inv).astype(BF16)
        for s, inv in zip(starts, inv_blk)
    ]
    dq, dk, dv, dc = ([], []), ([], []), ([], []), ([], [])
    for head in range(2):
        mine = first if head == 0 else jnp.logical_not(first)
        v_head = [jnp.where(mine, v, jnp.zeros_like(v)) for v in v_blk]
        dk_acc, dv_acc, row_acc, col_acc = [None] * 2, [None] * 2, [None] * 2, [None] * 2
        for i in range(2):
            expos, probs, inner = [], [], None
            inv_col = inv_blk[i][:, head * HEAD_DIM : head * HEAD_DIM + 1]
            for j in range(i + 1):
                expo = exp_ref[0, 0, head, :, (i + j) * BLOCK : (i + j + 1) * BLOCK]
                grad_prob = dot_nt(do_blk[i], v_head[j])
                wide = expo.astype(F32)
                part = jnp.sum(wide * grad_prob, axis=1, keepdims=True)
                inner = part if inner is None else inner + part
                expos.append((expo, wide))
                probs.append(grad_prob)
            inner = inner * inv_col
            dq_acc = None
            for j in range(i + 1):
                expo, wide = expos[j]
                grad_score = wide * (probs[j] - inner)
                low = grad_score.astype(BF16)
                if i == j:
                    signed = jnp.where(lower, low, -low)
                else:
                    signed = low
                part = dot_nn(low, k_blk[j])
                dq_acc = part if dq_acc is None else dq_acc + part
                part = dot_tn(low, q_blk[i])
                dk_acc[j] = part if dk_acc[j] is None else dk_acc[j] + part
                part = dot_tn(expo, do_blk[i])
                dv_acc[j] = part if dv_acc[j] is None else dv_acc[j] + part
                part = dot_nt(ones, signed)
                row_acc[i] = part if row_acc[i] is None else row_acc[i] + part
                part = dot_nn(ones, signed)
                col_acc[j] = part if col_acc[j] is None else col_acc[j] + part
            dq[i].append(dq_acc)
        for j in range(2):
            dk[j].append(dk_acc[j])
            dv[j].append(dv_acc[j])
            dc[j].append(row_acc[j] - col_acc[j])
    for i in range(2):
        rows = pl.ds(starts[i], BLOCK)
        dqkv_ref[rows, 0:LANES] = (jnp.where(first, *dq[i]) * 0.125).astype(BF16)
        dqkv_ref[rows, LANES : 2 * LANES] = jnp.where(first, *dk[i]).astype(BF16)
        dqkv_ref[rows, 2 * LANES : 3 * LANES] = jnp.where(first, *dv[i]).astype(BF16)

    row = lax.broadcasted_iota(jnp.int32, (8, BLOCK), 0)
    until = jnp.where(lower, 1.0, 0.0).astype(BF16)
    d_cum = [jnp.where(row == 0, *dc[i]) for i in range(2)]
    ends = jnp.sum(d_cum[1], axis=1, keepdims=True)
    pair = pl.program_id(1)
    spot = lax.broadcasted_iota(jnp.int32, (8, LANES), 0)
    place = jnp.where(spot < 2, 2 * pair + spot, 2 * pairs + 2 * pair + spot - 2)
    hit = (lax.broadcasted_iota(jnp.int32, (8, LANES), 1) == place) & (spot < 4)
    hit = jnp.where(hit, 1.0, 0.0).astype(F32)

    @pl.when(pair == 0)
    def _():
        split_ref[...] = jnp.zeros_like(split_ref)

    for i in range(2):
        rows = pl.ds(starts[i], BLOCK)
        high = d_cum[i].astype(BF16).astype(F32)
        rest = d_cum[i] - high
        middle = rest.astype(BF16).astype(F32)
        low = pltpu.roll(rest - middle, 4, 0)
        parts = jnp.where(row < 4, pltpu.roll(middle, 2, 0), jnp.where(row < 6, low, 0.0))
        parts = jnp.where(row < 2, high, parts).astype(BF16)
        sums = dot_nn(parts, until)
        back = sums + pltpu.roll(sums, 6, 0) + pltpu.roll(sums, 4, 0)
        if i == 0:
            back = back + ends
        logit = pltpu.roll(aux_ref[0, :, rows], 4, 0)
        grad = back * jax.nn.sigmoid(-logit)
        high = grad.astype(BF16).astype(F32)
        rest = pltpu.roll((grad - high).astype(BF16).astype(F32), 2, 0)
        both = jnp.where(row < 2, high, jnp.where(row < 4, rest, 0.0))
        old = split_ref[rows, :].astype(F32)
        split_ref[rows, :] = (old + dot_tn(both, hit)).astype(BF16)


def attend_back(y_index, qkv, d_out, inverse, expos, aux, packs, pairs):
    rows = qkv.shape[0] // packs
    wide = 3 * LANES
    grid_spec = pltpu.PrefetchScalarGridSpec(
        num_scalar_prefetch=1,
        grid=(packs, pairs),
        in_specs=[
            pl.BlockSpec((rows, wide), lambda p, h, y: (p, h)),
            pl.BlockSpec((rows, LANES), lambda p, h, y: (p, h)),
            pl.BlockSpec((rows, LANES), lambda p, h, y: (p, h)),
            pl.BlockSpec((1, 1, 2, BLOCK, 3 * BLOCK), lambda p, h, y: (p, h, 0, 0, 0)),
            pl.BlockSpec((1, 8, rows), lambda p, h, y: (h, 0, p)),
        ],
        out_specs=[
            pl.BlockSpec((rows, wide), lambda p, h, y: (p, h)),
            pl.BlockSpec((rows, LANES), lambda p, h, y: (p, 0)),
        ],
    )
    return pl.pallas_call(
        partial(attend_back_kernel, pairs),
        grid_spec=grid_spec,
        out_shape=(
            jax.ShapeDtypeStruct((packs * rows, pairs * wide), BF16),
            jax.ShapeDtypeStruct((packs * rows, LANES), BF16),
        ),
        cost_estimate=pl.CostEstimate(
            flops=packs * pairs * 2 * 18 * BLOCK * BLOCK * LANES * 2,
            bytes_accessed=20_000_000,
            transcendentals=0,
        ),
        name="attend_back",
    )(y_index, qkv, d_out, inverse, expos, aux)


def assemble_kernel(core_ref, low_ref, got_low_ref, high_ref, got_high_ref, *outs):
    core = core_ref[0]
    rows = outs[0].shape[0]
    own = pl.ds(pl.multiple_of(core * rows, 8), rows)
    count = outs[0].shape[1] // (2 * LANES)
    middle = low_ref.shape[1]
    spots = [[3 * p + which for p in range(count)] for which in range(3)]
    spots.append([3 * count + 1 + p for p in range(count)])
    for out, chosen in zip(outs, spots):
        for p, spot in enumerate(chosen):
            start = spot * LANES
            mine_ref, got_ref = low_ref, got_low_ref
            if start >= middle:
                start -= middle
                mine_ref, got_ref = high_ref, got_high_ref
            lanes = slice(start, start + LANES)
            mine, got = mine_ref[own, lanes], got_ref[:, lanes].astype(F32)
            left = slice(p * LANES, (p + 1) * LANES)
            right = slice((count + p) * LANES, (count + p + 1) * LANES)
            out[:, left] = jnp.where(core == 0, mine, got)
            out[:, right] = jnp.where(core == 0, got, mine)


def assemble(core, low, got_low, high, got_high, pairs):
    shape = jax.ShapeDtypeStruct((got_low.shape[0], 2 * pairs * LANES), F32)
    spec = pl.BlockSpec(memory_space=pltpu.VMEM)
    return pl.pallas_call(
        assemble_kernel,
        in_specs=[pl.BlockSpec(memory_space=pltpu.SMEM)] + [spec] * 4,
        out_specs=[spec] * 4,
        out_shape=[shape] * 4,
        name="assemble",
    )(core.astype(jnp.int32).reshape(1), low, got_low, high, got_high)


class Gathering:
    def __init__(self, at, shard):
        self.at, self.step, self.half = at, 1, at.depth
        self.whole = None
        self.waiting = [(shard, 0, 0)]
        self.send(shard, shard)

    def store(self, *others):
        for part, step, side in self.waiting:
            if others:
                part = after(part, *others)
            if self.whole is None:
                self.whole = jnp.zeros((2 * self.half,) + part.shape, part.dtype)
                if others:
                    self.whole = after(self.whole, *others)
            start = (self.at.block_of(step), side, 0, 0)
            self.whole = lax.dynamic_update_slice(self.whole, part[None], start)
        self.waiting = []

    def send(self, up, down):
        if self.step == self.half:
            up, down = up[:1], down[1:]
        self.came = (self.at.ring(up, 1), self.at.ring(down, -1))

    def take(self, *others):
        up, down = after_all(self.came, *others)
        side = 1 if self.step == self.half else 0
        self.waiting += [(up, -self.step, 0), (down, self.step, side)]
        return up, down

    def advance(self, *others):
        up, down = self.take(*others)
        self.step += 1
        self.send(up, down)
        return up, down

    def finish(self, *others):
        self.take(*others)
        self.store()
        return self.whole.reshape(-1, self.whole.shape[-1])


class Reduction:
    def __init__(self, at, grad, *others):
        self.at, self.step, self.half = at, 1, at.depth
        count = 2 * at.depth
        self.blocks = grad.reshape(count, 2, grad.shape[0] // (2 * count), grad.shape[1])
        far = self.own(self.half)
        self.sent = after_all((far[:1], far[1:]), *others) if others else (far[:1], far[1:])
        self.send()

    def own(self, step):
        start = (self.at.block_of(step), 0, 0, 0)
        return lax.dynamic_slice(self.blocks, start, (1,) + self.blocks.shape[1:])[0]

    def send(self):
        self.came = (self.at.ring(self.sent[0], 1), self.at.ring(self.sent[1], -1))

    def advance(self, *others):
        up, down = after_all(self.came, *others)
        ahead, behind = self.own(self.half - self.step), self.own(self.step - self.half)
        if self.step == 1:
            first = (ahead[:1].astype(F32) + up.astype(F32)).astype(BF16)
            second = (behind[1:].astype(F32) + down.astype(F32)).astype(BF16)
            up = jnp.concatenate([first, ahead[1:]], axis=0)
            down = jnp.concatenate([behind[:1], second], axis=0)
        else:
            up = (ahead.astype(F32) + up.astype(F32)).astype(BF16)
            down = (behind.astype(F32) + down.astype(F32)).astype(BF16)
        self.sent = (up, down)
        self.step += 1
        self.send()
        return up, down

    def finish(self, *others):
        up, down = after_all(self.came, *others)
        total = self.own(0).astype(F32) + up.astype(F32) + down.astype(F32)
        return total.reshape(-1, total.shape[-1])


class Place:
    def __init__(self):
        self.dp = lax.axis_size("dp")
        self.depth = self.dp // 4
        index = lax.axis_index("dp")
        self.core = index % 2
        self.x = (index // 2) % 2
        self.z = index // 4
        self.y = lax.axis_index("tensor")

    def swap_core(self, value):
        return lax.ppermute(value, "dp", [(i, i ^ 1) for i in range(self.dp)])

    def swap_y(self, value):
        return lax.ppermute(value, "tensor", [(0, 1), (1, 0)])

    def ring(self, value, step):
        spots = [4 * z for z in range(self.depth)]
        spots += [4 * z + 2 for z in reversed(range(self.depth))]
        count = len(spots)
        pairs = [
            (spots[r] + core, spots[(r + step) % count] + core)
            for r in range(count)
            for core in (0, 1)
        ]
        return lax.ppermute(value, "dp", pairs)

    def block_of(self, step):
        count = 2 * self.depth
        spot = (jnp.where(self.x == 0, self.z, count - 1 - self.z) + step + count) % count
        return jnp.where(spot < self.depth, 2 * spot, 2 * (count - 1 - spot) + 1)

    def sum_plane(self, value, rings, combine):
        step = 2
        rings = list(rings)
        while step < self.dp:
            value = combine(
                value, lax.ppermute(value, "dp", [(i, i ^ step) for i in range(self.dp)])
            )
            if rings:
                value = after(value, *rings.pop(0).advance(value))
            step *= 2
        return value

    def by_core(self, mine, other, axis):
        return jnp.where(
            self.core == 0,
            jnp.concatenate([mine, other], axis=axis),
            jnp.concatenate([other, mine], axis=axis),
        )

    def core_columns(self, weights):
        half = [w.shape[1] // 2 for w in weights]
        keep = [
            lax.dynamic_slice_in_dim(w, self.core * h, h, 1) for w, h in zip(weights, half)
        ]
        give = [
            lax.dynamic_slice_in_dim(w, (1 - self.core) * h, h, 1) for w, h in zip(weights, half)
        ]
        return keep, give

    def finish_grad(self, own):
        rows = own.shape[0] // 2
        keep = lax.dynamic_slice_in_dim(own, self.core * rows, rows, 0)
        return keep, self.swap_core(self.theirs(own)).astype(F32)

    def theirs(self, own):
        rows = own.shape[0] // 2
        return lax.dynamic_slice_in_dim(own, (1 - self.core) * rows, rows, 0).astype(BF16)

    def join(self, rows, near):
        both = jnp.concatenate([rows, near], axis=0)
        return jnp.concatenate([both, self.swap_core(both)], axis=0)

    def meet_core(self, left, right, dot):
        half = left.shape[0] // 2
        given = dot(left[half:], right).astype(BF16)
        got = self.swap_core(given)
        part = dot(after(left, given)[:half], right)
        return part, got


def after(value, *others):
    return lax.optimization_barrier((value,) + others)[0]


def after_all(values, *others):
    return lax.optimization_barrier(tuple(values) + others)[: len(values)]


def interleave(parts):
    starts = range(0, parts[0].shape[1], LANES)
    return jnp.concatenate([p[:, s : s + LANES] for s in starts for p in parts], axis=1)


def split_low(value):
    high = value.astype(BF16)
    return high, (value - high.astype(F32)).astype(BF16)


def paired_body(
    layer_in,
    segment_ids,
    norm1_gain,
    w_query,
    w_key,
    w_value,
    w_forget,
    forget_bias,
    w_output,
    norm2_gain,
    w_gate,
    w_up,
    w_down,
    clip_tau,
    out_grad,
):
    at = Place()
    rows_loc = layer_in.shape[0]
    pack = 2 * rows_loc
    width = layer_in.shape[1]
    heads = forget_bias.shape[0] // 2
    pairs = heads // 2
    y_index = at.y.astype(jnp.int32).reshape(1)
    d_rows = norm1_gain.shape[0]

    units = w_gate.shape[1] // 2
    keep, give = at.core_columns([w_query, w_key, w_value, w_output, w_forget])
    gains = jnp.stack([norm1_gain, norm2_gain], axis=1)
    pad = jnp.zeros((d_rows, LANES - 2 * heads - 2), BF16)

    def first_part(part):
        return jnp.concatenate(
            [interleave(part[:3]), part[4], part[4], gains, pad, part[3]], axis=1
        )

    attn_shard = at.by_core(first_part(keep)[None], at.swap_core(first_part(give))[None], 0)
    rows_near = at.swap_y(layer_in)
    qkv_cols = 3 * heads * HEAD_DIM
    in_cols = qkv_cols + LANES
    attn_ring = Gathering(at, attn_shard)
    keep, give = at.core_columns(after_all((w_gate, w_up, w_down), attn_shard))
    keep, give = jnp.concatenate(keep, axis=1), jnp.concatenate(give, axis=1)
    early = attn_ring.advance(keep, give)
    ffn_shard = at.by_core(after(keep, *early)[None], at.swap_core(after(give, *early))[None], 0)
    moved = attn_ring.advance(rows_near)
    attn_ring.store()
    grad_near = at.swap_y(after(out_grad, *moved))
    def first_norm(rows):
        rows = rows.astype(F32)
        return rows, lax.rsqrt(jnp.mean(rows * rows, axis=1, keepdims=True) + EPSILON)

    rows_all = at.join(layer_in, rows_near)
    x_all, scale_all = first_norm(rows_all)
    unit_all = x_all * scale_all
    attn_ring.advance(ffn_shard, unit_all)
    unit_all = after(unit_all, *attn_ring.came)
    attn_ring.store()
    ffn_ring = Gathering(at, after(ffn_shard, *attn_ring.came))
    attn_all = attn_ring.finish()
    w_in, wo_all = attn_all[:, :in_cols], attn_all[:, in_cols:]
    grad_rows = at.join(out_grad, grad_near)
    w_qkv = w_in[:, :qkv_cols]
    small = w_in[:, qkv_cols:].T
    forget_t = small[:heads]
    gain_one = small[2 * heads : 2 * heads + 1].astype(F32)
    gain_two = small[2 * heads + 1 : 2 * heads + 2].astype(F32)

    normed_one = (unit_all * gain_one).astype(BF16)
    x_own, scale_one = first_norm(layer_in)
    unit_one = x_own * scale_one
    qkv = dot_nn(normed_one, w_in).astype(BF16)

    bias = lax.dynamic_slice_in_dim(forget_bias, at.core * heads, heads, 0)
    logits = dot_nt(after(forget_t, qkv), normed_one) + bias[:, None]
    logs = jax.nn.log_sigmoid(logits).reshape(heads, 2, 2, rows_loc)
    steps = jnp.arange(rows_loc, dtype=jnp.int32)
    upper = (steps[:, None] <= steps[None, :]).astype(F32)
    sums = jnp.einsum("hpbt,ts->hpbs", logs, upper, precision=HIGHEST)
    total = sums[..., -1:]
    later = at.y.astype(F32)
    cumul = jnp.stack(
        [sums[:, :, 0] + later * total[:, :, 1], sums[:, :, 1] + (1.0 - later) * total[:, :, 0]],
        axis=2,
    ).reshape(heads, 2 * pack)
    seg_own = after(segment_ids, *early)[0].reshape(2, rows_loc)
    seg_own = jnp.where(at.y == 0, seg_own, seg_own[::-1]).reshape(1, pack)
    seg_both = jnp.concatenate([seg_own, at.swap_core(seg_own)], axis=1).astype(F32)
    aux = jnp.concatenate(
        [
            cumul.reshape(pairs, 2, 2 * pack),
            jnp.broadcast_to(seg_both[None], (pairs, 2, 2 * pack)),
            logits.reshape(pairs, 2, 2 * pack),
            jnp.zeros((pairs, 2, 2 * pack), F32),
        ],
        axis=1,
    )
    aux = after(aux, grad_near)
    mixed_other, inverse, expos, tops_other = attend(y_index, qkv, aux, 2, pairs, 1)
    moved = ffn_ring.advance(mixed_other)

    given = dot_nt(after(mixed_other, *moved), wo_all).astype(BF16)
    got = at.swap_core(given)
    mixed_own, inverse, expos, tops = attend(
        y_index, after(qkv, given), aux, 2, pairs, 0, (inverse, expos)
    )
    tops = jnp.concatenate([tops, tops_other], axis=0)
    maxima = jnp.max(tops[:, :, :2], axis=(0, 3)).reshape(heads)
    mixed = jnp.concatenate([mixed_own, mixed_other], axis=0)
    mine = dot_nt(mixed_own, wo_all) + after(got, mixed_own).astype(F32)
    given = mine[rows_loc:].astype(BF16)
    got = at.swap_y(given)
    ffn_ring.store(given)
    moved = ffn_ring.advance(given)
    (got,) = after_all((got,), *moved)
    resid = x_own + (mine[:rows_loc] + got.astype(F32))
    scale_two = lax.rsqrt(jnp.mean(resid * resid, axis=1, keepdims=True) + EPSILON)
    unit_two = resid * scale_two
    normed_own = (unit_two * gain_two).astype(BF16)
    near = at.swap_y(normed_own)
    ffn_ring.store(normed_own)
    moved = ffn_ring.advance(normed_own)
    (near,) = after_all((near,), maxima, *moved)
    normed_two = at.join(normed_own, near)
    ffn_ring.store(near)
    ffn_all = ffn_ring.finish()
    gu_all, down_all = ffn_all[:, : 2 * units], ffn_all[:, 2 * units :]

    gate_up = dot_nn(normed_two, gu_all)
    gate_pre, up_pre = gate_up[:, :units], gate_up[:, units:]
    gate_sig = jax.nn.sigmoid(gate_pre)
    gate_act = gate_pre * gate_sig
    hidden = (gate_act * up_pre).astype(BF16)
    grad_hidden = dot_nn(grad_rows, down_all)
    grad_gate = (grad_hidden * up_pre * gate_sig * (1.0 + gate_pre * (1.0 - gate_sig))).astype(BF16)
    grad_up = (grad_hidden * gate_act).astype(BF16)
    grad_gu = jnp.concatenate([grad_gate, grad_up], axis=1)

    down_sum = Reduction(at, dot_tn(grad_rows, hidden).astype(BF16))
    part, got = at.meet_core(after(grad_gu, *down_sum.sent), gu_all, dot_nt)
    mine = part + after(got, part).astype(F32)
    given = mine[rows_loc:].astype(BF16)
    got = at.swap_y(given)
    gu_sum = Reduction(at, dot_tn(normed_two, after(grad_gu, given)).astype(BF16))
    moved = down_sum.advance(gu_sum.blocks)

    (got,) = after_all((got,), *moved)
    grad_two = mine[:rows_loc] + got.astype(F32)
    weighted = gain_two * grad_two
    inner_two = jnp.mean(unit_two * weighted, axis=1, keepdims=True)
    norm2_part = jnp.sum(grad_two * unit_two, axis=0)
    grad_resid = out_grad.astype(F32) + scale_two * (weighted - unit_two * inner_two)
    grad_own = grad_resid.astype(BF16)
    near = at.swap_y(grad_own)
    moved = gu_sum.advance(grad_own)
    out_given = dot_nt(after(hidden, *moved)[pack:], down_all).astype(BF16)
    moved = down_sum.advance(out_given)
    out_part = dot_nt(after(hidden, *moved)[:pack], down_all)
    moved = gu_sum.advance(out_part)
    (near,) = after_all((near,), *moved)
    grad_attn = at.join(grad_own, near)

    out_got = at.swap_core(after(out_given, grad_attn))
    grad_mixed = dot_nn(grad_attn, wo_all).astype(BF16)
    out_own = out_part + after(out_got, grad_mixed).astype(F32)
    out_given = out_own[rows_loc:].astype(BF16)
    out_got = at.swap_y(out_given)
    moved = down_sum.advance(out_given)
    d_qkv, d_split = attend_back(
        y_index, qkv, after(grad_mixed, *moved), inverse, expos, aux, 2, pairs
    )
    moved = gu_sum.advance(d_qkv)
    middle = 7 * LANES
    low = dot_tn(normed_one, after(d_qkv, *moved)[:, :middle]).astype(BF16)
    total_down = down_sum.finish(low)
    low_sum = Reduction(at, low, total_down)
    d_in = jnp.concatenate([d_qkv, after(d_split, *low_sum.sent)], axis=1)
    bias_part = jnp.sum(d_split.astype(F32), axis=0)
    bias_part = bias_part[:heads] + bias_part[heads : 2 * heads]
    high = jnp.concatenate(
        [dot_tn(normed_one, d_in[:, middle:]), dot_tn(grad_attn, mixed)], axis=1
    ).astype(BF16)
    given = dot_nt(after(d_in, high)[pack:], w_in).astype(BF16)
    got = at.swap_core(given)
    total_gu = gu_sum.finish(given)
    high_sum = Reduction(at, high, total_gu)
    part = dot_nt(after(d_in, *high_sum.sent)[:pack], w_in)
    mine = part + after(got, part).astype(F32)
    given = mine[rows_loc:].astype(BF16)
    got = at.swap_y(given)
    layer_out = resid + (out_own[:rows_loc] + after(out_got, low).astype(F32))
    layer_out = layer_out.astype(BF16)
    moved = low_sum.advance(layer_out, *high_sum.sent)
    moved = high_sum.advance(*moved)
    (got,) = after_all((got,), *moved)

    grad_one = mine[:rows_loc] + got.astype(F32)
    weighted = gain_one * grad_one
    inner_one = jnp.mean(unit_one * weighted, axis=1, keepdims=True)
    norm1_part = jnp.sum(grad_one * unit_one, axis=0)
    x_grad = (grad_resid + scale_one * (weighted - unit_one * inner_one)).astype(BF16)
    moved = low_sum.advance(norm1_part)
    moved = high_sum.advance(*moved)

    lone = jnp.pad(jnp.stack([bias_part, maxima]), ((0, 4), (0, width - heads)))
    sums = at.sum_plane(
        jnp.concatenate([jnp.stack([norm1_part, norm2_part]), lone], axis=0),
        (low_sum, high_sum),
        lambda one, two: jnp.concatenate(
            [one[:3] + two[:3], jnp.maximum(one[3:], two[3:])], axis=0
        ),
    )
    other = at.swap_core(sums)
    cut = width // 2
    norms = sums[:2] + other[:2]
    norms = lax.dynamic_slice_in_dim(norms, at.y * cut, cut, 1) + at.swap_y(
        lax.dynamic_slice_in_dim(norms, (1 - at.y) * cut, cut, 1)
    )
    lone = at.by_core(sums[2:4, :heads], other[2:4, :heads], 1)
    g_bias = lone[0]
    clip_factor = jnp.minimum(1.0, clip_tau / jnp.maximum(lone[1], 1.0))
    columns = jnp.repeat(jnp.sqrt(clip_factor), HEAD_DIM)
    clipped_query = (w_query.astype(F32) * columns[None, :]).astype(BF16)
    clipped_key = (w_key.astype(F32) * columns[None, :]).astype(BF16)

    def place(own):
        keep, got = at.finish_grad(own)
        return at.by_core(keep, got, 1)

    g_down = place(total_down)
    keep, got = at.finish_grad(total_gu)
    g_gate = at.by_core(keep[:, :units], got[:, :units], 1)
    g_up = at.by_core(keep[:, units:], got[:, units:], 1)
    low, high = low_sum.finish(), high_sum.finish()
    got_low, got_high = at.swap_core(at.theirs(low)), at.swap_core(at.theirs(high))
    g_query, g_key, g_value, g_output = assemble(at.core, low, got_low, high, got_high, pairs)
    start = qkv_cols - middle
    mine = lax.dynamic_slice(high, (at.core * d_rows, start), (d_rows, 2 * heads))
    both = at.by_core(mine[None], got_high[None, :, start : start + 2 * heads].astype(F32), 0)
    g_forget = both[..., :heads] + both[..., heads:]
    g_forget = jnp.concatenate([g_forget[0], g_forget[1]], axis=1)

    return (
        layer_out,
        x_grad,
        norms[0],
        g_query,
        g_key,
        g_value,
        g_forget,
        g_bias,
        g_output,
        norms[1],
        g_gate,
        g_up,
        g_down,
        clip_factor,
        clipped_query,
        clipped_key,
    )


def pick_body(mesh):
    dp, tensor = mesh.shape["dp"], mesh.shape["tensor"]

    def body(*args):
        rows, heads = args[0].shape[0], args[7].shape[0]
        depth = dp // 4
        paired = (
            tensor == 2
            and dp % 4 == 0
            and depth & (depth - 1) == 0
            and rows == BLOCK
            and heads % 4 == 0
        )
        return (paired_body if paired else general_body)(*args)

    return body
def solution(mesh):
    return jax.shard_map(
        pick_body(mesh),
        mesh=mesh,
        in_specs=(
            P(("dp", "tensor"), None),
            P("dp", None),
            P("dp"),
            P("dp", "tensor"),
            P("dp", "tensor"),
            P("dp", "tensor"),
            P("dp", "tensor"),
            P("tensor"),
            P("dp", "tensor"),
            P("dp"),
            P("dp", "tensor"),
            P("dp", "tensor"),
            P("dp", "tensor"),
            P("tensor"),
            P(("dp", "tensor"), None),
        ),
        out_specs=(
            P(("dp", "tensor"), None),
            P(("dp", "tensor"), None),
            P("tensor"),
            P("dp", "tensor"),
            P("dp", "tensor"),
            P("dp", "tensor"),
            P("dp", "tensor"),
            P("tensor"),
            P("dp", "tensor"),
            P("tensor"),
            P("dp", "tensor"),
            P("dp", "tensor"),
            P("dp", "tensor"),
            P("tensor"),
            P("dp", "tensor"),
            P("dp", "tensor"),
        ),
        check_vma=False,
    )
```
